512 devices in a mesh: slab: 128 (over z, y, core), chan: 4 (over x).
Axes of the slice: x: 4, y: 8, z: 8, core: 2. Of those that a mesh axis runs over, the one named last changes fastest.
Arguments:
- field: bfloat16 [64, 256, 4096], P(None, 'slab'), may hold values from -6 to 6
- cotangent: bfloat16 [64, 256, 4096], P(None, 'slab'), may hold values from -10 to 10
- spectral_weight: bfloat16 [2, 64, 64, 512, 32], P(None, 'chan', None, 'slab'), may hold values from -4 to 4
- point_weight: bfloat16 [64, 64], replicated, may hold values from -0.75 to 0.75
- point_bias: bfloat16 [64], replicated, may hold values from -2 to 2
Outputs:
- grad_input: bfloat16 [64, 256, 4096], P('chan', 'slab')
- grad_spectral: float32 [2, 64, 64, 512, 32], P(None, 'chan', None, 'slab')
- grad_pointwise: float32 [64, 64], P('chan')
- grad_bias: float32 [64], replicated
The draws below stay inside these ranges and needn't reach their ends.
All inputs are finite; a program needn't handle non-finite values.
Results may differ from the reference program's by a relative error of at most 0.023.
Values may be sent and summed in bfloat16 or wider, within the bound.
No kernel may reach another device: no remote copies, remote signals or barrier semaphores. Data moves between devices by JAX's collectives and lax.ppermute only.
A program may use at most 64 MiB of HBM per device.

```python
import math
import jax
import jax.numpy as jnp
from jax import lax

C = 64
MX = 32
MY = 32
MZ = 16
NX = 256
NY = 64
NZ = 64
MODES = 512


def draw_cotangent(key, part):
    noise_key = jax.random.fold_in(key, 11)
    positions = jnp.arange(NX, dtype=jnp.float32) / (NX - 1)
    base_noise = jnp.clip(jax.random.normal(noise_key, (C, NX, NY * NZ), jnp.float32), -6.0, 6.0)
    plane_ramp = 0.5 + positions
    scaled = base_noise * plane_ramp[None, :, None]
    return scaled.astype(jnp.bfloat16)


def block_levels(stream_key, shape, split, least, largest):
    loudness = 1.0
    for dim, shards_of in split:
        steps = jax.random.uniform(jax.random.fold_in(jax.random.fold_in(stream_key, 6), dim), (shards_of,), jnp.float32, least / len(split), largest / len(split))
        loudness = loudness * jnp.repeat(jnp.exp(steps), shape[dim] // shards_of).reshape((-1,) + (1,) * (len(shape) - 1 - dim))
    return loudness


def noise(stream_key, extent, scale, reach, cuts=(), kind=jnp.bfloat16):
    loudness = block_levels(stream_key, extent, cuts, -0.22, 0.18) if cuts else 1.0
    array = jax.random.normal(stream_key, extent, jnp.float32) * scale * loudness
    return jnp.minimum(jnp.maximum(array, -reach), reach).astype(kind)


def setup_inputs(seed: int = 0) -> dict:
    key_list = jax.random.split(jax.random.key(seed), 6)
    return {
        "field": noise(key_list[0], (C, NX, NY * NZ), 1.0, 6.0, ((1, 128),)),
        "cotangent": draw_cotangent(jax.random.fold_in(key_list[5], 71), 0),
        "spectral_weight": noise(key_list[2], (2, C, C, MODES, MX), 0.7, 4.0, ((1, 4), (3, 128))),
        "point_weight": noise(key_list[3], (C, C), C ** -0.5, 0.75),
        "point_bias": noise(key_list[4], (C,), 0.5, 2.0),
    }


def kept_modes(total, length):
    mode_index = jnp.arange(total, dtype=jnp.int32)
    return jnp.where(mode_index < total // 2, mode_index, mode_index - total + length)

def phases(frequency, length):
    positions = jnp.arange(length, dtype=jnp.int32)
    wound_up = frequency[:, None] * positions[None, :] % length
    return 2.0 * math.pi / length * wound_up.astype(jnp.float32)

def make_tables():
    angle_z = phases(jnp.arange(MZ, dtype=jnp.int32), NZ)
    cosine_z = jnp.cos(angle_z)
    sine_z = jnp.sin(angle_z)
    forward_z = jnp.stack([cosine_z.T, -sine_z.T], 1).astype(jnp.bfloat16)
    weight_z = (jnp.where(jnp.arange(MZ) == 0, 1.0, 2.0) / (NX * NY * NZ)).astype(jnp.float32)
    scaled_z = jnp.stack([weight_z[:, None] * cosine_z, -weight_z[:, None] * sine_z], 1).astype(jnp.bfloat16)
    plain_z = jnp.stack([cosine_z, -sine_z], 1).astype(jnp.bfloat16)
    angle_y = phases(kept_modes(MY, NY), NY)
    cosine_y = jnp.cos(angle_y)
    sine_y = jnp.sin(angle_y)
    upper_rows = jnp.stack([cosine_y.T, -sine_y.T], -1)
    lower_rows = jnp.stack([sine_y.T, cosine_y.T], -1)
    forward_y = jnp.stack([upper_rows, lower_rows], 0).reshape(2 * NY, 2 * MY).astype(jnp.bfloat16)
    real_rows = jnp.stack([cosine_y, sine_y], 1)
    imag_rows = jnp.stack([-sine_y, cosine_y], 1)
    inverse_y = jnp.stack([real_rows, imag_rows], 1).reshape(2 * MY, 2 * NY).astype(jnp.bfloat16)
    angle_x = phases(kept_modes(MX, NX), NX)
    cosine_x = jnp.cos(angle_x).T.astype(jnp.bfloat16)
    sine_x = jnp.sin(angle_x).T.astype(jnp.bfloat16)
    return (forward_z, scaled_z, plain_z, forward_y, inverse_y, cosine_x, sine_x)

def product(form, left, right):
    return jnp.einsum(form, left.astype(jnp.float32), right.astype(jnp.float32), precision=lax.Precision.HIGHEST)

def to_modes(field_part, tables):
    forward_z, scaled_z, plain_z, forward_y, inverse_y, cosine_x, sine_x = tables
    channels = field_part.shape[0]
    grid_view = field_part.reshape(channels, NX, NY, NZ)
    section_one = product('cxyz,zpk->cxkpy', grid_view, forward_z).astype(jnp.bfloat16)
    section_one = section_one.reshape(channels, NX, MZ, 2 * NY)
    section_two = product('cxkm,mn->cxkn', section_one, forward_y).astype(jnp.bfloat16)
    pencils = section_two.reshape(channels, NX, MODES, 2)
    along_cos = product('cxmq,xk->cmqk', pencils, cosine_x)
    along_sin = product('cxmq,xk->cmqk', pencils, sine_x)
    real_part = along_cos[:, :, 0] + along_sin[:, :, 1]
    imag_part = along_cos[:, :, 1] - along_sin[:, :, 0]
    return jnp.stack([real_part, imag_part], 2)

def to_grid(spectra, tables, table_z):
    forward_z, scaled_z, plain_z, forward_y, inverse_y, cosine_x, sine_x = tables
    channels = spectra.shape[0]
    back_cos = product('cmqk,xk->cxmq', spectra, cosine_x)
    back_sin = product('cmqk,xk->cxmq', spectra, sine_x)
    real_part = back_cos[..., 0] - back_sin[..., 1]
    imag_part = back_cos[..., 1] + back_sin[..., 0]
    pencil_rows = jnp.stack([real_part, imag_part], -1).astype(jnp.bfloat16)
    slabs = pencil_rows.reshape(channels, NX, MZ, 2 * MY)
    section_two = product('cxkn,nm->cxkm', slabs, inverse_y).astype(jnp.bfloat16)
    section_two = section_two.reshape(channels, NX, MZ, 2, NY)
    grid_view = product('cxkpy,kpz->cxyz', section_two, table_z)
    return grid_view.reshape(channels, NX, NY * NZ)

def gelu_grad(pre_act):
    normal_cdf = 0.5 * (1.0 + jax.scipy.special.erf(pre_act / math.sqrt(2.0)))
    normal_pdf = jnp.exp(-0.5 * pre_act * pre_act) / math.sqrt(2.0 * math.pi)
    return normal_cdf + pre_act * normal_pdf

def reference(field, cotangent, spectral_weight, point_weight, point_bias):
    tables = make_tables()
    scaled_z = tables[1]
    plain_z = tables[2]
    coeff = to_modes(field, tables).astype(jnp.bfloat16)
    coeff_real = coeff[:, :, 0].astype(jnp.float32)
    coeff_imag = coeff[:, :, 1].astype(jnp.float32)
    real_weight = spectral_weight[0].astype(jnp.float32)
    imag_weight = spectral_weight[1].astype(jnp.float32)
    spec_real = product('imk,iomk->omk', coeff_real, real_weight) - product('imk,iomk->omk', coeff_imag, imag_weight)
    spec_imag = product('imk,iomk->omk', coeff_real, imag_weight) + product('imk,iomk->omk', coeff_imag, real_weight)
    spectra = jnp.stack([spec_real, spec_imag], 2)
    shaped = to_grid(spectra.astype(jnp.bfloat16), tables, scaled_z)
    pre_act = shaped + product('io,ixc->oxc', point_weight, field) + point_bias.astype(jnp.float32)[:, None, None]
    grad_pre = (cotangent.astype(jnp.float32) * gelu_grad(pre_act)).astype(jnp.bfloat16)
    mode_index = jnp.arange(MODES, dtype=jnp.int32)
    mode_scale = (jnp.where(mode_index // MY == 0, 1.0, 2.0) / (NX * NY * NZ)).astype(jnp.float32)
    grad_hat = (to_modes(grad_pre, tables) * mode_scale[None, :, None, None]).astype(jnp.bfloat16)
    grad_real = grad_hat[:, :, 0].astype(jnp.float32)
    grad_imag = grad_hat[:, :, 1].astype(jnp.float32)

    def one_row(row_pair):
        row_real, row_imag = row_pair
        part_real = row_real[None] * grad_real + row_imag[None] * grad_imag
        part_imag = row_real[None] * grad_imag - row_imag[None] * grad_real
        return jnp.stack([part_real, part_imag], 0)
    grad_spectral = jnp.moveaxis(lax.map(one_row, (coeff_real, coeff_imag)), 0, 1)
    adj_real = product('omk,iomk->imk', grad_real, real_weight) + product('omk,iomk->imk', grad_imag, imag_weight)
    adj_imag = product('omk,iomk->imk', grad_imag, real_weight) - product('omk,iomk->imk', grad_real, imag_weight)
    adjoint = jnp.stack([adj_real, adj_imag], 2).astype(jnp.bfloat16)
    spectral_back = to_grid(adjoint, tables, plain_z)
    grad_input = (spectral_back + product('io,oxc->ixc', point_weight, grad_pre)).astype(jnp.bfloat16)
    inverse_root = 1.0 / math.sqrt(NX * NY * NZ)
    grad_pointwise = product('ixc,oxc->io', field, grad_pre) * inverse_root
    grad_bias = lax.optimization_barrier(jnp.sum(grad_pre.astype(jnp.float32), axis=(1, 2))) * inverse_root
    return (grad_input, grad_spectral, grad_pointwise, grad_bias)
```

```python
import math

import jax
import jax.numpy as jnp
from jax import lax
from jax.sharding import PartitionSpec as P

MX = 32
MY = 32
MZ = 16
NX = 256
NY = 64
NZ = 64
RIDER = 128


def kept_modes(total, length):
    mode_index = jnp.arange(total, dtype=jnp.int32)
    return jnp.where(mode_index < total // 2, mode_index, mode_index - total + length)


def phases(frequency, length):
    positions = jnp.arange(length, dtype=jnp.int32)
    wound_up = frequency[:, None] * positions[None, :] % length
    return 2.0 * math.pi / length * wound_up.astype(jnp.float32)


def make_tables():
    angle_z = phases(jnp.arange(MZ, dtype=jnp.int32), NZ)
    cosine_z = jnp.cos(angle_z)
    sine_z = jnp.sin(angle_z)
    forward_z = jnp.stack([cosine_z.T, -sine_z.T], 1).astype(jnp.bfloat16)
    weight_z = (jnp.where(jnp.arange(MZ) == 0, 1.0, 2.0) / (NX * NY * NZ)).astype(jnp.float32)
    scaled_z = jnp.stack([weight_z[:, None] * cosine_z, -weight_z[:, None] * sine_z], 1).astype(
        jnp.bfloat16
    )
    plain_z = jnp.stack([cosine_z, -sine_z], 1).astype(jnp.bfloat16)
    angle_y = phases(kept_modes(MY, NY), NY)
    cosine_y = jnp.cos(angle_y)
    sine_y = jnp.sin(angle_y)
    upper_rows = jnp.stack([cosine_y.T, -sine_y.T], -1)
    lower_rows = jnp.stack([sine_y.T, cosine_y.T], -1)
    forward_y = jnp.stack([upper_rows, lower_rows], 0).reshape(2 * NY, 2 * MY).astype(jnp.bfloat16)
    real_rows = jnp.stack([cosine_y, sine_y], 1)
    imag_rows = jnp.stack([-sine_y, cosine_y], 1)
    inverse_y = jnp.stack([real_rows, imag_rows], 1).reshape(2 * MY, 2 * NY).astype(jnp.bfloat16)
    angle_x = phases(kept_modes(MX, NX), NX)
    cosine_x = jnp.cos(angle_x).T.astype(jnp.bfloat16)
    sine_x = jnp.sin(angle_x).T.astype(jnp.bfloat16)
    return (forward_z, scaled_z, plain_z, forward_y, inverse_y, cosine_x, sine_x)


def to_modes(field_part, tables, rider=None):
    forward_z, scaled_z, plain_z, forward_y, inverse_y, cosine_x, sine_x = tables
    channels = field_part.shape[0]
    planes = field_part.shape[1]
    grid_view = field_part.reshape(channels, planes, NY, NZ)
    section_one = jnp.einsum(
        "cxyz,zpk->cxkpy", grid_view, forward_z, preferred_element_type=jnp.float32
    ).astype(jnp.bfloat16)
    section_one = section_one.reshape(channels, planes, MZ, 2 * NY)
    section_two = jnp.einsum(
        "cxkm,mn->cxkn", section_one, forward_y, preferred_element_type=jnp.float32
    ).astype(jnp.bfloat16)
    section_two = section_two.reshape(channels, planes, 2 * MZ * MY)
    if rider is None:
        pencils = lax.all_to_all(section_two, "slab", split_axis=2, concat_axis=1, tiled=True)
    else:
        owners = rider.shape[0]
        rows = section_two.reshape(channels, planes, owners, -1)
        rows = jnp.transpose(rows, (2, 1, 3, 0)).reshape(owners, -1)
        rows, rider = exchange(rows, rider)
        rows = rows.reshape(owners, planes, -1, channels)
        pencils = jnp.transpose(rows, (3, 0, 1, 2))
    pencils = pencils.reshape(channels, NX, -1, 2)
    along_cos = jnp.einsum("cxmq,xk->cmqk", pencils, cosine_x, preferred_element_type=jnp.float32)
    along_sin = jnp.einsum("cxmq,xk->cmqk", pencils, sine_x, preferred_element_type=jnp.float32)
    real_part = along_cos[:, :, 0] + along_sin[:, :, 1]
    imag_part = along_cos[:, :, 1] - along_sin[:, :, 0]
    modes = jnp.stack([real_part, imag_part], 2)
    return modes if rider is None else (modes, rider)


def to_grid(spectra, tables, table_z, rider=None):
    forward_z, scaled_z, plain_z, forward_y, inverse_y, cosine_x, sine_x = tables
    channels = spectra.shape[0]
    back_cos = jnp.einsum("cmqk,xk->cxmq", spectra, cosine_x, preferred_element_type=jnp.float32)
    back_sin = jnp.einsum("cmqk,xk->cxmq", spectra, sine_x, preferred_element_type=jnp.float32)
    real_part = back_cos[..., 0] - back_sin[..., 1]
    imag_part = back_cos[..., 1] + back_sin[..., 0]
    pencil_rows = jnp.stack([real_part, imag_part], -1).astype(jnp.bfloat16)
    pencil_rows = pencil_rows.reshape(channels, NX, -1)
    if rider is None:
        slabs = lax.all_to_all(pencil_rows, "slab", split_axis=1, concat_axis=2, tiled=True)
        planes = slabs.shape[1]
    else:
        owners = rider.shape[0]
        planes = NX // owners
        rows = pencil_rows.reshape(channels, owners, planes, -1)
        rows = jnp.transpose(rows, (1, 2, 3, 0)).reshape(owners, -1)
        rows, rider = exchange(rows, rider)
        rows = rows.reshape(owners, planes, -1, channels)
        slabs = jnp.transpose(rows, (3, 1, 0, 2))
    slabs = slabs.reshape(channels, planes, MZ, 2 * MY)
    section_two = jnp.einsum(
        "cxkn,nm->cxkm", slabs, inverse_y, preferred_element_type=jnp.float32
    ).astype(jnp.bfloat16)
    section_two = section_two.reshape(channels, planes, MZ, 2, NY)
    grid_view = jnp.einsum(
        "cxkpy,kpz->cxyz", section_two, table_z, preferred_element_type=jnp.float32
    )
    grid = grid_view.reshape(channels, planes, NY * NZ)
    return grid if rider is None else (grid, rider)


def sum_over_chan(part):
    peers = lax.axis_size("chan")
    copies = jnp.broadcast_to(part[None], (peers,) + part.shape)
    arrived = lax.all_to_all(copies, "chan", split_axis=0, concat_axis=0, tiled=True)
    return jnp.sum(arrived.astype(jnp.float32), axis=0).astype(part.dtype)


def split_words(values):
    head = lax.reduce_precision(values, 8, 7)
    rest = values - head
    middle = lax.reduce_precision(rest, 8, 7)
    words = jnp.concatenate([head, middle, rest - middle], -1).astype(jnp.bfloat16)
    return jnp.pad(words, ((0, 0), (0, RIDER - words.shape[1])))


def join_words(words, count):
    wide = words.astype(jnp.float32)
    return wide[:, :count] + wide[:, count : 2 * count] + wide[:, 2 * count : 3 * count]


def exchange(rows, rider):
    width = rows.shape[1]
    arrived = lax.all_to_all(
        jnp.concatenate([rows, rider], 1), "slab", split_axis=0, concat_axis=0, tiled=True
    )
    return arrived[:, :width], arrived[:, width:]


def gelu_grad(pre_act):
    normal_cdf = 0.5 * (1.0 + jax.scipy.special.erf(pre_act / math.sqrt(2.0)))
    normal_pdf = jnp.exp(-0.5 * pre_act * pre_act) / math.sqrt(2.0 * math.pi)
    return normal_cdf + pre_act * normal_pdf


def body(field, cotangent, spectral_weight, point_weight, point_bias):
    tables = make_tables()
    scaled_z = tables[1]
    plain_z = tables[2]
    group_size = spectral_weight.shape[1]
    modes_dev = spectral_weight.shape[3]
    chan_start = lax.axis_index("chan") * group_size
    own_field = lax.dynamic_slice_in_dim(field, chan_start, group_size, 0)
    coeff = to_modes(own_field, tables).astype(jnp.bfloat16)
    coeff_real = coeff[:, :, 0]
    coeff_imag = coeff[:, :, 1]
    real_weight = spectral_weight[0]
    imag_weight = spectral_weight[1]
    spec_real = jnp.einsum(
        "imk,iomk->omk", coeff_real, real_weight, preferred_element_type=jnp.float32
    ) - jnp.einsum("imk,iomk->omk", coeff_imag, imag_weight, preferred_element_type=jnp.float32)
    spec_imag = jnp.einsum(
        "imk,iomk->omk", coeff_real, imag_weight, preferred_element_type=jnp.float32
    ) + jnp.einsum("imk,iomk->omk", coeff_imag, real_weight, preferred_element_type=jnp.float32)
    partial_spectra = jnp.stack([spec_real, spec_imag], 2)
    spectra = sum_over_chan(partial_spectra.astype(jnp.bfloat16))
    shaped = to_grid(spectra, tables, scaled_z)
    mixed = jnp.einsum("io,ixc->oxc", point_weight, field, preferred_element_type=jnp.float32)
    pre_act = shaped + mixed + point_bias.astype(jnp.float32)[:, None, None]
    grad_pre = (cotangent.astype(jnp.float32) * gelu_grad(pre_act)).astype(jnp.bfloat16)
    inverse_root = 1.0 / math.sqrt(NX * NY * NZ)
    weight_part = jnp.einsum("ixc,oxc->io", own_field, grad_pre, preferred_element_type=jnp.float32)
    bias_part = jnp.sum(grad_pre, axis=(1, 2), dtype=jnp.float32)
    owners = lax.axis_size("slab")
    sums = jnp.concatenate([weight_part.reshape(-1), bias_part])
    share = -(-sums.shape[0] // owners)
    sums = jnp.pad(sums, (0, share * owners - sums.shape[0])).reshape(owners, share)
    mode_index = lax.axis_index("slab") * modes_dev + jnp.arange(modes_dev, dtype=jnp.int32)
    mode_scale = (jnp.where(mode_index // MY == 0, 1.0, 2.0) / (NX * NY * NZ)).astype(jnp.float32)
    grad_modes, rider = to_modes(grad_pre, tables, split_words(sums))
    grad_hat = (grad_modes * mode_scale[None, :, None, None]).astype(jnp.bfloat16)
    owned = jnp.sum(join_words(rider, share), axis=0) * inverse_root
    owned = jnp.broadcast_to(owned[None], (owners, share))
    grad_real = grad_hat[:, :, 0]
    grad_imag = grad_hat[:, :, 1]
    outer_real = jnp.einsum(
        "imk,omk->iomk", coeff_real, grad_real, preferred_element_type=jnp.float32
    ) + jnp.einsum("imk,omk->iomk", coeff_imag, grad_imag, preferred_element_type=jnp.float32)
    outer_imag = jnp.einsum(
        "imk,omk->iomk", coeff_real, grad_imag, preferred_element_type=jnp.float32
    ) - jnp.einsum("imk,omk->iomk", coeff_imag, grad_real, preferred_element_type=jnp.float32)
    grad_spectral = jnp.stack([outer_real, outer_imag], 0)
    adj_real = jnp.einsum(
        "omk,iomk->imk", grad_real, real_weight, preferred_element_type=jnp.float32
    ) + jnp.einsum("omk,iomk->imk", grad_imag, imag_weight, preferred_element_type=jnp.float32)
    adj_imag = jnp.einsum(
        "omk,iomk->imk", grad_imag, real_weight, preferred_element_type=jnp.float32
    ) - jnp.einsum("omk,iomk->imk", grad_real, imag_weight, preferred_element_type=jnp.float32)
    adjoint = jnp.stack([adj_real, adj_imag], 2).astype(jnp.bfloat16)
    spectral_back, rider = to_grid(adjoint, tables, plain_z, split_words(owned))
    own_rows = lax.dynamic_slice_in_dim(point_weight, chan_start, group_size, 0)
    point_back = jnp.einsum("io,oxc->ixc", own_rows, grad_pre, preferred_element_type=jnp.float32)
    grad_input = (spectral_back + point_back).astype(jnp.bfloat16)
    totals = join_words(rider, share).reshape(-1)
    grad_pointwise = totals[: weight_part.size].reshape(weight_part.shape)
    grad_bias = totals[weight_part.size : weight_part.size + bias_part.size]
    return (grad_input, grad_spectral, grad_pointwise, grad_bias)


def solution(mesh):
    placed = (
        P(None, "slab", None),
        P(None, "slab", None),
        P(None, "chan", None, "slab", None),
        P(),
        P(),
    )
    return jax.shard_map(
        body,
        mesh=mesh,
        in_specs=placed,
        out_specs=(
            P("chan", "slab", None),
            P(None, "chan", None, "slab", None),
            P("chan", None),
            P(),
        ),
        check_vma=False,
    )
```

```python
import math

import jax
import jax.numpy as jnp
import numpy as np
from jax import lax
from jax.experimental import pallas as pl
from jax.experimental.pallas import tpu as pltpu
from jax.sharding import PartitionSpec as P

MX = 32
MY = 32
MZ = 16
NX = 256
NY = 64
NZ = 64
C = 64
OWN = 16
SLAB = 128
PLANES = 2
LOW = 4
HIGH = 8
CELLS = NY * NZ
LANES = 128
HALF = 64
CHUNK = 10
BACK = 4
SHARE = 7
INVERSE_ROOT = 1.0 / math.sqrt(NX * NY * NZ)
F32 = jnp.float32
BF16 = jnp.bfloat16


def kept(total, length):
    index = np.arange(total)
    return np.where(index < total // 2, index, index - total + length)


def waves(frequency, length):
    wound = (frequency[:, None] * np.arange(length)[None, :]) % length
    angle = np.float32(2.0 * math.pi / length) * wound.astype(np.float32)
    return np.cos(angle), np.sin(angle)


def table(values):
    return jnp.asarray(np.asarray(values, np.float32)).astype(BF16)


def axis_tables():
    cos_z, sin_z = waves(np.arange(MZ), NZ)
    cos_y, sin_y = waves(kept(MY, NY), NY)
    cos_x, sin_x = waves(kept(MX, NX), NX)
    return cos_z, sin_z, cos_y, sin_y, cos_x, sin_x


def rows_of_ky(real, imag):
    both = np.stack([real, imag], 1).reshape(HIGH, LOW, 2, -1)
    return np.transpose(both, (0, 2, 1, 3))


def middle_tables():
    cos_z, sin_z, cos_y, sin_y, _, _ = axis_tables()
    weight = (np.where(np.arange(MZ) == 0, 1.0, 2.0) / (NX * NY * NZ))[:, None]
    to_z = np.stack([weight * cos_z, -weight * sin_z], 1).reshape(2 * MZ, NZ).T
    from_z = np.concatenate([cos_z, -sin_z], 0)
    real = np.stack([cos_y, sin_y], 1).reshape(MY, 2 * NY)
    imag = np.stack([-sin_y, cos_y], 1).reshape(MY, 2 * NY)
    to_y = rows_of_ky(real, imag).reshape(2 * MY, 2 * NY).T
    real = np.stack([cos_y, sin_y], 2).reshape(MY, 2 * NY)
    imag = np.stack([-sin_y, cos_y], 2).reshape(MY, 2 * NY)
    from_y = rows_of_ky(real, imag).reshape(HIGH, 8, 2 * NY)
    from_y = np.concatenate([from_y, np.zeros((HIGH, CHUNK - 8, 2 * NY))], 1)
    from_y = from_y.reshape(HIGH * CHUNK, 2 * NY)
    pick = np.zeros((SLAB, CHUNK, 32))
    owner = np.arange(SLAB)
    pick[owner, 8, np.minimum(owner // SHARE, OWN)] = 1.0
    return to_y, to_z, from_z, from_y, pick.reshape(SLAB * CHUNK, 32)


def pencil_tables():
    _, _, _, _, cos_x, sin_x = axis_tables()
    along = np.concatenate([cos_x, sin_x], 0)
    split = along.reshape(2 * MX, SLAB, PLANES)
    spread = np.transpose(split, (2, 0, 1)).reshape(2 * PLANES * MX, SLAB)
    back = np.transpose(split, (2, 1, 0)).reshape(NX, 2 * MX)
    return along, spread, spread.T, back


def mm(left, right):
    return jnp.dot(left, right, preferred_element_type=F32)


def swap(values):
    return pltpu.roll(values, HALF, 1)


def lane_of(shape):
    return lax.broadcasted_iota(jnp.int32, shape, 1)


def gelu_grad(pre_act):
    normal_cdf = 0.5 * (1.0 + lax.erf(pre_act * (1.0 / math.sqrt(2.0))))
    normal_pdf = jnp.exp(-0.5 * pre_act * pre_act) * (1.0 / math.sqrt(2.0 * math.pi))
    return normal_cdf + pre_act * normal_pdf


def two_words(values):
    head = values.astype(BF16).astype(F32)
    rest = values - head
    return jnp.where(lane_of(values.shape) < HALF, head, swap(rest))


def middle_kernel(
    modes, base, cot, own, to_y, to_z, from_z, from_y, pick, grad, out, up, flat, down
):
    @pl.loop(0, MZ, unroll=4)
    def _(kz):
        start = pl.multiple_of(kz * 64, 64)
        up[pl.ds(pl.multiple_of(kz * 128, 128), 128), :] = mm(
            to_y[...], modes[pl.ds(start, 64), :]
        )

    @pl.loop(0, NY // 2, unroll=4)
    def _(pair):
        left = up[pl.ds(pair * 2, 2 * MZ, stride=NY), :]
        right = up[pl.ds(pair * 2 + 1, 2 * MZ, stride=NY), :]
        both = jnp.concatenate([left, right], 1).astype(BF16)
        grid = mm(to_z[...], both)
        start = pl.multiple_of(pair * 128, 128)
        flat[pl.ds(start, 64), :] = grid[:, :LANES] + base[pl.ds(start, 64), :]
        start = pl.multiple_of(pair * 128 + 64, 64)
        flat[pl.ds(start, 64), :] = grid[:, LANES:] + base[pl.ds(start, 64), :]

    @pl.loop(0, CELLS // 64, unroll=2)
    def _(block):
        rows = pl.ds(pl.multiple_of(block * 64, 64), 64)
        grad[rows, :] = (cot[rows, :].astype(F32) * gelu_grad(flat[rows, :])).astype(BF16)

    @pl.loop(0, NY // 2, unroll=4)
    def _(pair):
        start = pl.multiple_of(pair * 128, 128)
        left = grad[pl.ds(start, 64), :]
        right = grad[pl.ds(pl.multiple_of(start + 64, 64), 64), :]
        lines = mm(from_z[...], jnp.concatenate([left, right], 1))
        start = pl.multiple_of(pair * 64, 64)
        down[pl.ds(start, 32), :] = lines[:, :LANES]
        down[pl.ds(pl.multiple_of(start + 32, 32), 32), :] = lines[:, LANES:]

    sums = mm(own[...], grad[...])
    lower = sums[:OWN] + swap(sums[OWN : 2 * OWN])
    bias = sums[2 * OWN : 2 * OWN + 8] + swap(sums[2 * OWN : 2 * OWN + 8])
    words = two_words(jnp.concatenate([lower, bias, jnp.zeros_like(bias)], 0)).astype(BF16)

    @pl.loop(0, MZ, unroll=4)
    def _(kz):
        lines = down[pl.ds(kz, 2 * NY, stride=MZ), :].astype(BF16)
        rows = pl.ds(pl.multiple_of(kz * HIGH * CHUNK, HIGH * CHUNK), HIGH * CHUNK)
        out[rows, :] = (mm(from_y[...], lines) + mm(pick[rows, :], words)).astype(BF16)


def in_vmem(count):
    return [pl.BlockSpec(memory_space=pltpu.VMEM)] * count


def call(kernel, shapes, scratch, flops, *operands):
    moved = sum(s.size * s.dtype.itemsize for s in list(operands) + list(shapes))
    return pl.pallas_call(
        kernel,
        out_shape=shapes,
        in_specs=in_vmem(len(operands)),
        out_specs=in_vmem(len(shapes)),
        scratch_shapes=scratch,
        cost_estimate=pl.CostEstimate(flops=flops, bytes_accessed=moved, transcendentals=0),
        compiler_params=pltpu.CompilerParams(vmem_limit_bytes=40 * 2**20),
    )(*operands)


def middle(modes, base, cot, own):
    tables = [table(t) for t in middle_tables()]
    shapes = (
        jax.ShapeDtypeStruct((CELLS, LANES), BF16),
        jax.ShapeDtypeStruct((SLAB * CHUNK, LANES), BF16),
    )
    scratch = [
        pltpu.VMEM((2 * NY * MZ, LANES), F32),
        pltpu.VMEM((CELLS, LANES), F32),
        pltpu.VMEM((2 * NY * MZ, LANES), F32),
    ]
    return call(middle_kernel, shapes, scratch, 400_000_000, modes, base, cot, own, *tables)


def mix_kernel(pencils, weight, along, coeff, out):
    both = mm(along[...], pencils[...])
    lane = lane_of((MX, LANES))
    turned = swap(both[MX:])
    modes = both[:MX] + jnp.where(lane < HALF, turned, -turned)
    modes = modes.astype(BF16).astype(F32)
    coeff[...] = modes
    for m in range(LOW):
        rows = pl.ds(m * MX, MX)
        real = jnp.zeros((MX, C), F32)
        imag = jnp.zeros((MX, C), F32)
        for i in range(OWN):
            at = m * OWN + i
            left = jnp.broadcast_to(modes[:, at : at + 1], (MX, C))
            right = jnp.broadcast_to(modes[:, HALF + at : HALF + at + 1], (MX, C))
            weight_real = weight[0, i, rows, :].astype(F32)
            weight_imag = weight[1, i, rows, :].astype(F32)
            real += left * weight_real - right * weight_imag
            imag += left * weight_imag + right * weight_real
        part = jnp.concatenate([real, imag], 1).astype(BF16)
        for peer in range(4):
            out[peer, rows, :] = part


def mix(pencils, weight):
    along = table(pencil_tables()[0])
    shapes = (
        jax.ShapeDtypeStruct((MX, LANES), F32),
        jax.ShapeDtypeStruct((4, LOW * MX, LANES), BF16),
    )
    return call(mix_kernel, shapes, [], 4_000_000, pencils, weight, along)


def spread_kernel(parts, spread, out, rows):
    total = parts[0].astype(F32)
    for peer in range(1, 4):
        total += parts[peer].astype(F32)
    lane = lane_of((MX, LANES))
    for m in range(LOW):
        here = total[m * MX : (m + 1) * MX]
        there = swap(here)
        zero = jnp.zeros_like(here)
        a = jnp.where(lane < HALF, here, zero)
        b = jnp.where(lane < HALF, there, zero)
        c = jnp.where(lane < HALF, zero, there)
        d = jnp.where(lane < HALF, zero, here)
        top = jnp.concatenate([a, b], 1)
        second = jnp.concatenate([-b, a], 1)
        third = jnp.concatenate([c, d], 1)
        last = jnp.concatenate([-d, c], 1)
        block = jnp.concatenate([top, second, third, last], 0).astype(BF16)
        planes = mm(spread[...], block)
        rows[pl.ds(m, SLAB, stride=8), :] = planes[:, :LANES]
        rows[pl.ds(LOW + m, SLAB, stride=8), :] = planes[:, LANES:]
    out[...] = rows[...].astype(BF16)


def spread_planes(parts):
    shapes = (jax.ShapeDtypeStruct((SLAB * 8, LANES), BF16),)
    scratch = [pltpu.VMEM((SLAB * 8, LANES), F32)]
    spread = table(pencil_tables()[2])
    return call(spread_kernel, shapes, scratch, 40_000_000, parts, spread)[0]


def adjoint_kernel(pencils, weight, gather, back, scale, hat, out, wide, rows):
    wide[...] = pencils[...].astype(F32)
    lane = lane_of((MX, LANES))
    adjoint = jnp.zeros((MX, LANES), F32)
    factor = scale[0:1, :]
    for m in range(LOW):
        left = wide[pl.ds(m, SLAB, stride=CHUNK), :]
        right = wide[pl.ds(LOW + m, SLAB, stride=CHUNK), :]
        both = mm(gather[...], jnp.concatenate([left, right], 1).astype(BF16))
        first = both[: 2 * MX, :LANES] + swap(both[2 * MX :, :LANES])
        second = both[: 2 * MX, LANES:] + swap(both[2 * MX :, LANES:])
        real = (first[:MX] + second[MX:]) * factor
        imag = (second[:MX] - first[MX:]) * factor
        real = real.astype(BF16).astype(F32)[:, :C]
        imag = imag.astype(BF16).astype(F32)[:, :C]
        at_m = pl.ds(m * MX, MX)
        hat[0, at_m, :] = real
        hat[1, at_m, :] = imag
        for i in range(OWN):
            weight_real = weight[0, i, at_m, :].astype(F32)
            weight_imag = weight[1, i, at_m, :].astype(F32)
            sum_real = jnp.sum(real * weight_real + imag * weight_imag, 1, keepdims=True)
            sum_imag = jnp.sum(imag * weight_real - real * weight_imag, 1, keepdims=True)
            adjoint = jnp.where(lane == m * OWN + i, sum_real, adjoint)
            adjoint = jnp.where(lane == HALF + m * OWN + i, sum_imag, adjoint)
    turned = swap(adjoint)
    lower = jnp.where(lane < HALF, -turned, turned)
    planes = mm(back[...], jnp.concatenate([adjoint, lower], 0).astype(BF16))
    for plane in range(PLANES):
        rows[pl.ds(plane, SLAB, stride=BACK), :] = planes[plane * SLAB : (plane + 1) * SLAB]
    rider = wide[pl.ds(8, SLAB, stride=CHUNK), :]
    total = jnp.sum(rider, 0, keepdims=True)
    total = jnp.broadcast_to(total, (8, LANES))
    total = two_words((total + swap(total)) * INVERSE_ROOT)
    rows[pl.ds(2, SLAB, stride=BACK), :] = jnp.broadcast_to(total[:1], (SLAB, LANES))
    rows[pl.ds(3, SLAB, stride=BACK), :] = jnp.zeros((SLAB, LANES), F32)
    out[...] = rows[...].astype(BF16)


def adjoint_planes(pencils, weight, scale):
    _, gather, _, back = pencil_tables()
    shapes = (
        jax.ShapeDtypeStruct((2, LOW * MX, C), F32),
        jax.ShapeDtypeStruct((SLAB * BACK, LANES), BF16),
    )
    scratch = [
        pltpu.VMEM((SLAB * CHUNK, LANES), F32),
        pltpu.VMEM((SLAB * BACK, LANES), F32),
    ]
    return call(
        adjoint_kernel, shapes, scratch, 40_000_000,
        pencils, weight, table(gather), table(back), scale,
    )


def outer_kernel(coeff, hat, out):
    modes = coeff[...]
    for m in range(LOW):
        rows = pl.ds(m * MX, MX)
        real = hat[0, rows, :]
        imag = hat[1, rows, :]
        for i in range(OWN):
            at = m * OWN + i
            left = jnp.broadcast_to(modes[:, at : at + 1], (MX, C))
            right = jnp.broadcast_to(modes[:, HALF + at : HALF + at + 1], (MX, C))
            out[0, i, rows, :] = left * real + right * imag
            out[1, i, rows, :] = left * imag - right * real


def outer(coeff, hat):
    shapes = (jax.ShapeDtypeStruct((2, OWN, LOW * MX, C), F32),)
    return call(outer_kernel, shapes, [], 8_000_000, coeff, hat)[0]


def own_modes(own_field):
    cos_z, sin_z, cos_y, sin_y, _, _ = axis_tables()
    forward_z = table(np.stack([cos_z.T, -sin_z.T], 1))
    upper = np.stack([cos_y.T, -sin_y.T], -1)
    lower = np.stack([sin_y.T, cos_y.T], -1)
    forward_y = table(np.stack([upper, lower], 0).reshape(2 * NY, 2 * MY))
    grid_view = own_field.reshape(OWN, PLANES, NY, NZ)
    lines = jnp.einsum("cxyz,zpk->cxkpy", grid_view, forward_z, preferred_element_type=F32)
    lines = lines.astype(BF16).reshape(OWN, PLANES, MZ, 2 * NY)
    modes = jnp.einsum("cxkm,mn->cxkn", lines, forward_y, preferred_element_type=F32)
    modes = modes.astype(BF16).reshape(OWN, PLANES, SLAB, LOW, 2)
    return jnp.transpose(modes, (2, 1, 4, 3, 0)).reshape(SLAB, PLANES, LANES)


def own_grid(planes):
    cos_z, sin_z, cos_y, sin_y, _, _ = axis_tables()
    plain_z = table(np.stack([cos_z, -sin_z], 1))
    real = np.stack([cos_y, sin_y], 1)
    imag = np.stack([-sin_y, cos_y], 1)
    inverse_y = table(np.stack([real, imag], 1).reshape(2 * MY, 2 * NY))
    modes = planes.reshape(SLAB, PLANES, 2, LOW, OWN)
    modes = jnp.transpose(modes, (4, 1, 0, 3, 2)).reshape(OWN, PLANES, MZ, 2 * MY)
    lines = jnp.einsum("cxkn,nm->cxkm", modes, inverse_y, preferred_element_type=F32)
    lines = lines.astype(BF16).reshape(OWN, PLANES, MZ, 2, NY)
    grid = jnp.einsum("cxkpy,kpz->cxyz", lines, plain_z, preferred_element_type=F32)
    return grid.reshape(OWN, PLANES, CELLS)


def over(values, axis):
    return lax.all_to_all(values, axis, split_axis=0, concat_axis=0, tiled=True)


def paired(matrix):
    zero = jnp.zeros_like(matrix)
    upper = jnp.concatenate([matrix, zero], 1)
    lower = jnp.concatenate([zero, matrix], 1)
    return jnp.concatenate([upper, lower], 0)


def body(field, cotangent, spectral_weight, point_weight, point_bias):
    chan_start = lax.axis_index("chan") * OWN
    own_field = lax.dynamic_slice_in_dim(field, chan_start, OWN, 0)
    own_rows = lax.dynamic_slice_in_dim(point_weight, chan_start, OWN, 0)
    weight = jnp.transpose(spectral_weight, (0, 1, 3, 4, 2)).reshape(2, OWN, LOW * MX, C)
    first = own_modes(own_field)
    field, cotangent, own_field, first = lax.optimization_barrier(
        (field, cotangent, own_field, first)
    )
    pencils = over(first, "slab").reshape(NX, LANES)

    cells = jnp.transpose(field, (2, 1, 0)).reshape(CELLS, LANES)
    cot = jnp.transpose(cotangent, (2, 1, 0)).reshape(CELLS, LANES)
    bias = jnp.tile(point_bias.astype(F32), 2)[None]
    base = mm(cells, paired(point_weight)) + bias
    own = jnp.transpose(own_field, (1, 0, 2)).reshape(2 * OWN, CELLS)
    own = jnp.concatenate([own, jnp.ones((8, CELLS), BF16)], 0)

    coeff, parts = mix(pencils, weight)
    parts = over(parts, "chan")
    planes = spread_planes(parts)
    modes = over(planes.reshape(SLAB, 8, LANES), "slab").reshape(SLAB * 8, LANES)
    grad, rows = middle(modes, base, cot, own)
    arrived = over(rows.reshape(SLAB * CHUNK // 2, 2, LANES), "slab").reshape(SLAB * CHUNK, LANES)
    point_back = mm(paired(own_rows), grad.T)
    kz_weight = jnp.where(lax.axis_index("slab") < HIGH, 1.0, 2.0) / (NX * NY * NZ)
    scale = jnp.full((8, LANES), kz_weight, F32)
    hat, rows = adjoint_planes(arrived, weight, scale)
    final = over(rows.reshape(SLAB, BACK, LANES), "slab")
    outer_part = outer(coeff, hat).reshape(2, OWN, LOW, MX, C)
    grad_spectral = jnp.transpose(outer_part, (0, 1, 4, 2, 3))
    point_back = jnp.transpose(point_back.reshape(PLANES, OWN, CELLS), (1, 0, 2))
    grad_input = (own_grid(final[:, :PLANES]) + point_back).astype(BF16)
    words = final[: SHARE * (OWN + 1) : SHARE, 2].astype(F32)
    totals = words[:, :HALF] + words[:, HALF:]
    return grad_input, grad_spectral, totals[:OWN], totals[OWN]


def solution(mesh):
    placed = (
        P(None, "slab", None),
        P(None, "slab", None),
        P(None, "chan", None, "slab", None),
        P(),
        P(),
    )
    return jax.shard_map(
        body,
        mesh=mesh,
        in_specs=placed,
        out_specs=(
            P("chan", "slab", None),
            P(None, "chan", None, "slab", None),
            P("chan", None),
            P(),
        ),
        check_vma=False,
    )
```

```python
import math

import jax
import jax.numpy as jnp
import numpy as np
from jax import lax
from jax.experimental import pallas as pl
from jax.experimental.pallas import tpu as pltpu
from jax.sharding import PartitionSpec as P

MX = 32
MY = 32
MZ = 16
NX = 256
NY = 64
NZ = 64
C = 64
OWN = 16
SLAB = 128
PLANES = 2
LOW = 4
HIGH = 8
CELLS = NY * NZ
LANES = 128
HALF = 64
CHUNK = 10
BACK = 4
SHARE = 7
INVERSE_ROOT = 1.0 / math.sqrt(NX * NY * NZ)
F32 = jnp.float32
BF16 = jnp.bfloat16


def kept(total, length):
    index = np.arange(total)
    return np.where(index < total // 2, index, index - total + length)


def waves(frequency, length):
    wound = (frequency[:, None] * np.arange(length)[None, :]) % length
    angle = np.float32(2.0 * math.pi / length) * wound.astype(np.float32)
    return np.cos(angle), np.sin(angle)


def table(values):
    return jnp.asarray(np.asarray(values, np.float32)).astype(BF16)


def axis_tables():
    cos_z, sin_z = waves(np.arange(MZ), NZ)
    cos_y, sin_y = waves(kept(MY, NY), NY)
    cos_x, sin_x = waves(kept(MX, NX), NX)
    return cos_z, sin_z, cos_y, sin_y, cos_x, sin_x


def rows_of_ky(real, imag):
    both = np.stack([real, imag], 1).reshape(HIGH, LOW, 2, -1)
    return np.transpose(both, (0, 2, 1, 3))


def pack_tables():
    cos_z, sin_z, cos_y, sin_y, cos_x, sin_x = axis_tables()
    weight = (np.where(np.arange(MZ) == 0, 1.0, 2.0) / (NX * NY * NZ))[:, None]
    to_z = np.stack([weight * cos_z, -weight * sin_z], 1).reshape(2 * MZ, NZ).T
    from_z = np.concatenate([cos_z, -sin_z], 0)
    real = np.stack([cos_y, sin_y], 1).reshape(MY, 2 * NY)
    imag = np.stack([-sin_y, cos_y], 1).reshape(MY, 2 * NY)
    to_y = rows_of_ky(real, imag).reshape(2 * MY, 2 * NY).T
    real = np.stack([cos_y, sin_y], 2).reshape(MY, 2 * NY)
    imag = np.stack([-sin_y, cos_y], 2).reshape(MY, 2 * NY)
    from_y = rows_of_ky(real, imag).reshape(HIGH, 8, 2 * NY)
    from_y = np.concatenate([from_y, np.zeros((HIGH, CHUNK - 8, 2 * NY))], 1)
    from_y = from_y.reshape(HIGH * CHUNK, 2 * NY)
    pick = np.zeros((SLAB, 32))
    owner = np.arange(SLAB)
    pick[owner, np.minimum(owner // SHARE, OWN)] = 1.0
    split = np.concatenate([cos_x, sin_x], 0).reshape(2 * MX, SLAB, PLANES)
    gather = np.transpose(split, (2, 0, 1)).reshape(2 * PLANES * MX, SLAB)
    quarter = NY // 4
    cos_q = np.transpose(cos_y[:, :quarter].reshape(HIGH, LOW, quarter), (1, 0, 2))
    sin_q = np.transpose(sin_y[:, :quarter].reshape(HIGH, LOW, quarter), (1, 0, 2))
    lines_z = from_z.reshape(2 * MZ, NZ)
    pair_from_z = np.kron(np.eye(2), lines_z)
    plain_z = np.stack([cos_z, -sin_z], 1).reshape(2 * MZ, NZ)
    pair_to_z = np.kron(np.eye(2), plain_z)
    real = np.stack([cos_q, sin_q], -1)
    imag = np.stack([-sin_q, cos_q], -1)
    own_from_y = np.stack([real, imag], 2).reshape(2 * MY, 2 * quarter)
    real = np.stack([cos_q, -sin_q], -1)
    imag = np.stack([sin_q, cos_q], -1)
    own_to_y = np.stack([real, imag], 1)
    own_to_y = np.pad(own_to_y, ((0, 0), (0, 0), (0, 0), (0, 0), (0, BACK - 2)))
    own_to_y = np.transpose(own_to_y, (0, 1, 3, 2, 4)).reshape(LOW * 2 * quarter, HIGH * BACK)
    parts = dict(
        to_y=to_y, to_z=to_z, from_z=from_z, from_y=from_y, pick=pick,
        gather=gather, spread=gather.T, pair_to_z=pair_to_z, own_to_y=own_to_y,
    )
    early = dict(pair_from_z=pair_from_z, own_from_y=own_from_y)
    places = {}
    packed = []
    for group in (early, parts):
        rows = []
        start = 0
        for name, part in group.items():
            places[name] = (start, part.shape[0], part.shape[1])
            start += part.shape[0]
            rows.append(np.pad(part, ((0, 0), (0, LANES - part.shape[1]))))
        packed.append(np.concatenate(rows, 0))
    return places, packed[0], packed[1]


PLACES, EARLY, PACKED = pack_tables()


def get(tables, name):
    start, rows, lanes = PLACES[name]
    return tables[start : start + rows, :lanes]


def mm(left, right):
    return jnp.dot(left, right, preferred_element_type=F32)


def swap(values):
    return pltpu.roll(values, HALF, 1)


def turn(values, shift):
    return pltpu.roll(values, shift, 1)


def quarter_turns(real, imag, forward):
    lane = lane_of(real.shape)
    even = (lane // 32) % 2 == 0
    sign = jnp.where(lane < HALF, 1.0, -1.0)
    sums, gaps = [], []
    for part in (real, imag):
        other = swap(part)
        sums.append(part + other)
        gaps.append(part - other)
    if forward:
        cross = (gaps[1], -gaps[0])
    else:
        cross = (-gaps[1], gaps[0])
    return [
        jnp.where(even, e + sign * turn(e, 96), sign * turn(d, 32) + c)
        for e, d, c in zip(sums, gaps, cross)
    ]


def by_group(blocks):
    group = lane_of(blocks[0].shape) // 32
    out = blocks[0]
    for index in range(1, 4):
        out = jnp.where(group == index, blocks[index], out)
    return out


def lane_of(shape):
    return lax.broadcasted_iota(jnp.int32, shape, 1)


def gelu_grad(pre_act):
    normal_cdf = 0.5 * (1.0 + lax.erf(pre_act * (1.0 / math.sqrt(2.0))))
    normal_pdf = jnp.exp(-0.5 * pre_act * pre_act) * (1.0 / math.sqrt(2.0 * math.pi))
    return normal_cdf + pre_act * normal_pdf


def two_words(values):
    head = values.astype(BF16).astype(F32)
    rest = values - head
    return jnp.where(lane_of(values.shape) < HALF, head, swap(rest))


def middle_kernel(
    modes, bases, cots, owns, tables, grad_out, out,
    up, flat, down, rows, grad, packed, base, cot, own, sem
):
    loads = [
        pltpu.make_async_copy(source, target, sem.at[index + 3])
        for index, (source, target) in enumerate(((bases, base), (cots, cot), (owns, own)))
    ]
    for load in loads:
        load.start()

    @pl.loop(0, MZ, unroll=4)
    def _(kz):
        start = pl.multiple_of(kz * 64, 64)
        up[pl.ds(pl.multiple_of(kz * 128, 128), 128), :] = mm(
            get(tables, "to_y"), modes[pl.ds(start, 64), :]
        )

    loads[0].wait()

    @pl.loop(0, NY // 2, unroll=4)
    def _(pair):
        left = up[pl.ds(pair * 2, 2 * MZ, stride=NY), :]
        right = up[pl.ds(pair * 2 + 1, 2 * MZ, stride=NY), :]
        both = jnp.concatenate([left, right], 1).astype(BF16)
        grid = mm(get(tables, "to_z"), both)
        start = pl.multiple_of(pair * 128, 128)
        flat[pl.ds(start, 64), :] = grid[:, :LANES] + base[pl.ds(start, 64), :]
        start = pl.multiple_of(pair * 128 + 64, 64)
        flat[pl.ds(start, 64), :] = grid[:, LANES:] + base[pl.ds(start, 64), :]

    loads[1].wait()

    def block_of(block, total):
        here = pl.ds(pl.multiple_of(block * 64, 64), 64)
        values = cot[here, :].astype(F32) * gelu_grad(flat[here, :])
        values = values.astype(BF16)
        grad[here, :] = values
        return total + jnp.sum(values.astype(F32).reshape(8, 8, LANES), 0)

    bias = lax.fori_loop(0, CELLS // 64, block_of, jnp.zeros((8, LANES), F32), unroll=2)
    bias = jnp.broadcast_to(jnp.sum(bias, 0, keepdims=True), (8, LANES))
    save = pltpu.make_async_copy(grad, grad_out, sem.at[0])
    save.start()

    @pl.loop(0, NY // 2, unroll=4)
    def _(pair):
        start = pl.multiple_of(pair * 128, 128)
        left = grad[pl.ds(start, 64), :]
        right = grad[pl.ds(pl.multiple_of(start + 64, 64), 64), :]
        lines = mm(get(tables, "from_z"), jnp.concatenate([left, right], 1))
        start = pl.multiple_of(pair * 64, 64)
        down[pl.ds(start, 32), :] = lines[:, :LANES]
        down[pl.ds(pl.multiple_of(start + 32, 32), 32), :] = lines[:, LANES:]

    loads[2].wait()
    sums = jnp.zeros((2 * OWN, LANES), F32)
    for quarter in range(4):
        cells = pl.ds(quarter * 1024, 1024)
        sums += mm(own[quarter * 32 : quarter * 32 + 32, :], grad[cells, :])
    lower = sums[:OWN] + swap(sums[OWN:])
    bias = bias + swap(bias)
    words = two_words(jnp.concatenate([lower, bias, jnp.zeros_like(bias)], 0)).astype(BF16)

    flat[:SLAB, :] = mm(get(tables, "pick"), words)
    sends = []
    half_rows = SLAB * CHUNK // 2
    for half in range(2):

        @pl.loop(half * MZ // 2, (half + 1) * MZ // 2, unroll=4)
        def _(kz):
            lines = down[pl.ds(kz, 2 * NY, stride=MZ), :].astype(BF16)
            start = pl.multiple_of(kz * HIGH * CHUNK, HIGH * CHUNK)
            rows[pl.ds(start, HIGH * CHUNK), :] = mm(get(tables, "from_y"), lines)

        here = pl.ds(half * half_rows, half_rows)
        rows[pl.ds(half * half_rows + 8, SLAB // 2, stride=CHUNK), :] = flat[
            half * SLAB // 2 : (half + 1) * SLAB // 2, :
        ]
        packed[here, :] = rows[here, :].astype(BF16)
        sends.append(pltpu.make_async_copy(packed.at[here, :], out.at[here, :], sem.at[half + 1]))
        sends[half].start()
    for send in sends + [save]:
        send.wait()


def places(count, anywhere):
    kinds = [pltpu.HBM if index in anywhere else pltpu.VMEM for index in range(count)]
    return [pl.BlockSpec(memory_space=kind) for kind in kinds]


def call(kernel, shapes, scratch, flops, room, *operands, anywhere=(), anywhere_out=()):
    moved = sum(s.size * s.dtype.itemsize for s in list(operands) + list(shapes))
    return pl.pallas_call(
        kernel,
        out_shape=shapes,
        in_specs=places(len(operands), anywhere),
        out_specs=places(len(shapes), anywhere_out),
        scratch_shapes=scratch,
        cost_estimate=pl.CostEstimate(flops=flops, bytes_accessed=moved, transcendentals=0),
        compiler_params=pltpu.CompilerParams(vmem_limit_bytes=room * 2**20),
    )(*operands)


def middle(modes, base, cot, own, tables):
    shapes = (
        jax.ShapeDtypeStruct((CELLS, LANES), BF16),
        jax.ShapeDtypeStruct((SLAB * CHUNK, LANES), BF16),
    )
    scratch = [
        pltpu.VMEM((2 * NY * MZ, LANES), F32),
        pltpu.VMEM((CELLS, LANES), F32),
        pltpu.VMEM((2 * NY * MZ, LANES), F32),
        pltpu.VMEM((SLAB * CHUNK, LANES), F32),
        pltpu.VMEM((CELLS, LANES), BF16),
        pltpu.VMEM((SLAB * CHUNK, LANES), BF16),
        pltpu.VMEM((CELLS, LANES), F32),
        pltpu.VMEM((CELLS, LANES), BF16),
        pltpu.VMEM((LANES, CELLS // 4), BF16),
        pltpu.SemaphoreType.DMA((6,)),
    ]
    return call(
        middle_kernel, shapes, scratch, 400_000_000, 52, modes, base, cot, own, tables,
        anywhere=(1, 2, 3), anywhere_out=(0, 1),
    )


def own_kernel(field, tables, out, lines):
    for pair in range(8):
        part = lax.dot_general(
            get(tables, "pair_from_z"),
            field[:, pair * LANES : (pair + 1) * LANES],
            (((1,), (1,)), ((), ())),
            preferred_element_type=F32,
        )
        for half in range(2):
            top = half * 32
            real, imag = quarter_turns(part[top : top + 16], part[top + 16 : top + 32], True)
            start = (pair * 2 + half) * 32
            lines[start : start + 16, :] = real
            lines[start + 16 : start + 32, :] = imag
    for pair in range(MZ // 2):
        left = lines[pl.ds(2 * pair, 32, stride=MZ), :]
        right = lines[pl.ds(2 * pair + 1, 32, stride=MZ), :]
        both = jnp.concatenate([left, right], 1).astype(BF16)
        both = mm(get(tables, "own_from_y"), both)
        for half in range(2):
            part = both[:, half * LANES : (half + 1) * LANES]
            part = by_group([part[low * 16 : low * 16 + 16] for low in range(LOW)])
            start = (2 * pair + half) * 16
            out[start : start + 16, :] = part.astype(BF16)


def own_modes(own, tables):
    shapes = (jax.ShapeDtypeStruct((2 * SLAB, LANES), BF16),)
    scratch = [pltpu.VMEM((NY // 4 * 2 * MZ, LANES), F32)]
    return call(own_kernel, shapes, scratch, 4_000_000, 8, own, tables)[0]


def grid_kernel(modes, point, tables, out, sums, bias, lines, wide):
    wide[...] = modes[...].astype(F32)
    for kz in range(MZ):
        both = mm(get(tables, "own_to_y"), modes[kz * 32 : kz * 32 + 32, :])
        both = by_group([both[low * 32 : low * 32 + 32] for low in range(LOW)])
        real, imag = quarter_turns(both[:16], both[16:], False)
        lines[kz * 32 : kz * 32 + 16, :] = real
        lines[kz * 32 + 16 : kz * 32 + 32, :] = imag
    for pair in range(8):
        left = lines[pl.ds(2 * pair, 2 * MZ, stride=16), :]
        right = lines[pl.ds(2 * pair + 1, 2 * MZ, stride=16), :]
        both = jnp.concatenate([left, right], 0).T.astype(BF16)
        both = mm(both, get(tables, "pair_to_z"))
        for quarter in range(4):
            start = quarter * 1024 + pair * LANES
            here = both[quarter * 32 : quarter * 32 + 32] + point[:, start : start + LANES]
            out[:, start : start + LANES] = here.astype(BF16)
    words = wide[pl.ds(2, OWN, stride=BACK * SHARE), :]
    sums[...] = (words + swap(words))[:, :HALF]
    words = wide[pl.ds(BACK * SHARE * OWN + 2, 8, stride=1), :]
    bias[...] = (words + swap(words))[:1, :HALF]


def own_grid(modes, point, tables):
    shapes = (
        jax.ShapeDtypeStruct((2 * OWN, CELLS), BF16),
        jax.ShapeDtypeStruct((OWN, C), F32),
        jax.ShapeDtypeStruct((1, C), F32),
    )
    scratch = [pltpu.VMEM((2 * NY // 4 * MZ, LANES), F32), pltpu.VMEM((SLAB * BACK, LANES), F32)]
    return call(grid_kernel, shapes, scratch, 8_000_000, 8, modes, point, tables)


def along_x(tables, left, right):
    both = mm(get(tables, "gather"), jnp.concatenate([left, right], 1).astype(BF16))
    return both[: 2 * MX], both[2 * MX :]


def mix_kernel(pencils, weight, tables, coeff, out, wide):
    wide[...] = pencils[...].astype(F32)
    left = wide[pl.ds(0, SLAB, stride=2), :]
    right = wide[pl.ds(1, SLAB, stride=2), :]
    near, far = along_x(tables, left, right)
    near = near + jnp.concatenate([turn(far[:, :LANES], 112), turn(far[:, LANES:], 112)], 1)
    modes_real = (near[:MX, :LANES] + near[MX:, LANES:]).astype(BF16).astype(F32)
    modes_imag = (near[:MX, LANES:] - near[MX:, :LANES]).astype(BF16).astype(F32)
    coeff[0] = modes_real
    coeff[1] = modes_imag
    for m in range(LOW):
        rows = pl.ds(m * MX, MX)
        real = jnp.zeros((MX, C), F32)
        imag = jnp.zeros((MX, C), F32)
        for i in range(OWN):
            at = m * 32 + i
            left = jnp.broadcast_to(modes_real[:, at : at + 1], (MX, C))
            right = jnp.broadcast_to(modes_imag[:, at : at + 1], (MX, C))
            weight_real = weight[0, i, rows, :].astype(F32)
            weight_imag = weight[1, i, rows, :].astype(F32)
            real += left * weight_real - right * weight_imag
            imag += left * weight_imag + right * weight_real
        part = jnp.concatenate([real, imag], 1).astype(BF16)
        for peer in range(4):
            out[peer, rows, :] = part


def mix(pencils, weight, tables):
    shapes = (
        jax.ShapeDtypeStruct((2, MX, LANES), F32),
        jax.ShapeDtypeStruct((4, LOW * MX, LANES), BF16),
    )
    scratch = [pltpu.VMEM((2 * SLAB, LANES), F32)]
    return call(mix_kernel, shapes, scratch, 4_000_000, 8, pencils, weight, tables)


def spread_kernel(parts, tables, out, rows):
    total = parts[0].astype(F32)
    for peer in range(1, 4):
        total += parts[peer].astype(F32)
    lane = lane_of((MX, LANES))
    for m in range(LOW):
        here = total[m * MX : (m + 1) * MX]
        there = swap(here)
        zero = jnp.zeros_like(here)
        a = jnp.where(lane < HALF, here, zero)
        b = jnp.where(lane < HALF, there, zero)
        c = jnp.where(lane < HALF, zero, there)
        d = jnp.where(lane < HALF, zero, here)
        top = jnp.concatenate([a, b], 1)
        second = jnp.concatenate([-b, a], 1)
        third = jnp.concatenate([c, d], 1)
        last = jnp.concatenate([-d, c], 1)
        block = jnp.concatenate([top, second, third, last], 0).astype(BF16)
        planes = mm(get(tables, "spread"), block)
        rows[pl.ds(m, SLAB, stride=8), :] = planes[:, :LANES]
        rows[pl.ds(LOW + m, SLAB, stride=8), :] = planes[:, LANES:]
    out[...] = rows[...].astype(BF16)


def spread_planes(parts, tables):
    shapes = (jax.ShapeDtypeStruct((SLAB * 8, LANES), BF16),)
    scratch = [pltpu.VMEM((SLAB * 8, LANES), F32)]
    return call(spread_kernel, shapes, scratch, 40_000_000, 8, parts, tables)[0]


def adjoint_kernel(pencils, weights, tables, scale, hat, out, wide, rows, weight, sem):
    load = pltpu.make_async_copy(weights, weight, sem)
    load.start()
    wide[...] = pencils[...].astype(F32)
    lane = lane_of((MX, LANES))
    near_real = jnp.zeros((MX, LANES), F32)
    near_imag = jnp.zeros((MX, LANES), F32)
    factor = scale[0:1, :]
    for m in range(LOW):
        left = wide[pl.ds(m, SLAB, stride=CHUNK), :]
        right = wide[pl.ds(LOW + m, SLAB, stride=CHUNK), :]
        near, far = along_x(tables, left, right)
        first = near[:, :LANES] + swap(far[:, :LANES])
        second = near[:, LANES:] + swap(far[:, LANES:])
        real = (first[:MX] + second[MX:]) * factor
        imag = (second[:MX] - first[MX:]) * factor
        hat[0, pl.ds(m * MX, MX), :] = real.astype(BF16).astype(F32)[:, :C]
        hat[1, pl.ds(m * MX, MX), :] = imag.astype(BF16).astype(F32)[:, :C]
    load.wait()
    for m in range(LOW):
        at_m = pl.ds(m * MX, MX)
        real = hat[0, at_m, :]
        imag = hat[1, at_m, :]
        for i in range(OWN):
            weight_real = weight[0, i, at_m, :].astype(F32)
            weight_imag = weight[1, i, at_m, :].astype(F32)
            sum_real = jnp.sum(real * weight_real + imag * weight_imag, 1, keepdims=True)
            sum_imag = jnp.sum(imag * weight_real - real * weight_imag, 1, keepdims=True)
            near_real = jnp.where(lane == m * 32 + i, sum_real, near_real)
            near_imag = jnp.where(lane == m * 32 + i, sum_imag, near_imag)
    far_real = turn(near_real, 16)
    far_imag = turn(near_imag, 16)
    top = jnp.concatenate([near_real, near_imag], 1)
    second = jnp.concatenate([-near_imag, near_real], 1)
    third = jnp.concatenate([far_real, far_imag], 1)
    last = jnp.concatenate([-far_imag, far_real], 1)
    block = jnp.concatenate([top, second, third, last], 0).astype(BF16)
    planes = mm(get(tables, "spread"), block)
    rows[pl.ds(0, SLAB, stride=BACK), :] = planes[:, :LANES]
    rows[pl.ds(1, SLAB, stride=BACK), :] = planes[:, LANES:]
    rider = wide[pl.ds(8, SLAB, stride=CHUNK), :]
    total = jnp.sum(rider, 0, keepdims=True)
    total = jnp.broadcast_to(total, (8, LANES))
    total = two_words((total + swap(total)) * INVERSE_ROOT)
    rows[pl.ds(2, SLAB, stride=BACK), :] = jnp.broadcast_to(total[:1], (SLAB, LANES))
    rows[pl.ds(3, SLAB, stride=BACK), :] = jnp.zeros((SLAB, LANES), F32)
    out[...] = rows[...].astype(BF16)


def adjoint_planes(pencils, weight, tables, scale):
    shapes = (
        jax.ShapeDtypeStruct((2, LOW * MX, C), F32),
        jax.ShapeDtypeStruct((SLAB * BACK, LANES), BF16),
    )
    scratch = [
        pltpu.VMEM((SLAB * CHUNK, LANES), F32),
        pltpu.VMEM((SLAB * BACK, LANES), F32),
        pltpu.VMEM((2, OWN, LOW * MX, C), BF16),
        pltpu.SemaphoreType.DMA,
    ]
    return call(
        adjoint_kernel, shapes, scratch, 40_000_000, 50, pencils, weight, tables, scale, anywhere=(1,)
    )


def outer_kernel(coeff, hat, out):
    modes_real = coeff[0]
    modes_imag = coeff[1]
    for m in range(LOW):
        rows = pl.ds(m * MX, MX)
        real = hat[0, rows, :]
        imag = hat[1, rows, :]
        for i in range(OWN):
            at = m * 32 + i
            left = jnp.broadcast_to(modes_real[:, at : at + 1], (MX, C))
            right = jnp.broadcast_to(modes_imag[:, at : at + 1], (MX, C))
            out[0, i, rows, :] = left * real + right * imag
            out[1, i, rows, :] = left * imag - right * real


def outer(coeff, hat):
    shapes = (jax.ShapeDtypeStruct((2, OWN, LOW * MX, C), F32),)
    return call(outer_kernel, shapes, [], 8_000_000, 8, coeff, hat)[0]


def over(values, axis):
    return lax.all_to_all(values, axis, split_axis=0, concat_axis=0, tiled=True)


def paired(matrix):
    zero = jnp.zeros_like(matrix)
    upper = jnp.concatenate([matrix, zero], 1)
    lower = jnp.concatenate([zero, matrix], 1)
    return jnp.concatenate([upper, lower], 0)


def body(field, cotangent, spectral_weight, point_weight, point_bias):
    chan_start = lax.axis_index("chan") * OWN
    own = lax.dynamic_slice_in_dim(field, chan_start, OWN, 0)
    own = jnp.transpose(own.reshape(OWN, PLANES, 4, CELLS // 4), (2, 1, 0, 3))
    own = own.reshape(LANES, CELLS // 4)
    own_rows = lax.dynamic_slice_in_dim(point_weight, chan_start, OWN, 0)
    weight = jnp.transpose(spectral_weight, (0, 1, 3, 4, 2)).reshape(2, OWN, LOW * MX, C)
    tables = table(PACKED)
    first = own_modes(own, table(EARLY))
    field, cotangent, first = lax.optimization_barrier((field, cotangent, first))
    pencils = over(first.reshape(SLAB, PLANES, LANES), "slab").reshape(NX, LANES)

    cells = jnp.transpose(field, (2, 1, 0)).reshape(CELLS, LANES)
    cot = jnp.transpose(cotangent, (2, 1, 0)).reshape(CELLS, LANES)
    bias = jnp.tile(point_bias.astype(F32), 2)[None]
    base = mm(cells, paired(point_weight)) + bias
    coeff, parts = mix(pencils, weight, tables)
    parts = over(parts, "chan")
    planes = spread_planes(parts, tables)
    modes = over(planes.reshape(SLAB, 8, LANES), "slab").reshape(SLAB * 8, LANES)
    grad, rows = middle(modes, base, cot, own, tables)
    arrived = over(rows.reshape(SLAB * CHUNK // 2, 2, LANES), "slab").reshape(SLAB * CHUNK, LANES)
    point_back = mm(paired(own_rows), grad.T)
    kz_weight = jnp.where(lax.axis_index("slab") < HIGH, 1.0, 2.0) / (NX * NY * NZ)
    scale = jnp.full((8, LANES), kz_weight, F32)
    hat, rows = adjoint_planes(arrived, weight, tables, scale)
    final = over(rows.reshape(SLAB, BACK, LANES), "slab").reshape(SLAB * BACK, LANES)
    outer_part = outer(coeff, hat).reshape(2, OWN, LOW, MX, C)
    grad_spectral = jnp.transpose(outer_part, (0, 1, 4, 2, 3))
    planes, grad_pointwise, grad_bias = own_grid(final, point_back, tables)
    grad_input = jnp.transpose(planes.reshape(PLANES, OWN, CELLS), (1, 0, 2))
    return grad_input, grad_spectral, grad_pointwise, grad_bias[0]


def solution(mesh):
    placed = (
        P(None, "slab", None),
        P(None, "slab", None),
        P(None, "chan", None, "slab", None),
        P(),
        P(),
    )
    return jax.shard_map(
        body,
        mesh=mesh,
        in_specs=placed,
        out_specs=(
            P("chan", "slab", None),
            P(None, "chan", None, "slab", None),
            P("chan", None),
            P(),
        ),
        check_vma=False,
    )
```

```python
import math

import jax
import jax.numpy as jnp
import numpy as np
from jax import lax
from jax.experimental import pallas as pl
from jax.experimental.pallas import tpu as pltpu
from jax.sharding import PartitionSpec as P

MX = 32
MY = 32
MZ = 16
NX = 256
NY = 64
NZ = 64
C = 64
OWN = 16
SLAB = 128
PLANES = 2
LOW = 4
HIGH = 8
CELLS = NY * NZ
LANES = 128
HALF = 64
CHUNK = 10
BACK = 4
SHARE = 7
INVERSE_ROOT = 1.0 / math.sqrt(NX * NY * NZ)
F32 = jnp.float32
BF16 = jnp.bfloat16


def kept(total, length):
    index = np.arange(total)
    return np.where(index < total // 2, index, index - total + length)


def waves(frequency, length):
    wound = (frequency[:, None] * np.arange(length)[None, :]) % length
    angle = np.float32(2.0 * math.pi / length) * wound.astype(np.float32)
    return np.cos(angle), np.sin(angle)


def table(values):
    return jnp.asarray(np.asarray(values, np.float32)).astype(BF16)


def axis_tables():
    cos_z, sin_z = waves(np.arange(MZ), NZ)
    cos_y, sin_y = waves(kept(MY, NY), NY)
    cos_x, sin_x = waves(kept(MX, NX), NX)
    return cos_z, sin_z, cos_y, sin_y, cos_x, sin_x


def rows_of_ky(real, imag):
    both = np.stack([real, imag], 1).reshape(HIGH, LOW, 2, -1)
    return np.transpose(both, (0, 2, 1, 3))


def pack_tables():
    cos_z, sin_z, cos_y, sin_y, cos_x, sin_x = axis_tables()
    weight = (np.where(np.arange(MZ) == 0, 1.0, 2.0) / (NX * NY * NZ))[:, None]
    plain_z = np.stack([cos_z, -sin_z], 1)
    wide = plain_z[:, :, None, None, :] * np.eye(8)[None, None, :, :, None]
    tall = (weight[:, :, None, None, None] * wide).reshape(256, 512).T
    wide = wide.reshape(256, 512)
    real = np.stack([cos_y, sin_y], 1).reshape(MY, 2 * NY)
    imag = np.stack([-sin_y, cos_y], 1).reshape(MY, 2 * NY)
    to_y = rows_of_ky(real, imag).reshape(2 * MY, 2 * NY).T
    from_y = rows_of_ky(real, imag).reshape(HIGH, 8, 2 * NY)
    from_y = np.concatenate([from_y, np.zeros((HIGH, CHUNK - 8, 2 * NY))], 1)
    from_y = from_y.reshape(HIGH * CHUNK, 2 * NY)
    pick = np.zeros((SLAB, 32))
    owner = np.arange(SLAB)
    pick[owner, np.minimum(owner // SHARE, OWN)] = 1.0
    split = np.concatenate([cos_x, sin_x], 0).reshape(2 * MX, SLAB, PLANES)
    gather = np.transpose(split, (2, 0, 1)).reshape(2 * PLANES * MX, SLAB)
    quarter = NY // 4
    cos_q = np.transpose(cos_y[:, :quarter].reshape(HIGH, LOW, quarter), (1, 0, 2))
    sin_q = np.transpose(sin_y[:, :quarter].reshape(HIGH, LOW, quarter), (1, 0, 2))
    real = np.stack([cos_q, sin_q], 2)
    imag = np.stack([-sin_q, cos_q], 2)
    own_from_y = np.stack([real, imag], 2).reshape(2 * MY, 2 * quarter)
    real = np.stack([cos_q, -sin_q], -1)
    imag = np.stack([sin_q, cos_q], -1)
    own_to_y = np.stack([real, imag], 1)
    own_to_y = np.pad(own_to_y, ((0, 0), (0, 0), (0, 0), (0, 0), (0, BACK - 2)))
    own_to_y = np.transpose(own_to_y, (0, 1, 3, 2, 4)).reshape(LOW * 2 * quarter, HIGH * BACK)
    parts = dict(
        to_y=to_y, from_y=from_y, pick=pick, gather=gather, spread=gather.T,
    )
    side = np.zeros((256, LANES))
    side[: 2 * MY, : 2 * quarter] = own_from_y
    side[2 * MY : 2 * MY + 8 * quarter, : HIGH * BACK] = own_to_y
    wide = np.concatenate([wide, side], 1)
    places = {}
    rows = []
    start = 0
    for name, part in parts.items():
        places[name] = (start, part.shape[0], part.shape[1])
        start += part.shape[0]
        rows.append(np.pad(part, ((0, 0), (0, LANES - part.shape[1]))))
    return places, np.concatenate(rows, 0), wide, tall


PLACES, PACKED, WIDE, TALL = pack_tables()


def wide_part(wide):
    return wide[:, :512]


def own_from_y(wide):
    return wide[:64, 512:544]


def own_to_y(wide):
    return wide[64:192, 512:544]


def get(tables, name):
    start, rows, lanes = PLACES[name]
    return tables[start : start + rows, :lanes]


def mm(left, right):
    return jnp.dot(left, right, preferred_element_type=F32)


def swap(values):
    return pltpu.roll(values, HALF, 1)


def turn(values, shift):
    return pltpu.roll(values, shift, 1)


def quarter_turns(real, imag, forward):
    lane = lane_of(real.shape)
    even = (lane // 32) % 2 == 0
    sign = jnp.where(lane < HALF, 1.0, -1.0)
    sums, gaps = [], []
    for part in (real, imag):
        other = swap(part)
        sums.append(part + other)
        gaps.append(part - other)
    if forward:
        cross = (gaps[1], -gaps[0])
    else:
        cross = (-gaps[1], gaps[0])
    return [
        jnp.where(even, e + sign * turn(e, 96), sign * turn(d, 32) + c)
        for e, d, c in zip(sums, gaps, cross)
    ]


def by_group(blocks):
    group = lane_of(blocks[0].shape) // 32
    out = blocks[0]
    for index in range(1, 4):
        out = jnp.where(group == index, blocks[index], out)
    return out


def lane_of(shape):
    return lax.broadcasted_iota(jnp.int32, shape, 1)


def gelu_grad(pre_act):
    normal_cdf = 0.5 + 0.5 * lax.erf(pre_act * (1.0 / math.sqrt(2.0)))
    bell = jnp.exp2(pre_act * pre_act * (-0.5 * math.log2(math.e)))
    return normal_cdf + (pre_act * (1.0 / math.sqrt(2.0 * math.pi))) * bell


def two_words(values):
    head = values.astype(BF16).astype(F32)
    rest = values - head
    return jnp.where(lane_of(values.shape) < HALF, head, swap(rest))


def middle_kernel(
    modes, bases, cots, own, wide, tall, tables, grad_out, out,
    up, flat, down, rows, grad, packed, base, cot, sem
):
    pairs = ((bases, base), (cots, cot))
    loads = [
        pltpu.make_async_copy(source, target, sem.at[index + 3])
        for index, (source, target) in enumerate(pairs)
    ]
    for load in loads:
        load.start()

    @pl.loop(0, MZ, unroll=4)
    def _(kz):
        start = pl.multiple_of(kz * 64, 64)
        lines = mm(get(tables, "to_y"), modes[pl.ds(start, 64), :])
        up[pl.ds(2 * kz, 2), :, :] = lines.reshape(2, NY, LANES)

    loads[0].wait()
    for pair in range(4):
        sides = [
            up[:, (2 * pair + side) * 8 : (2 * pair + side) * 8 + 8, :].reshape(256, LANES)
            for side in range(2)
        ]
        grid = mm(tall[...], jnp.concatenate(sides, 1).astype(BF16))
        for side in range(2):
            cells = pl.ds((2 * pair + side) * 512, 512)
            flat[cells, :] = grid[:, side * LANES : (side + 1) * LANES] + base[cells, :]
    loads[1].wait()

    @pl.loop(0, CELLS // 64, unroll=4)
    def _(block):
        here = pl.ds(pl.multiple_of(block * 64, 64), 64)
        grad[here, :] = (cot[here, :].astype(F32) * gelu_grad(flat[here, :])).astype(BF16)

    save = pltpu.make_async_copy(grad, grad_out, sem.at[0])
    save.start()
    for pair in range(4):
        sides = [grad[(2 * pair + side) * 512 : (2 * pair + side) * 512 + 512, :] for side in range(2)]
        lines = mm(wide_part(wide), jnp.concatenate(sides, 1)).reshape(2 * MZ, 8, 2 * LANES)
        for side in range(2):
            group = (2 * pair + side) * 8
            down[:, group : group + 8, :] = lines[:, :, side * LANES : (side + 1) * LANES]

    sums = jnp.zeros((3 * OWN, LANES), F32)
    for quarter in range(4):
        cells = pl.ds(quarter * 1024, 1024)
        left = own[quarter * 32 : quarter * 32 + 32, :]
        left = jnp.concatenate([left, jnp.ones((OWN, CELLS // 4), BF16)], 0)
        sums += mm(left, grad[cells, :])
    lower = sums[:OWN] + swap(sums[OWN : 2 * OWN])
    bias = sums[2 * OWN : 2 * OWN + 8] + swap(sums[2 * OWN : 2 * OWN + 8])
    words = two_words(jnp.concatenate([lower, bias, jnp.zeros_like(bias)], 0)).astype(BF16)

    flat[:SLAB, :] = mm(get(tables, "pick"), words)
    sends = []
    half_rows = SLAB * CHUNK // 2
    for half in range(2):

        @pl.loop(half * MZ // 2, (half + 1) * MZ // 2, unroll=4)
        def _(kz):
            lines = down[pl.ds(2 * kz, 2), :, :].reshape(2 * NY, LANES).astype(BF16)
            start = pl.multiple_of(kz * HIGH * CHUNK, HIGH * CHUNK)
            rows[pl.ds(start, HIGH * CHUNK), :] = mm(get(tables, "from_y"), lines)

        here = pl.ds(half * half_rows, half_rows)
        rows[pl.ds(half * half_rows + 8, SLAB // 2, stride=CHUNK), :] = flat[
            half * SLAB // 2 : (half + 1) * SLAB // 2, :
        ]
        packed[here, :] = rows[here, :].astype(BF16)
        sends.append(pltpu.make_async_copy(packed.at[here, :], out.at[here, :], sem.at[half + 1]))
        sends[half].start()
    for send in sends + [save]:
        send.wait()


def places(count, anywhere):
    kinds = [pltpu.HBM if index in anywhere else pltpu.VMEM for index in range(count)]
    return [pl.BlockSpec(memory_space=kind) for kind in kinds]


def call(kernel, shapes, scratch, flops, room, *operands, anywhere=(), anywhere_out=()):
    moved = sum(s.size * s.dtype.itemsize for s in list(operands) + list(shapes))
    return pl.pallas_call(
        kernel,
        out_shape=shapes,
        in_specs=places(len(operands), anywhere),
        out_specs=places(len(shapes), anywhere_out),
        scratch_shapes=scratch,
        cost_estimate=pl.CostEstimate(flops=flops, bytes_accessed=moved, transcendentals=0),
        compiler_params=pltpu.CompilerParams(vmem_limit_bytes=room * 2**20),
    )(*operands)


def middle(modes, base, cot, own, wide, tables):
    shapes = (
        jax.ShapeDtypeStruct((CELLS, LANES), BF16),
        jax.ShapeDtypeStruct((SLAB * CHUNK, LANES), BF16),
    )
    scratch = [
        pltpu.VMEM((2 * MZ, NY, LANES), F32),
        pltpu.VMEM((CELLS, LANES), F32),
        pltpu.VMEM((2 * MZ, NY, LANES), F32),
        pltpu.VMEM((SLAB * CHUNK, LANES), F32),
        pltpu.VMEM((CELLS, LANES), BF16),
        pltpu.VMEM((SLAB * CHUNK, LANES), BF16),
        pltpu.VMEM((CELLS, LANES), F32),
        pltpu.VMEM((CELLS, LANES), BF16),
        pltpu.SemaphoreType.DMA((5,)),
    ]
    return call(
        middle_kernel, shapes, scratch, 400_000_000, 52,
        modes, base, cot, own, wide, table(TALL), tables,
        anywhere=(1, 2), anywhere_out=(0, 1),
    )


def own_kernel(field, wide, out, lines):
    for group in range(2):
        part = lax.dot_general(
            wide_part(wide),
            field[:, group * 512 : (group + 1) * 512],
            (((1,), (1,)), ((), ())),
            preferred_element_type=F32,
        ).reshape(MZ, 2, 8, LANES)
        real = part[:, 0].reshape(MZ * 8, LANES)
        imag = part[:, 1].reshape(MZ * 8, LANES)
        real, imag = quarter_turns(real, imag, True)
        lines[:, 0, group * 8 : group * 8 + 8, :] = real.reshape(MZ, 8, LANES)
        lines[:, 1, group * 8 : group * 8 + 8, :] = imag.reshape(MZ, 8, LANES)
    for pair in range(MZ // 2):
        left = lines[2 * pair].reshape(32, LANES)
        right = lines[2 * pair + 1].reshape(32, LANES)
        both = jnp.concatenate([left, right], 1).astype(BF16)
        both = mm(own_from_y(wide), both)
        for half in range(2):
            part = both[:, half * LANES : (half + 1) * LANES]
            part = by_group([part[low * 16 : low * 16 + 16] for low in range(LOW)])
            start = (2 * pair + half) * 16
            out[start : start + 16, :] = part.astype(BF16)


def own_modes(own, wide):
    shapes = (jax.ShapeDtypeStruct((2 * SLAB, LANES), BF16),)
    scratch = [pltpu.VMEM((MZ, 2, NY // 4, LANES), F32)]
    return call(own_kernel, shapes, scratch, 4_000_000, 8, own, wide)[0]


def grid_kernel(modes, point, wide_z, out, sums, bias, lines, wide):
    wide[...] = modes[...].astype(F32)
    for kz in range(MZ):
        both = mm(own_to_y(wide_z), modes[kz * 32 : kz * 32 + 32, :])
        both = by_group([both[low * 32 : low * 32 + 32] for low in range(LOW)])
        real, imag = quarter_turns(both[:16], both[16:], False)
        lines[kz, 0] = real
        lines[kz, 1] = imag
    for group in range(2):
        both = lines[:, :, group * 8 : group * 8 + 8, :].reshape(256, LANES)
        both = mm(both.T.astype(BF16), wide_part(wide_z))
        for quarter in range(4):
            cells = pl.ds(quarter * 1024 + group * 512, 512)
            here = both[quarter * 32 : quarter * 32 + 32] + point[:, cells]
            out[:, cells] = here.astype(BF16)
    words = wide[pl.ds(2, OWN, stride=BACK * SHARE), :]
    sums[...] = (words + swap(words))[:, :HALF]
    words = wide[pl.ds(BACK * SHARE * OWN + 2, 8, stride=1), :]
    bias[...] = (words + swap(words))[:1, :HALF]


def own_grid(modes, point, wide):
    shapes = (
        jax.ShapeDtypeStruct((2 * OWN, CELLS), BF16),
        jax.ShapeDtypeStruct((OWN, C), F32),
        jax.ShapeDtypeStruct((1, C), F32),
    )
    scratch = [pltpu.VMEM((MZ, 2, NY // 4, LANES), F32), pltpu.VMEM((SLAB * BACK, LANES), F32)]
    return call(grid_kernel, shapes, scratch, 8_000_000, 8, modes, point, wide)


def along_x(tables, left, right):
    both = mm(get(tables, "gather"), jnp.concatenate([left, right], 1).astype(BF16))
    return both[: 2 * MX], both[2 * MX :]


def mix_kernel(pencils, weight, tables, coeff, out, wide):
    wide[...] = pencils[...].astype(F32)
    left = wide[pl.ds(0, SLAB, stride=2), :]
    right = wide[pl.ds(1, SLAB, stride=2), :]
    near, far = along_x(tables, left, right)
    near = near + jnp.concatenate([turn(far[:, :LANES], 112), turn(far[:, LANES:], 112)], 1)
    modes_real = (near[:MX, :LANES] + near[MX:, LANES:]).astype(BF16).astype(F32)
    modes_imag = (near[:MX, LANES:] - near[MX:, :LANES]).astype(BF16).astype(F32)
    coeff[0] = modes_real
    coeff[1] = modes_imag
    for m in range(LOW):
        rows = pl.ds(m * MX, MX)
        real = jnp.zeros((MX, C), F32)
        imag = jnp.zeros((MX, C), F32)
        for i in range(OWN):
            at = m * 32 + i
            left = jnp.broadcast_to(modes_real[:, at : at + 1], (MX, C))
            right = jnp.broadcast_to(modes_imag[:, at : at + 1], (MX, C))
            weight_real = weight[0, i, rows, :].astype(F32)
            weight_imag = weight[1, i, rows, :].astype(F32)
            real += left * weight_real - right * weight_imag
            imag += left * weight_imag + right * weight_real
        part = jnp.concatenate([real, imag], 1).astype(BF16)
        for peer in range(4):
            out[peer, rows, :] = part


def mix(pencils, weight, tables):
    shapes = (
        jax.ShapeDtypeStruct((2, MX, LANES), F32),
        jax.ShapeDtypeStruct((4, LOW * MX, LANES), BF16),
    )
    scratch = [pltpu.VMEM((2 * SLAB, LANES), F32)]
    return call(mix_kernel, shapes, scratch, 4_000_000, 8, pencils, weight, tables)


def spread_kernel(parts, tables, out, rows):
    total = parts[0].astype(F32)
    for peer in range(1, 4):
        total += parts[peer].astype(F32)
    lane = lane_of((MX, LANES))
    for m in range(LOW):
        here = total[m * MX : (m + 1) * MX]
        there = swap(here)
        zero = jnp.zeros_like(here)
        a = jnp.where(lane < HALF, here, zero)
        b = jnp.where(lane < HALF, there, zero)
        c = jnp.where(lane < HALF, zero, there)
        d = jnp.where(lane < HALF, zero, here)
        top = jnp.concatenate([a, b], 1)
        second = jnp.concatenate([-b, a], 1)
        third = jnp.concatenate([c, d], 1)
        last = jnp.concatenate([-d, c], 1)
        block = jnp.concatenate([top, second, third, last], 0).astype(BF16)
        planes = mm(get(tables, "spread"), block)
        rows[pl.ds(m, SLAB, stride=8), :] = planes[:, :LANES]
        rows[pl.ds(LOW + m, SLAB, stride=8), :] = planes[:, LANES:]
    out[...] = rows[...].astype(BF16)


def spread_planes(parts, tables):
    shapes = (jax.ShapeDtypeStruct((SLAB * 8, LANES), BF16),)
    scratch = [pltpu.VMEM((SLAB * 8, LANES), F32)]
    return call(spread_kernel, shapes, scratch, 40_000_000, 8, parts, tables)[0]


def adjoint_kernel(pencils, weights, tables, scale, hat, out, wide, rows, weight, sem):
    load = pltpu.make_async_copy(weights, weight, sem)
    load.start()
    wide[...] = pencils[...].astype(F32)
    lane = lane_of((MX, LANES))
    near_real = jnp.zeros((MX, LANES), F32)
    near_imag = jnp.zeros((MX, LANES), F32)
    factor = scale[0:1, :]
    for m in range(LOW):
        left = wide[pl.ds(m, SLAB, stride=CHUNK), :]
        right = wide[pl.ds(LOW + m, SLAB, stride=CHUNK), :]
        near, far = along_x(tables, left, right)
        first = near[:, :LANES] + swap(far[:, :LANES])
        second = near[:, LANES:] + swap(far[:, LANES:])
        real = (first[:MX] + second[MX:]) * factor
        imag = (second[:MX] - first[MX:]) * factor
        hat[0, pl.ds(m * MX, MX), :] = real.astype(BF16).astype(F32)[:, :C]
        hat[1, pl.ds(m * MX, MX), :] = imag.astype(BF16).astype(F32)[:, :C]
    load.wait()
    for m in range(LOW):
        at_m = pl.ds(m * MX, MX)
        real = hat[0, at_m, :]
        imag = hat[1, at_m, :]
        for i in range(OWN):
            weight_real = weight[0, i, at_m, :].astype(F32)
            weight_imag = weight[1, i, at_m, :].astype(F32)
            sum_real = jnp.sum(real * weight_real + imag * weight_imag, 1, keepdims=True)
            sum_imag = jnp.sum(imag * weight_real - real * weight_imag, 1, keepdims=True)
            near_real = jnp.where(lane == m * 32 + i, sum_real, near_real)
            near_imag = jnp.where(lane == m * 32 + i, sum_imag, near_imag)
    far_real = turn(near_real, 16)
    far_imag = turn(near_imag, 16)
    top = jnp.concatenate([near_real, near_imag], 1)
    second = jnp.concatenate([-near_imag, near_real], 1)
    third = jnp.concatenate([far_real, far_imag], 1)
    last = jnp.concatenate([-far_imag, far_real], 1)
    block = jnp.concatenate([top, second, third, last], 0).astype(BF16)
    planes = mm(get(tables, "spread"), block)
    rows[pl.ds(0, SLAB, stride=BACK), :] = planes[:, :LANES]
    rows[pl.ds(1, SLAB, stride=BACK), :] = planes[:, LANES:]
    rider = wide[pl.ds(8, SLAB, stride=CHUNK), :]
    total = jnp.sum(rider, 0, keepdims=True)
    total = jnp.broadcast_to(total, (8, LANES))
    total = two_words((total + swap(total)) * INVERSE_ROOT)
    rows[pl.ds(2, SLAB, stride=BACK), :] = jnp.broadcast_to(total[:1], (SLAB, LANES))
    rows[pl.ds(3, SLAB, stride=BACK), :] = jnp.zeros((SLAB, LANES), F32)
    out[...] = rows[...].astype(BF16)


def adjoint_planes(pencils, weight, tables, scale):
    shapes = (
        jax.ShapeDtypeStruct((2, LOW * MX, C), F32),
        jax.ShapeDtypeStruct((SLAB * BACK, LANES), BF16),
    )
    scratch = [
        pltpu.VMEM((SLAB * CHUNK, LANES), F32),
        pltpu.VMEM((SLAB * BACK, LANES), F32),
        pltpu.VMEM((2, OWN, LOW * MX, C), BF16),
        pltpu.SemaphoreType.DMA,
    ]
    return call(
        adjoint_kernel, shapes, scratch, 40_000_000, 50, pencils, weight, tables, scale, anywhere=(1,)
    )


def outer_kernel(coeff, hat, out):
    modes_real = coeff[0]
    modes_imag = coeff[1]
    for m in range(LOW):
        rows = pl.ds(m * MX, MX)
        real = hat[0, rows, :]
        imag = hat[1, rows, :]
        for i in range(OWN):
            at = m * 32 + i
            left = jnp.broadcast_to(modes_real[:, at : at + 1], (MX, C))
            right = jnp.broadcast_to(modes_imag[:, at : at + 1], (MX, C))
            out[0, i, rows, :] = left * real + right * imag
            out[1, i, rows, :] = left * imag - right * real


def outer(coeff, hat):
    shapes = (jax.ShapeDtypeStruct((2, OWN, LOW * MX, C), F32),)
    return call(outer_kernel, shapes, [], 8_000_000, 8, coeff, hat)[0]


def over(values, axis):
    return lax.all_to_all(values, axis, split_axis=0, concat_axis=0, tiled=True)


def paired(matrix):
    zero = jnp.zeros_like(matrix)
    upper = jnp.concatenate([matrix, zero], 1)
    lower = jnp.concatenate([zero, matrix], 1)
    return jnp.concatenate([upper, lower], 0)


def body(field, cotangent, spectral_weight, point_weight, point_bias):
    chan_start = lax.axis_index("chan") * OWN
    own = lax.dynamic_slice_in_dim(field, chan_start, OWN, 0)
    own = jnp.transpose(own.reshape(OWN, PLANES, 4, CELLS // 4), (2, 1, 0, 3))
    own = own.reshape(LANES, CELLS // 4)
    own_rows = lax.dynamic_slice_in_dim(point_weight, chan_start, OWN, 0)
    weight = jnp.transpose(spectral_weight, (0, 1, 3, 4, 2)).reshape(2, OWN, LOW * MX, C)
    tables = table(PACKED)
    wide = table(WIDE)
    first = own_modes(own, wide)
    field, cotangent, first = lax.optimization_barrier((field, cotangent, first))
    pencils = over(first.reshape(SLAB, PLANES, LANES), "slab").reshape(NX, LANES)

    cells = jnp.transpose(field, (2, 1, 0)).reshape(CELLS, LANES)
    cot = jnp.transpose(cotangent, (2, 1, 0)).reshape(CELLS, LANES)
    bias = jnp.tile(point_bias.astype(F32), 2)[None]
    base = mm(cells, paired(point_weight)) + bias
    coeff, parts = mix(pencils, weight, tables)
    parts = over(parts, "chan")
    planes = spread_planes(parts, tables)
    modes = over(planes.reshape(SLAB, 8, LANES), "slab").reshape(SLAB * 8, LANES)
    grad, rows = middle(modes, base, cot, own, wide, tables)
    arrived = over(rows.reshape(SLAB * CHUNK // 2, 2, LANES), "slab").reshape(SLAB * CHUNK, LANES)
    point_back = mm(paired(own_rows), grad.T)
    kz_weight = jnp.where(lax.axis_index("slab") < HIGH, 1.0, 2.0) / (NX * NY * NZ)
    scale = jnp.full((8, LANES), kz_weight, F32)
    hat, rows = adjoint_planes(arrived, weight, tables, scale)
    final = over(rows.reshape(SLAB, BACK, LANES), "slab").reshape(SLAB * BACK, LANES)
    outer_part = outer(coeff, hat).reshape(2, OWN, LOW, MX, C)
    grad_spectral = jnp.transpose(outer_part, (0, 1, 4, 2, 3))
    planes, grad_pointwise, grad_bias = own_grid(final, point_back, wide)
    grad_input = jnp.transpose(planes.reshape(PLANES, OWN, CELLS), (1, 0, 2))
    return grad_input, grad_spectral, grad_pointwise, grad_bias[0]


def solution(mesh):
    placed = (
        P(None, "slab", None),
        P(None, "slab", None),
        P(None, "chan", None, "slab", None),
        P(),
        P(),
    )
    return jax.shard_map(
        body,
        mesh=mesh,
        in_specs=placed,
        out_specs=(
            P("chan", "slab", None),
            P(None, "chan", None, "slab", None),
            P("chan", None),
            P(),
        ),
        check_vma=False,
    )
```

```python
import math

import jax
import jax.numpy as jnp
import numpy as np
from jax import lax
from jax.experimental import pallas as pl
from jax.experimental.pallas import tpu as pltpu
from jax.sharding import PartitionSpec as P

MX = 32
MY = 32
MZ = 16
NX = 256
NY = 64
NZ = 64
C = 64
OWN = 16
SLAB = 128
PLANES = 2
LOW = 4
HIGH = 8
CELLS = NY * NZ
LANES = 128
HALF = 64
CHUNK = 10
BACK = 4
SHARE = 7
PITCH = 66
OWN_ROOM = 56
INVERSE_ROOT = 1.0 / math.sqrt(NX * NY * NZ)
F32 = jnp.float32
BF16 = jnp.bfloat16


def kept(total, length):
    index = np.arange(total)
    return np.where(index < total // 2, index, index - total + length)


def waves(frequency, length):
    wound = (frequency[:, None] * np.arange(length)[None, :]) % length
    angle = np.float32(2.0 * math.pi / length) * wound.astype(np.float32)
    return np.cos(angle), np.sin(angle)


def table(values):
    return jnp.asarray(np.asarray(values, np.float32)).astype(BF16)


def axis_tables():
    cos_z, sin_z = waves(np.arange(MZ), NZ)
    cos_y, sin_y = waves(kept(MY, NY), NY)
    cos_x, sin_x = waves(kept(MX, NX), NX)
    return cos_z, sin_z, cos_y, sin_y, cos_x, sin_x


def rows_of_ky(real, imag):
    both = np.stack([real, imag], 1).reshape(HIGH, LOW, 2, -1)
    return np.transpose(both, (0, 2, 1, 3))


def pack_tables():
    cos_z, sin_z, cos_y, sin_y, cos_x, sin_x = axis_tables()
    weight = (np.where(np.arange(MZ) == 0, 1.0, 2.0) / (NX * NY * NZ))[:, None]
    plain_z = np.stack([cos_z, -sin_z], 1)
    wide = plain_z[:, :, None, None, :] * np.eye(8)[None, None, :, :, None]
    tall = (weight[:, :, None, None, None] * wide).reshape(256, 512).T
    wide = wide.reshape(256, 512)
    real = np.stack([cos_y, sin_y], 1).reshape(MY, 2 * NY)
    imag = np.stack([-sin_y, cos_y], 1).reshape(MY, 2 * NY)
    to_y = rows_of_ky(real, imag).reshape(2 * MY, 2 * NY).T
    from_y = rows_of_ky(real, imag).reshape(HIGH, 8, 2 * NY)
    from_y = np.concatenate([from_y, np.zeros((HIGH, CHUNK - 8, 2 * NY))], 1)
    from_y = from_y.reshape(HIGH * CHUNK, 2 * NY)
    pick = np.zeros((SLAB, 32))
    owner = np.arange(SLAB)
    pick[owner, np.minimum(owner // SHARE, OWN)] = 1.0
    split = np.concatenate([cos_x, sin_x], 0).reshape(2 * MX, SLAB, PLANES)
    gather = np.transpose(split, (2, 0, 1)).reshape(2 * PLANES * MX, SLAB)
    quarter = NY // 4
    cos_q = np.transpose(cos_y[:, :quarter].reshape(HIGH, LOW, quarter), (1, 0, 2))
    sin_q = np.transpose(sin_y[:, :quarter].reshape(HIGH, LOW, quarter), (1, 0, 2))
    real = np.stack([cos_q, sin_q], 2)
    imag = np.stack([-sin_q, cos_q], 2)
    own_from_y = np.stack([real, imag], 2).reshape(2 * MY, 2 * quarter)
    real = np.stack([cos_q, -sin_q], -1)
    imag = np.stack([sin_q, cos_q], -1)
    own_to_y = np.stack([real, imag], 1)
    own_to_y = np.pad(own_to_y, ((0, 0), (0, 0), (0, 0), (0, 0), (0, BACK - 2)))
    own_to_y = np.transpose(own_to_y, (0, 1, 3, 2, 4)).reshape(LOW * 2 * quarter, HIGH * BACK)
    parts = dict(
        to_y=to_y, from_y=from_y, pick=pick,
    )
    side = np.zeros((256, LANES))
    side[: 2 * MY, : 2 * quarter] = own_from_y
    side[2 * MY : 2 * MY + 8 * quarter, : HIGH * BACK] = own_to_y
    wide = np.concatenate([wide, side], 1)
    places = {}
    rows = []
    start = 0
    for name, part in parts.items():
        places[name] = (start, part.shape[0], part.shape[1])
        start += part.shape[0]
        rows.append(np.pad(part, ((0, 0), (0, LANES - part.shape[1]))))
    places["gather"] = (0, SLAB, SLAB)
    places["spread"] = (SLAB, SLAB, SLAB)
    pencil = np.concatenate([gather, gather.T], 0)
    return places, np.concatenate(rows, 0), pencil, wide, tall


PLACES, PACKED, PENCIL, WIDE, TALL = pack_tables()


def wide_part(wide):
    return wide[:, :512]


def own_from_y(wide):
    return wide[:64, 512:544]


def own_to_y(wide):
    return wide[64:192, 512:544]


def get(tables, name):
    start, rows, lanes = PLACES[name]
    return tables[start : start + rows, :lanes]


def mm(left, right):
    return jnp.dot(left, right, preferred_element_type=F32)


def swap(values):
    return pltpu.roll(values, HALF, 1)


def turn(values, shift):
    return pltpu.roll(values, shift, 1)


def quarter_turns(real, imag, forward):
    lane = lane_of(real.shape)
    even = (lane // 32) % 2 == 0
    sign = jnp.where(lane < HALF, 1.0, -1.0)
    sums, gaps = [], []
    for part in (real, imag):
        other = swap(part)
        sums.append(part + other)
        gaps.append(part - other)
    if forward:
        cross = (gaps[1], -gaps[0])
    else:
        cross = (-gaps[1], gaps[0])
    return [
        jnp.where(even, e + sign * turn(e, 96), sign * turn(d, 32) + c)
        for e, d, c in zip(sums, gaps, cross)
    ]


def by_group(blocks):
    group = lane_of(blocks[0].shape) // 32
    out = blocks[0]
    for index in range(1, 4):
        out = jnp.where(group == index, blocks[index], out)
    return out


def lane_of(shape):
    return lax.broadcasted_iota(jnp.int32, shape, 1)


def gelu_grad(pre_act):
    normal_cdf = 0.5 + 0.5 * lax.erf(pre_act * (1.0 / math.sqrt(2.0)))
    bell = jnp.exp2(pre_act * pre_act * (-0.5 * math.log2(math.e)))
    return normal_cdf + (pre_act * (1.0 / math.sqrt(2.0 * math.pi))) * bell


def two_words(values):
    head = values.astype(BF16).astype(F32)
    rest = values - head
    return jnp.where(lane_of(values.shape) < HALF, head, swap(rest))


def middle_kernel(
    modes, bases, cots, own, wide, tall, tables, grad_out, out,
    up, flat, down, rows, grad, packed, base, cot, sem
):
    pairs = ((bases, base), (cots, cot))
    loads = [
        pltpu.make_async_copy(source, target, sem.at[index + 3])
        for index, (source, target) in enumerate(pairs)
    ]
    for load in loads:
        load.start()

    @pl.loop(0, MZ, unroll=4)
    def _(kz):
        start = pl.multiple_of(kz * 64, 64)
        lines = mm(get(tables, "to_y"), modes[pl.ds(start, 64), :])
        up[pl.ds(2 * kz, 2), :, :] = lines.reshape(2, NY, LANES)

    loads[0].wait()
    for pair in range(4):
        sides = [
            up[:, (2 * pair + side) * 8 : (2 * pair + side) * 8 + 8, :].reshape(256, LANES)
            for side in range(2)
        ]
        grid = mm(tall[...], jnp.concatenate(sides, 1).astype(BF16))
        for side in range(2):
            cells = pl.ds((2 * pair + side) * 512, 512)
            flat[cells, :] = grid[:, side * LANES : (side + 1) * LANES] + base[cells, :]
    loads[1].wait()

    @pl.loop(0, CELLS // 64, unroll=4)
    def _(block):
        here = pl.ds(pl.multiple_of(block * 64, 64), 64)
        grad[here, :] = (cot[here, :].astype(F32) * gelu_grad(flat[here, :])).astype(BF16)

    save = pltpu.make_async_copy(grad, grad_out, sem.at[0])
    save.start()
    for pair in range(4):
        sides = [grad[(2 * pair + side) * 512 : (2 * pair + side) * 512 + 512, :] for side in range(2)]
        lines = mm(wide_part(wide), jnp.concatenate(sides, 1)).reshape(2 * MZ, 8, 2 * LANES)
        for side in range(2):
            group = (2 * pair + side) * 8
            down[:, group : group + 8, :] = lines[:, :, side * LANES : (side + 1) * LANES]

    sums = jnp.zeros((3 * OWN, LANES), F32)
    for quarter in range(4):
        cells = pl.ds(quarter * 1024, 1024)
        left = own[quarter * 32 : quarter * 32 + 32, :]
        left = jnp.concatenate([left, jnp.ones((OWN, CELLS // 4), BF16)], 0)
        sums += mm(left, grad[cells, :])
    lower = sums[:OWN] + swap(sums[OWN : 2 * OWN])
    bias = sums[2 * OWN : 2 * OWN + 8] + swap(sums[2 * OWN : 2 * OWN + 8])
    words = two_words(jnp.concatenate([lower, bias, jnp.zeros_like(bias)], 0)).astype(BF16)

    flat[:SLAB, :] = mm(get(tables, "pick"), words)
    sends = []
    half_rows = SLAB * CHUNK // 2
    for half in range(2):

        @pl.loop(half * MZ // 2, (half + 1) * MZ // 2, unroll=4)
        def _(kz):
            lines = down[pl.ds(2 * kz, 2), :, :].reshape(2 * NY, LANES).astype(BF16)
            start = pl.multiple_of(kz * HIGH * CHUNK, HIGH * CHUNK)
            rows[pl.ds(start, HIGH * CHUNK), :] = mm(get(tables, "from_y"), lines)

        here = pl.ds(half * half_rows, half_rows)
        rows[pl.ds(half * half_rows + 8, SLAB // 2, stride=CHUNK), :] = flat[
            half * SLAB // 2 : (half + 1) * SLAB // 2, :
        ]
        packed[here, :] = rows[here, :].astype(BF16)
        sends.append(pltpu.make_async_copy(packed.at[here, :], out.at[here, :], sem.at[half + 1]))
        sends[half].start()
    for send in sends + [save]:
        send.wait()


def places(count, anywhere):
    kinds = [pltpu.HBM if index in anywhere else pltpu.VMEM for index in range(count)]
    return [pl.BlockSpec(memory_space=kind) for kind in kinds]


def call(kernel, shapes, scratch, flops, room, *operands, anywhere=(), anywhere_out=()):
    moved = sum(s.size * s.dtype.itemsize for s in list(operands) + list(shapes))
    return pl.pallas_call(
        kernel,
        out_shape=shapes,
        in_specs=places(len(operands), anywhere),
        out_specs=places(len(shapes), anywhere_out),
        scratch_shapes=scratch,
        cost_estimate=pl.CostEstimate(flops=flops, bytes_accessed=moved, transcendentals=0),
        compiler_params=pltpu.CompilerParams(vmem_limit_bytes=room * 2**20),
    )(*operands)


def middle(modes, base, cot, own, wide, tables):
    shapes = (
        jax.ShapeDtypeStruct((CELLS, LANES), BF16),
        jax.ShapeDtypeStruct((SLAB * CHUNK, LANES), BF16),
    )
    scratch = [
        pltpu.VMEM((2 * MZ, NY, LANES), F32),
        pltpu.VMEM((CELLS, LANES), F32),
        pltpu.VMEM((2 * MZ, NY, LANES), F32),
        pltpu.VMEM((SLAB * CHUNK, LANES), F32),
        pltpu.VMEM((CELLS, LANES), BF16),
        pltpu.VMEM((SLAB * CHUNK, LANES), BF16),
        pltpu.VMEM((CELLS, LANES), F32),
        pltpu.VMEM((CELLS, LANES), BF16),
        pltpu.SemaphoreType.DMA((5,)),
    ]
    return call(
        middle_kernel, shapes, scratch, 400_000_000, 52,
        modes, base, cot, own, wide, table(TALL), tables,
        anywhere=(1, 2), anywhere_out=(0, 1),
    )


def own_kernel(field, wides, out, own, raw, spread, lines, wide, sem):
    start = pl.multiple_of(lax.axis_index("chan") * (OWN * HALF), OWN * HALF)
    fetch = pltpu.make_async_copy(field.at[pl.ds(start, OWN * HALF), :], raw, sem.at[0])
    fetch.start()
    load = pltpu.make_async_copy(wides, wide, sem.at[1])
    load.start()
    fetch.wait()
    for c in range(OWN):
        spread[c * PITCH : c * PITCH + HALF, :] = raw[c * HALF : (c + 1) * HALF, :].astype(F32)
    for tile in range(8):
        parts = [
            spread[pl.ds((quarter * 8 + tile) * 2 + plane, OWN, stride=PITCH), :]
            for quarter in range(4)
            for plane in range(PLANES)
        ]
        own[:, tile * LANES : (tile + 1) * LANES] = jnp.concatenate(parts, 0).astype(BF16)
    load.wait()
    for group in range(2):
        part = lax.dot_general(
            wide_part(wide),
            own[:, group * 512 : (group + 1) * 512],
            (((1,), (1,)), ((), ())),
            preferred_element_type=F32,
        ).reshape(MZ, 2, 8, LANES)
        real = part[:, 0].reshape(MZ * 8, LANES)
        imag = part[:, 1].reshape(MZ * 8, LANES)
        real, imag = quarter_turns(real, imag, True)
        lines[:, 0, group * 8 : group * 8 + 8, :] = real.reshape(MZ, 8, LANES)
        lines[:, 1, group * 8 : group * 8 + 8, :] = imag.reshape(MZ, 8, LANES)
    for pair in range(MZ // 2):
        left = lines[2 * pair].reshape(32, LANES)
        right = lines[2 * pair + 1].reshape(32, LANES)
        both = jnp.concatenate([left, right], 1).astype(BF16)
        both = mm(own_from_y(wide), both)
        for half in range(2):
            part = both[:, half * LANES : (half + 1) * LANES]
            part = by_group([part[low * 16 : low * 16 + 16] for low in range(LOW)])
            start = (2 * pair + half) * 16
            out[start : start + 16, :] = part.astype(BF16)


def own_modes(field, wide):
    shapes = (
        jax.ShapeDtypeStruct((2 * SLAB, LANES), BF16),
        jax.ShapeDtypeStruct((LANES, CELLS // 4), BF16),
    )
    scratch = [
        pltpu.VMEM((OWN * HALF, LANES), BF16),
        pltpu.VMEM((OWN * PITCH, LANES), F32),
        pltpu.VMEM((MZ, 2, NY // 4, LANES), F32),
        pltpu.VMEM((256, 640), BF16),
        pltpu.SemaphoreType.DMA((2,)),
    ]
    return call(own_kernel, shapes, scratch, 4_000_000, OWN_ROOM, field, wide, anywhere=(0, 1))


def grid_kernel(modes, point, wide_z, out, sums, bias, lines, wide, spread):
    wide[...] = modes[...].astype(F32)
    for kz in range(MZ):
        both = mm(own_to_y(wide_z), modes[kz * 32 : kz * 32 + 32, :])
        both = by_group([both[low * 32 : low * 32 + 32] for low in range(LOW)])
        real, imag = quarter_turns(both[:16], both[16:], False)
        lines[kz, 0] = real
        lines[kz, 1] = imag
    for group in range(2):
        both = lines[:, :, group * 8 : group * 8 + 8, :].reshape(256, LANES)
        both = mm(both.T.astype(BF16), wide_part(wide_z))
        for quarter in range(4):
            cells = pl.ds(quarter * 1024 + group * 512, 512)
            here = both[quarter * 32 : quarter * 32 + 32] + point[:, cells]
            for plane in range(PLANES):
                for tile in range(4):
                    first = (quarter * 8 + group * 4 + tile) * 2 + plane
                    spread[pl.ds(first, OWN, stride=PITCH), :] = here[
                        plane * OWN : (plane + 1) * OWN, tile * LANES : (tile + 1) * LANES
                    ]
    for i in range(OWN):
        out[i * HALF : (i + 1) * HALF, :] = spread[i * PITCH : i * PITCH + HALF, :].astype(BF16)
    words = wide[pl.ds(2, OWN, stride=BACK * SHARE), :]
    sums[...] = (words + swap(words))[:, :HALF]
    words = wide[pl.ds(BACK * SHARE * OWN + 2, 8, stride=1), :]
    bias[...] = (words + swap(words))[:1, :HALF]


def own_grid(modes, point, wide):
    shapes = (
        jax.ShapeDtypeStruct((OWN * HALF, LANES), BF16),
        jax.ShapeDtypeStruct((OWN, C), F32),
        jax.ShapeDtypeStruct((1, C), F32),
    )
    scratch = [
        pltpu.VMEM((MZ, 2, NY // 4, LANES), F32),
        pltpu.VMEM((SLAB * BACK, LANES), F32),
        pltpu.VMEM((OWN * PITCH, LANES), F32),
    ]
    return call(grid_kernel, shapes, scratch, 8_000_000, 8, modes, point, wide)


def along_x(tables, left, right):
    both = mm(get(tables, "gather"), jnp.concatenate([left, right], 1).astype(BF16))
    return both[: 2 * MX], both[2 * MX :]


def mix_kernel(pencils, weight, tables, coeff, out, wide):
    wide[...] = pencils[...].astype(F32)
    left = wide[pl.ds(0, SLAB, stride=2), :]
    right = wide[pl.ds(1, SLAB, stride=2), :]
    near, far = along_x(tables, left, right)
    near = near + jnp.concatenate([turn(far[:, :LANES], 112), turn(far[:, LANES:], 112)], 1)
    modes_real = (near[:MX, :LANES] + near[MX:, LANES:]).astype(BF16).astype(F32)
    modes_imag = (near[:MX, LANES:] - near[MX:, :LANES]).astype(BF16).astype(F32)
    coeff[0] = modes_real
    coeff[1] = modes_imag
    for m in range(LOW):
        rows = pl.ds(m * MX, MX)
        real = jnp.zeros((MX, C), F32)
        imag = jnp.zeros((MX, C), F32)
        for i in range(OWN):
            at = m * 32 + i
            left = jnp.broadcast_to(modes_real[:, at : at + 1], (MX, C))
            right = jnp.broadcast_to(modes_imag[:, at : at + 1], (MX, C))
            weight_real = weight[0, i, rows, :].astype(F32)
            weight_imag = weight[1, i, rows, :].astype(F32)
            real += left * weight_real - right * weight_imag
            imag += left * weight_imag + right * weight_real
        part = jnp.concatenate([real, imag], 1).astype(BF16)
        for peer in range(4):
            out[peer, rows, :] = part


def mix(pencils, weight, tables):
    shapes = (
        jax.ShapeDtypeStruct((2, MX, LANES), F32),
        jax.ShapeDtypeStruct((4, LOW * MX, LANES), BF16),
    )
    scratch = [pltpu.VMEM((2 * SLAB, LANES), F32)]
    return call(mix_kernel, shapes, scratch, 4_000_000, 8, pencils, weight, tables)


def spread_kernel(parts, tables, out, rows):
    total = parts[0].astype(F32)
    for peer in range(1, 4):
        total += parts[peer].astype(F32)
    lane = lane_of((MX, LANES))
    for m in range(LOW):
        here = total[m * MX : (m + 1) * MX]
        there = swap(here)
        zero = jnp.zeros_like(here)
        a = jnp.where(lane < HALF, here, zero)
        b = jnp.where(lane < HALF, there, zero)
        c = jnp.where(lane < HALF, zero, there)
        d = jnp.where(lane < HALF, zero, here)
        top = jnp.concatenate([a, b], 1)
        second = jnp.concatenate([-b, a], 1)
        third = jnp.concatenate([c, d], 1)
        last = jnp.concatenate([-d, c], 1)
        block = jnp.concatenate([top, second, third, last], 0).astype(BF16)
        planes = mm(get(tables, "spread"), block)
        rows[pl.ds(m, SLAB, stride=8), :] = planes[:, :LANES]
        rows[pl.ds(LOW + m, SLAB, stride=8), :] = planes[:, LANES:]
    out[...] = rows[...].astype(BF16)


def spread_planes(parts, tables):
    shapes = (jax.ShapeDtypeStruct((SLAB * 8, LANES), BF16),)
    scratch = [pltpu.VMEM((SLAB * 8, LANES), F32)]
    return call(spread_kernel, shapes, scratch, 40_000_000, 8, parts, tables)[0]


def adjoint_kernel(pencils, weights, tables, scale, hat, out, wide, rows, weight, sem):
    load = pltpu.make_async_copy(weights, weight, sem)
    load.start()
    wide[...] = pencils[...].astype(F32)
    lane = lane_of((MX, LANES))
    near_real = jnp.zeros((MX, LANES), F32)
    near_imag = jnp.zeros((MX, LANES), F32)
    factor = scale[0:1, :]
    for m in range(LOW):
        left = wide[pl.ds(m, SLAB, stride=CHUNK), :]
        right = wide[pl.ds(LOW + m, SLAB, stride=CHUNK), :]
        near, far = along_x(tables, left, right)
        first = near[:, :LANES] + swap(far[:, :LANES])
        second = near[:, LANES:] + swap(far[:, LANES:])
        real = (first[:MX] + second[MX:]) * factor
        imag = (second[:MX] - first[MX:]) * factor
        hat[0, pl.ds(m * MX, MX), :] = real.astype(BF16).astype(F32)[:, :C]
        hat[1, pl.ds(m * MX, MX), :] = imag.astype(BF16).astype(F32)[:, :C]
    load.wait()
    for m in range(LOW):
        at_m = pl.ds(m * MX, MX)
        real = hat[0, at_m, :]
        imag = hat[1, at_m, :]
        for i in range(OWN):
            weight_real = weight[0, i, at_m, :].astype(F32)
            weight_imag = weight[1, i, at_m, :].astype(F32)
            sum_real = jnp.sum(real * weight_real + imag * weight_imag, 1, keepdims=True)
            sum_imag = jnp.sum(imag * weight_real - real * weight_imag, 1, keepdims=True)
            near_real = jnp.where(lane == m * 32 + i, sum_real, near_real)
            near_imag = jnp.where(lane == m * 32 + i, sum_imag, near_imag)
    far_real = turn(near_real, 16)
    far_imag = turn(near_imag, 16)
    top = jnp.concatenate([near_real, near_imag], 1)
    second = jnp.concatenate([-near_imag, near_real], 1)
    third = jnp.concatenate([far_real, far_imag], 1)
    last = jnp.concatenate([-far_imag, far_real], 1)
    block = jnp.concatenate([top, second, third, last], 0).astype(BF16)
    planes = mm(get(tables, "spread"), block)
    rows[pl.ds(0, SLAB, stride=BACK), :] = planes[:, :LANES]
    rows[pl.ds(1, SLAB, stride=BACK), :] = planes[:, LANES:]
    rider = wide[pl.ds(8, SLAB, stride=CHUNK), :]
    total = jnp.sum(rider, 0, keepdims=True)
    total = jnp.broadcast_to(total, (8, LANES))
    total = two_words((total + swap(total)) * INVERSE_ROOT)
    rows[pl.ds(2, SLAB, stride=BACK), :] = jnp.broadcast_to(total[:1], (SLAB, LANES))
    rows[pl.ds(3, SLAB, stride=BACK), :] = jnp.zeros((SLAB, LANES), F32)
    out[...] = rows[...].astype(BF16)


def adjoint_planes(pencils, weight, tables, scale):
    shapes = (
        jax.ShapeDtypeStruct((2, LOW * MX, C), F32),
        jax.ShapeDtypeStruct((SLAB * BACK, LANES), BF16),
    )
    scratch = [
        pltpu.VMEM((SLAB * CHUNK, LANES), F32),
        pltpu.VMEM((SLAB * BACK, LANES), F32),
        pltpu.VMEM((2, OWN, LOW * MX, C), BF16),
        pltpu.SemaphoreType.DMA,
    ]
    return call(
        adjoint_kernel, shapes, scratch, 40_000_000, 50, pencils, weight, tables, scale, anywhere=(1,)
    )


def outer_kernel(coeff, hat, out):
    modes_real = coeff[0]
    modes_imag = coeff[1]
    for m in range(LOW):
        rows = pl.ds(m * MX, MX)
        real = hat[0, rows, :]
        imag = hat[1, rows, :]
        for i in range(OWN):
            at = m * 32 + i
            left = jnp.broadcast_to(modes_real[:, at : at + 1], (MX, C))
            right = jnp.broadcast_to(modes_imag[:, at : at + 1], (MX, C))
            out[0, i, rows, :] = left * real + right * imag
            out[1, i, rows, :] = left * imag - right * real


def outer(coeff, hat):
    shapes = (jax.ShapeDtypeStruct((2, OWN, LOW * MX, C), F32),)
    return call(outer_kernel, shapes, [], 8_000_000, 8, coeff, hat)[0]


def over(values, axis):
    return lax.all_to_all(values, axis, split_axis=0, concat_axis=0, tiled=True)


def paired(matrix):
    zero = jnp.zeros_like(matrix)
    upper = jnp.concatenate([matrix, zero], 1)
    lower = jnp.concatenate([zero, matrix], 1)
    return jnp.concatenate([upper, lower], 0)


def body(field, cotangent, spectral_weight, point_weight, point_bias):
    chan_start = lax.axis_index("chan") * OWN
    own_rows = lax.dynamic_slice_in_dim(point_weight, chan_start, OWN, 0)
    weight = jnp.transpose(spectral_weight, (0, 1, 3, 4, 2)).reshape(2, OWN, LOW * MX, C)
    tables = table(PENCIL)
    wide = table(WIDE)
    rows = jnp.transpose(field.reshape(C, PLANES, 32, LANES), (0, 2, 1, 3)).reshape(CELLS, LANES)
    first, own = own_modes(rows, wide)
    field, cotangent, first = lax.optimization_barrier((field, cotangent, first))
    pencils = over(first.reshape(SLAB, PLANES, LANES), "slab").reshape(NX, LANES)

    cells = jnp.transpose(field, (2, 1, 0)).reshape(CELLS, LANES)
    cot = jnp.transpose(cotangent, (2, 1, 0)).reshape(CELLS, LANES)
    bias = jnp.tile(point_bias.astype(F32), 2)[None]
    base = mm(cells, paired(point_weight)) + bias
    pencils, base, cot = lax.optimization_barrier((pencils, base, cot))
    coeff, parts = mix(pencils, weight, tables)
    parts = over(parts, "chan")
    planes = spread_planes(parts, tables)
    modes = over(planes.reshape(SLAB, 8, LANES), "slab").reshape(SLAB * 8, LANES)
    grad, rows = middle(modes, base, cot, own, wide, table(PACKED))
    arrived = over(rows.reshape(SLAB * CHUNK // 2, 2, LANES), "slab").reshape(SLAB * CHUNK, LANES)
    point_back = mm(paired(own_rows), grad.T)
    kz_weight = jnp.where(lax.axis_index("slab") < HIGH, 1.0, 2.0) / (NX * NY * NZ)
    scale = jnp.full((8, LANES), kz_weight, F32)
    hat, rows = adjoint_planes(arrived, weight, tables, scale)
    final = over(rows.reshape(SLAB, BACK, LANES), "slab").reshape(SLAB * BACK, LANES)
    outer_part = outer(coeff, hat).reshape(2, OWN, LOW, MX, C)
    grad_spectral = jnp.transpose(outer_part, (0, 1, 4, 2, 3))
    planes, grad_pointwise, grad_bias = own_grid(final, point_back, wide)
    grad_input = jnp.transpose(planes.reshape(OWN, 32, PLANES, LANES), (0, 2, 1, 3))
    grad_input = grad_input.reshape(OWN, PLANES, CELLS)
    return grad_input, grad_spectral, grad_pointwise, grad_bias[0]


def solution(mesh):
    placed = (
        P(None, "slab", None),
        P(None, "slab", None),
        P(None, "chan", None, "slab", None),
        P(),
        P(),
    )
    return jax.shard_map(
        body,
        mesh=mesh,
        in_specs=placed,
        out_specs=(
            P("chan", "slab", None),
            P(None, "chan", None, "slab", None),
            P("chan", None),
            P(),
        ),
        check_vma=False,
    )
```

```python
import math

import jax
import jax.numpy as jnp
import numpy as np
from jax import lax
from jax.experimental import pallas as pl
from jax.experimental.pallas import tpu as pltpu
from jax.sharding import PartitionSpec as P

MX = 32
MY = 32
MZ = 16
NX = 256
NY = 64
NZ = 64
C = 64
OWN = 16
SLAB = 128
PLANES = 2
LOW = 4
HIGH = 8
CELLS = NY * NZ
LANES = 128
HALF = 64
CHUNK = 10
BACK = 4
SHARE = 7
PITCH = 66
OWN_ROOM = 56
INVERSE_ROOT = 1.0 / math.sqrt(NX * NY * NZ)
F32 = jnp.float32
BF16 = jnp.bfloat16


def kept(total, length):
    index = np.arange(total)
    return np.where(index < total // 2, index, index - total + length)


def waves(frequency, length):
    wound = (frequency[:, None] * np.arange(length)[None, :]) % length
    angle = np.float32(2.0 * math.pi / length) * wound.astype(np.float32)
    return np.cos(angle), np.sin(angle)


def table(values):
    return jnp.asarray(np.asarray(values, np.float32)).astype(BF16)


def axis_tables():
    cos_z, sin_z = waves(np.arange(MZ), NZ)
    cos_y, sin_y = waves(kept(MY, NY), NY)
    cos_x, sin_x = waves(kept(MX, NX), NX)
    return cos_z, sin_z, cos_y, sin_y, cos_x, sin_x


def rows_of_ky(real, imag):
    both = np.stack([real, imag], 1).reshape(HIGH, LOW, 2, -1)
    return np.transpose(both, (0, 2, 1, 3))


def pack_tables():
    cos_z, sin_z, cos_y, sin_y, cos_x, sin_x = axis_tables()
    weight = (np.where(np.arange(MZ) == 0, 1.0, 2.0) / (NX * NY * NZ))[:, None]
    plain_z = np.stack([cos_z, -sin_z], 1)
    wide = plain_z[:, :, None, None, :] * np.eye(8)[None, None, :, :, None]
    tall = (weight[:, :, None, None, None] * wide).reshape(256, 512).T
    wide = wide.reshape(256, 512)
    real = np.stack([cos_y, sin_y], 1).reshape(MY, 2 * NY)
    imag = np.stack([-sin_y, cos_y], 1).reshape(MY, 2 * NY)
    to_y = rows_of_ky(real, imag).reshape(2 * MY, 2 * NY).T
    from_y = rows_of_ky(real, imag).reshape(HIGH, 8, 2 * NY)
    from_y = np.concatenate([from_y, np.zeros((HIGH, CHUNK - 8, 2 * NY))], 1)
    from_y = from_y.reshape(HIGH * CHUNK, 2 * NY)
    pick = np.zeros((SLAB, 32))
    owner = np.arange(SLAB)
    pick[owner, np.minimum(owner // SHARE, OWN)] = 1.0
    split = np.concatenate([cos_x, sin_x], 0).reshape(2 * MX, SLAB, PLANES)
    gather = np.transpose(split, (2, 0, 1)).reshape(2 * PLANES * MX, SLAB)
    quarter = NY // 4
    cos_q = np.transpose(cos_y[:, :quarter].reshape(HIGH, LOW, quarter), (1, 0, 2))
    sin_q = np.transpose(sin_y[:, :quarter].reshape(HIGH, LOW, quarter), (1, 0, 2))
    real = np.stack([cos_q, sin_q], 2)
    imag = np.stack([-sin_q, cos_q], 2)
    own_from_y = np.stack([real, imag], 2).reshape(2 * MY, 2 * quarter)
    real = np.stack([cos_q, -sin_q], -1)
    imag = np.stack([sin_q, cos_q], -1)
    own_to_y = np.stack([real, imag], 1)
    own_to_y = np.pad(own_to_y, ((0, 0), (0, 0), (0, 0), (0, 0), (0, BACK - 2)))
    own_to_y = np.transpose(own_to_y, (0, 1, 3, 2, 4)).reshape(LOW * 2 * quarter, HIGH * BACK)
    parts = dict(
        to_y=to_y, from_y=from_y, pick=pick,
    )
    side = np.zeros((256, LANES))
    side[: 2 * MY, : 2 * quarter] = own_from_y
    side[2 * MY : 2 * MY + 8 * quarter, : HIGH * BACK] = own_to_y
    wide = np.concatenate([wide, side], 1)
    places = {}
    rows = []
    start = 0
    for name, part in parts.items():
        places[name] = (start, part.shape[0], part.shape[1])
        start += part.shape[0]
        rows.append(np.pad(part, ((0, 0), (0, LANES - part.shape[1]))))
    places["gather"] = (0, SLAB, SLAB)
    places["spread"] = (SLAB, SLAB, SLAB)
    pencil = np.concatenate([gather, gather.T], 0)
    return places, np.concatenate(rows, 0), pencil, wide, tall


PLACES, PACKED, PENCIL, WIDE, TALL = pack_tables()


def wide_part(wide):
    return wide[:, :512]


def own_from_y(wide):
    return wide[:64, 512:544]


def own_to_y(wide):
    return wide[64:192, 512:544]


def get(tables, name):
    start, rows, lanes = PLACES[name]
    return tables[start : start + rows, :lanes]


def mm(left, right):
    return jnp.dot(left, right, preferred_element_type=F32)


def swap(values):
    return pltpu.roll(values, HALF, 1)


def turn(values, shift):
    return pltpu.roll(values, shift, 1)


def quarter_turns(real, imag, forward):
    lane = lane_of(real.shape)
    even = (lane // 32) % 2 == 0
    sign = jnp.where(lane < HALF, 1.0, -1.0)
    sums, gaps = [], []
    for part in (real, imag):
        other = swap(part)
        sums.append(part + other)
        gaps.append(part - other)
    if forward:
        cross = (gaps[1], -gaps[0])
    else:
        cross = (-gaps[1], gaps[0])
    return [
        jnp.where(even, e + sign * turn(e, 96), sign * turn(d, 32) + c)
        for e, d, c in zip(sums, gaps, cross)
    ]


def by_group(blocks):
    group = lane_of(blocks[0].shape) // 32
    out = blocks[0]
    for index in range(1, 4):
        out = jnp.where(group == index, blocks[index], out)
    return out


def lane_of(shape):
    return lax.broadcasted_iota(jnp.int32, shape, 1)


def twice_gelu_grad(pre_act):
    bell = jnp.exp2(pre_act * pre_act * (-0.5 * math.log2(math.e)))
    bell = (pre_act * math.sqrt(2.0 / math.pi)) * bell
    return (1.0 + lax.erf(pre_act * (1.0 / math.sqrt(2.0)))) + bell


def two_words(values):
    head = values.astype(BF16).astype(F32)
    rest = values - head
    return jnp.where(lane_of(values.shape) < HALF, head, swap(rest))


def middle_kernel(
    modes, bases, cots, own, wide, tall, tables, grad_out, out,
    up, flat, down, rows, grad, base, cot, sem
):
    pairs = ((bases, base), (cots, cot))
    loads = [
        pltpu.make_async_copy(source, target, sem.at[index + 1])
        for index, (source, target) in enumerate(pairs)
    ]
    for load in loads:
        load.start()

    @pl.loop(0, MZ, unroll=4)
    def _(kz):
        start = pl.multiple_of(kz * 64, 64)
        lines = mm(get(tables, "to_y"), modes[pl.ds(start, 64), :])
        up[pl.ds(2 * kz, 2), :, :] = lines.reshape(2, NY, LANES)

    loads[0].wait()
    for pair in range(4):
        sides = [
            up[:, (2 * pair + side) * 8 : (2 * pair + side) * 8 + 8, :].reshape(256, LANES)
            for side in range(2)
        ]
        grid = mm(tall[...], jnp.concatenate(sides, 1).astype(BF16))
        for side in range(2):
            cells = pl.ds((2 * pair + side) * 512, 512)
            flat[cells, :] = grid[:, side * LANES : (side + 1) * LANES] + base[cells, :]
    loads[1].wait()

    @pl.loop(0, CELLS // 64, unroll=4)
    def _(block):
        here = pl.ds(pl.multiple_of(block * 64, 64), 64)
        grad[here, :] = (cot[here, :].astype(F32) * twice_gelu_grad(flat[here, :])).astype(BF16)

    save = pltpu.make_async_copy(grad, grad_out, sem.at[0])
    save.start()
    for pair in range(4):
        sides = [grad[(2 * pair + side) * 512 : (2 * pair + side) * 512 + 512, :] for side in range(2)]
        lines = mm(wide_part(wide), jnp.concatenate(sides, 1)).reshape(2 * MZ, 8, 2 * LANES)
        for side in range(2):
            group = (2 * pair + side) * 8
            down[:, group : group + 8, :] = lines[:, :, side * LANES : (side + 1) * LANES]

    sums = jnp.zeros((3 * OWN, LANES), F32)
    for quarter in range(4):
        cells = pl.ds(quarter * 1024, 1024)
        left = own[quarter * 32 : quarter * 32 + 32, :]
        left = jnp.concatenate([left, jnp.ones((OWN, CELLS // 4), BF16)], 0)
        sums += mm(left, grad[cells, :])
    lower = sums[:OWN] + swap(sums[OWN : 2 * OWN])
    bias = sums[2 * OWN : 2 * OWN + 8] + swap(sums[2 * OWN : 2 * OWN + 8])
    words = two_words(jnp.concatenate([lower, bias, jnp.zeros_like(bias)], 0)).astype(BF16)

    flat[:SLAB, :] = mm(get(tables, "pick"), words)
    half_rows = SLAB * CHUNK // 2
    for half in range(2):

        @pl.loop(half * MZ // 2, (half + 1) * MZ // 2, unroll=4)
        def _(kz):
            lines = down[pl.ds(2 * kz, 2), :, :].reshape(2 * NY, LANES).astype(BF16)
            start = pl.multiple_of(kz * HIGH * CHUNK, HIGH * CHUNK)
            rows[pl.ds(start, HIGH * CHUNK), :] = mm(get(tables, "from_y"), lines)

        here = pl.ds(half * half_rows, half_rows)
        rows[pl.ds(half * half_rows + 8, SLAB // 2, stride=CHUNK), :] = flat[
            half * SLAB // 2 : (half + 1) * SLAB // 2, :
        ]
        out[here, :] = rows[here, :].astype(BF16)
    save.wait()


def places(count, anywhere):
    kinds = [pltpu.HBM if index in anywhere else pltpu.VMEM for index in range(count)]
    return [pl.BlockSpec(memory_space=kind) for kind in kinds]


def call(kernel, shapes, scratch, flops, room, *operands, anywhere=(), anywhere_out=()):
    moved = sum(s.size * s.dtype.itemsize for s in list(operands) + list(shapes))
    return pl.pallas_call(
        kernel,
        out_shape=shapes,
        in_specs=places(len(operands), anywhere),
        out_specs=places(len(shapes), anywhere_out),
        scratch_shapes=scratch,
        cost_estimate=pl.CostEstimate(flops=flops, bytes_accessed=moved, transcendentals=0),
        compiler_params=pltpu.CompilerParams(vmem_limit_bytes=room * 2**20),
    )(*operands)


def middle(modes, base, cot, own, wide, tables):
    shapes = (
        jax.ShapeDtypeStruct((CELLS, LANES), BF16),
        jax.ShapeDtypeStruct((SLAB * CHUNK, LANES), BF16),
    )
    scratch = [
        pltpu.VMEM((2 * MZ, NY, LANES), F32),
        pltpu.VMEM((CELLS, LANES), F32),
        pltpu.VMEM((2 * MZ, NY, LANES), F32),
        pltpu.VMEM((SLAB * CHUNK, LANES), F32),
        pltpu.VMEM((CELLS, LANES), BF16),
        pltpu.VMEM((CELLS, LANES), F32),
        pltpu.VMEM((CELLS, LANES), BF16),
        pltpu.SemaphoreType.DMA((3,)),
    ]
    return call(
        middle_kernel, shapes, scratch, 400_000_000, 52,
        modes, base, cot, own, wide, table(TALL), tables,
        anywhere=(1, 2), anywhere_out=(0,),
    )


def own_kernel(field, wides, out, own, raw, spread, lines, wide, sem):
    start = pl.multiple_of(lax.axis_index("chan") * (OWN * HALF), OWN * HALF)
    fetch = pltpu.make_async_copy(field.at[pl.ds(start, OWN * HALF), :], raw, sem.at[0])
    fetch.start()
    load = pltpu.make_async_copy(wides, wide, sem.at[1])
    load.start()
    fetch.wait()
    for c in range(OWN):
        spread[c * PITCH : c * PITCH + HALF, :] = raw[c * HALF : (c + 1) * HALF, :].astype(F32)
    for tile in range(8):
        parts = [
            spread[pl.ds((quarter * 8 + tile) * 2 + plane, OWN, stride=PITCH), :]
            for quarter in range(4)
            for plane in range(PLANES)
        ]
        own[:, tile * LANES : (tile + 1) * LANES] = jnp.concatenate(parts, 0).astype(BF16)
    load.wait()
    for group in range(2):
        part = lax.dot_general(
            wide_part(wide),
            own[:, group * 512 : (group + 1) * 512],
            (((1,), (1,)), ((), ())),
            preferred_element_type=F32,
        ).reshape(MZ, 2, 8, LANES)
        real = part[:, 0].reshape(MZ * 8, LANES)
        imag = part[:, 1].reshape(MZ * 8, LANES)
        real, imag = quarter_turns(real, imag, True)
        lines[:, 0, group * 8 : group * 8 + 8, :] = real.reshape(MZ, 8, LANES)
        lines[:, 1, group * 8 : group * 8 + 8, :] = imag.reshape(MZ, 8, LANES)
    for pair in range(MZ // 2):
        left = lines[2 * pair].reshape(32, LANES)
        right = lines[2 * pair + 1].reshape(32, LANES)
        both = jnp.concatenate([left, right], 1).astype(BF16)
        both = mm(own_from_y(wide), both)
        for half in range(2):
            part = both[:, half * LANES : (half + 1) * LANES]
            part = by_group([part[low * 16 : low * 16 + 16] for low in range(LOW)])
            start = (2 * pair + half) * 16
            out[start : start + 16, :] = part.astype(BF16)


def own_modes(field, wide):
    shapes = (
        jax.ShapeDtypeStruct((2 * SLAB, LANES), BF16),
        jax.ShapeDtypeStruct((LANES, CELLS // 4), BF16),
    )
    scratch = [
        pltpu.VMEM((OWN * HALF, LANES), BF16),
        pltpu.VMEM((OWN * PITCH, LANES), F32),
        pltpu.VMEM((MZ, 2, NY // 4, LANES), F32),
        pltpu.VMEM((256, 640), BF16),
        pltpu.SemaphoreType.DMA((2,)),
    ]
    return call(own_kernel, shapes, scratch, 4_000_000, OWN_ROOM, field, wide, anywhere=(0, 1))


def grid_kernel(modes, point, wide_z, out, sums, bias, lines, wide, spread):
    wide[...] = modes[...].astype(F32)
    for kz in range(MZ):
        both = mm(own_to_y(wide_z), modes[kz * 32 : kz * 32 + 32, :])
        both = by_group([both[low * 32 : low * 32 + 32] for low in range(LOW)])
        real, imag = quarter_turns(both[:16], both[16:], False)
        lines[kz, 0] = real
        lines[kz, 1] = imag
    for group in range(2):
        both = lines[:, :, group * 8 : group * 8 + 8, :].reshape(256, LANES)
        both = mm(both.T.astype(BF16), wide_part(wide_z))
        for quarter in range(4):
            cells = pl.ds(quarter * 1024 + group * 512, 512)
            here = both[quarter * 32 : quarter * 32 + 32] + point[:, cells]
            for plane in range(PLANES):
                for tile in range(4):
                    first = (quarter * 8 + group * 4 + tile) * 2 + plane
                    spread[pl.ds(first, OWN, stride=PITCH), :] = here[
                        plane * OWN : (plane + 1) * OWN, tile * LANES : (tile + 1) * LANES
                    ]
    for i in range(OWN):
        out[i * HALF : (i + 1) * HALF, :] = spread[i * PITCH : i * PITCH + HALF, :].astype(BF16)
    words = wide[pl.ds(2, OWN, stride=BACK * SHARE), :]
    sums[...] = (words + swap(words))[:, :HALF]
    words = wide[pl.ds(BACK * SHARE * OWN + 2, 8, stride=1), :]
    bias[...] = (words + swap(words))[:1, :HALF]


def own_grid(modes, point, wide):
    shapes = (
        jax.ShapeDtypeStruct((OWN * HALF, LANES), BF16),
        jax.ShapeDtypeStruct((OWN, C), F32),
        jax.ShapeDtypeStruct((1, C), F32),
    )
    scratch = [
        pltpu.VMEM((MZ, 2, NY // 4, LANES), F32),
        pltpu.VMEM((SLAB * BACK, LANES), F32),
        pltpu.VMEM((OWN * PITCH, LANES), F32),
    ]
    return call(grid_kernel, shapes, scratch, 8_000_000, 8, modes, point, wide)


def along_x(tables, left, right):
    both = mm(get(tables, "gather"), jnp.concatenate([left, right], 1).astype(BF16))
    return both[: 2 * MX], both[2 * MX :]


def mix_kernel(pencils, weight, tables, coeff, out, wide):
    wide[...] = pencils[...].astype(F32)
    left = wide[pl.ds(0, SLAB, stride=2), :]
    right = wide[pl.ds(1, SLAB, stride=2), :]
    near, far = along_x(tables, left, right)
    near = near + jnp.concatenate([turn(far[:, :LANES], 112), turn(far[:, LANES:], 112)], 1)
    modes_real = (near[:MX, :LANES] + near[MX:, LANES:]).astype(BF16).astype(F32)
    modes_imag = (near[:MX, LANES:] - near[MX:, :LANES]).astype(BF16).astype(F32)
    lane = lane_of((MX, LANES))
    coeff[0] = modes_real
    coeff[1] = modes_imag
    for m in range(LOW):
        rows = pl.ds(m * MX, MX)
        straight = jnp.zeros((MX, LANES), F32)
        crossed = jnp.zeros((MX, LANES), F32)
        for i in range(OWN):
            at = m * 32 + i
            here = weight[i, rows, :].astype(F32)
            straight += jnp.broadcast_to(modes_real[:, at : at + 1], (MX, LANES)) * here
            crossed += jnp.broadcast_to(modes_imag[:, at : at + 1], (MX, LANES)) * here
        crossed = swap(crossed)
        part = straight + jnp.where(lane < HALF, -crossed, crossed)
        part = part.astype(BF16)
        for peer in range(4):
            out[peer, rows, :] = part


def mix(pencils, weight, tables):
    shapes = (
        jax.ShapeDtypeStruct((2, MX, LANES), F32),
        jax.ShapeDtypeStruct((4, LOW * MX, LANES), BF16),
    )
    scratch = [pltpu.VMEM((2 * SLAB, LANES), F32)]
    return call(mix_kernel, shapes, scratch, 4_000_000, 8, pencils, weight, tables)


def spread_kernel(parts, tables, out, rows):
    total = parts[0].astype(F32)
    for peer in range(1, 4):
        total += parts[peer].astype(F32)
    lane = lane_of((MX, LANES))
    for m in range(LOW):
        here = total[m * MX : (m + 1) * MX]
        there = swap(here)
        zero = jnp.zeros_like(here)
        a = jnp.where(lane < HALF, here, zero)
        b = jnp.where(lane < HALF, there, zero)
        c = jnp.where(lane < HALF, zero, there)
        d = jnp.where(lane < HALF, zero, here)
        top = jnp.concatenate([a, b], 1)
        second = jnp.concatenate([-b, a], 1)
        third = jnp.concatenate([c, d], 1)
        last = jnp.concatenate([-d, c], 1)
        block = jnp.concatenate([top, second, third, last], 0).astype(BF16)
        planes = mm(get(tables, "spread"), block)
        rows[pl.ds(m, SLAB, stride=8), :] = planes[:, :LANES]
        rows[pl.ds(LOW + m, SLAB, stride=8), :] = planes[:, LANES:]
    out[...] = rows[...].astype(BF16)


def spread_planes(parts, tables):
    shapes = (jax.ShapeDtypeStruct((SLAB * 8, LANES), BF16),)
    scratch = [pltpu.VMEM((SLAB * 8, LANES), F32)]
    return call(spread_kernel, shapes, scratch, 40_000_000, 8, parts, tables)[0]


def adjoint_kernel(pencils, weights, tables, scale, hat, out, wide, rows, weight, sem):
    load = pltpu.make_async_copy(weights, weight, sem)
    load.start()
    wide[...] = pencils[...].astype(F32)
    lane = lane_of((MX, LANES))
    near_real = jnp.zeros((MX, LANES), F32)
    near_imag = jnp.zeros((MX, LANES), F32)
    factor = scale[0:1, :]
    both_hats = []
    for m in range(LOW):
        left = wide[pl.ds(m, SLAB, stride=CHUNK), :]
        right = wide[pl.ds(LOW + m, SLAB, stride=CHUNK), :]
        near, far = along_x(tables, left, right)
        first = near[:, :LANES] + swap(far[:, :LANES])
        second = near[:, LANES:] + swap(far[:, LANES:])
        real = (first[:MX] + second[MX:]) * factor
        imag = (second[:MX] - first[MX:]) * factor
        real = real.astype(BF16).astype(F32)
        imag = imag.astype(BF16).astype(F32)
        hat[0, pl.ds(m * MX, MX), :] = real[:, :C]
        hat[1, pl.ds(m * MX, MX), :] = imag[:, :C]
        both_hats.append(
            (
                jnp.where(lane < HALF, real, swap(imag)),
                jnp.where(lane < HALF, imag, -swap(real)),
            )
        )
    load.wait()
    for m in range(LOW):
        straight, crossed = both_hats[m]
        for i in range(OWN):
            here = weight[i, pl.ds(m * MX, MX), :].astype(F32)
            sum_real = jnp.sum(straight * here, 1, keepdims=True)
            sum_imag = jnp.sum(crossed * here, 1, keepdims=True)
            near_real = jnp.where(lane == m * 32 + i, sum_real, near_real)
            near_imag = jnp.where(lane == m * 32 + i, sum_imag, near_imag)
    far_real = turn(near_real, 16)
    far_imag = turn(near_imag, 16)
    top = jnp.concatenate([near_real, near_imag], 1)
    second = jnp.concatenate([-near_imag, near_real], 1)
    third = jnp.concatenate([far_real, far_imag], 1)
    last = jnp.concatenate([-far_imag, far_real], 1)
    block = jnp.concatenate([top, second, third, last], 0).astype(BF16)
    planes = mm(get(tables, "spread"), block)
    rows[pl.ds(0, SLAB, stride=BACK), :] = planes[:, :LANES]
    rows[pl.ds(1, SLAB, stride=BACK), :] = planes[:, LANES:]
    rider = wide[pl.ds(8, SLAB, stride=CHUNK), :]
    total = jnp.sum(rider, 0, keepdims=True)
    total = jnp.broadcast_to(total, (8, LANES))
    total = two_words((total + swap(total)) * INVERSE_ROOT)
    rows[pl.ds(2, SLAB, stride=BACK), :] = jnp.broadcast_to(total[:1], (SLAB, LANES))
    rows[pl.ds(3, SLAB, stride=BACK), :] = jnp.zeros((SLAB, LANES), F32)
    out[...] = rows[...].astype(BF16)


def adjoint_planes(pencils, weight, tables, scale):
    shapes = (
        jax.ShapeDtypeStruct((2, LOW * MX, C), F32),
        jax.ShapeDtypeStruct((SLAB * BACK, LANES), BF16),
    )
    scratch = [
        pltpu.VMEM((SLAB * CHUNK, LANES), F32),
        pltpu.VMEM((SLAB * BACK, LANES), F32),
        pltpu.VMEM((OWN, LOW * MX, LANES), BF16),
        pltpu.SemaphoreType.DMA,
    ]
    return call(
        adjoint_kernel, shapes, scratch, 40_000_000, 50, pencils, weight, tables, scale, anywhere=(1,)
    )


def outer_kernel(coeff, hat, out):
    modes_real = coeff[0]
    modes_imag = coeff[1]
    for m in range(LOW):
        rows = pl.ds(m * MX, MX)
        real = hat[0, rows, :]
        imag = hat[1, rows, :]
        for i in range(OWN):
            at = m * 32 + i
            left = jnp.broadcast_to(modes_real[:, at : at + 1], (MX, C))
            right = jnp.broadcast_to(modes_imag[:, at : at + 1], (MX, C))
            out[0, i, rows, :] = left * real + right * imag
            out[1, i, rows, :] = left * imag - right * real


def outer(coeff, hat):
    shapes = (jax.ShapeDtypeStruct((2, OWN, LOW * MX, C), F32),)
    return call(outer_kernel, shapes, [], 8_000_000, 8, coeff, hat)[0]


def over(values, axis):
    return lax.all_to_all(values, axis, split_axis=0, concat_axis=0, tiled=True)


def paired(matrix):
    zero = jnp.zeros_like(matrix)
    upper = jnp.concatenate([matrix, zero], 1)
    lower = jnp.concatenate([zero, matrix], 1)
    return jnp.concatenate([upper, lower], 0)


def body(field, cotangent, spectral_weight, point_weight, point_bias):
    chan_start = lax.axis_index("chan") * OWN
    own_rows = lax.dynamic_slice_in_dim(point_weight, chan_start, OWN, 0)
    weight = jnp.transpose(spectral_weight, (0, 1, 3, 4, 2)).reshape(2, OWN, LOW * MX, C)
    own_rows_of = paired(own_rows)
    tables = table(PENCIL)
    wide = table(WIDE)
    rows = jnp.transpose(field.reshape(C, PLANES, 32, LANES), (0, 2, 1, 3)).reshape(CELLS, LANES)
    first, own = own_modes(rows, wide)
    field, cotangent, weight, first = lax.optimization_barrier(
        (field, cotangent, weight, first)
    )
    pencils = over(first.reshape(SLAB, PLANES, LANES), "slab").reshape(NX, LANES)

    cells = jnp.transpose(field, (2, 1, 0)).reshape(CELLS, LANES)
    cot = jnp.transpose(cotangent, (2, 1, 0)).reshape(CELLS, LANES)
    cot = mm(cot, 0.5 * jnp.eye(LANES, dtype=BF16)).astype(BF16)
    weight = jnp.concatenate([weight[0], weight[1]], -1)
    bias = jnp.tile(point_bias.astype(F32), 2)[None]
    base = mm(cells, paired(point_weight)) + bias
    kz_weight = jnp.where(lax.axis_index("slab") < HIGH, 1.0, 2.0) / (NX * NY * NZ)
    scale = jnp.full((8, LANES), kz_weight, F32)
    pencils, base, cot, weight, own_rows_of, scale = lax.optimization_barrier(
        (pencils, base, cot, weight, own_rows_of, scale)
    )
    coeff, parts = mix(pencils, weight, tables)
    parts = over(parts, "chan")
    planes = spread_planes(parts, tables)
    modes = over(planes.reshape(SLAB, 8, LANES), "slab").reshape(SLAB * 8, LANES)
    grad, rows = middle(modes, base, cot, own, wide, table(PACKED))
    arrived = over(rows.reshape(SLAB * CHUNK // 2, 2, LANES), "slab").reshape(SLAB * CHUNK, LANES)
    point_back = mm(own_rows_of, grad.T)
    hat, rows = adjoint_planes(arrived, weight, tables, scale)
    final = over(rows.reshape(SLAB, BACK, LANES), "slab").reshape(SLAB * BACK, LANES)
    outer_part = outer(coeff, hat).reshape(2, OWN, LOW, MX, C)
    grad_spectral = jnp.transpose(outer_part, (0, 1, 4, 2, 3))
    planes, grad_pointwise, grad_bias = own_grid(final, point_back, wide)
    grad_input = jnp.transpose(planes.reshape(OWN, 32, PLANES, LANES), (0, 2, 1, 3))
    grad_input = grad_input.reshape(OWN, PLANES, CELLS)
    return grad_input, grad_spectral, grad_pointwise, grad_bias[0]


def solution(mesh):
    placed = (
        P(None, "slab", None),
        P(None, "slab", None),
        P(None, "chan", None, "slab", None),
        P(),
        P(),
    )
    return jax.shard_map(
        body,
        mesh=mesh,
        in_specs=placed,
        out_specs=(
            P("chan", "slab", None),
            P(None, "chan", None, "slab", None),
            P("chan", None),
            P(),
        ),
        check_vma=False,
    )
```

```python
import math

import jax
import jax.numpy as jnp
import numpy as np
from jax import lax
from jax.experimental import pallas as pl
from jax.experimental.pallas import tpu as pltpu
from jax.sharding import PartitionSpec as P

MX = 32
MY = 32
MZ = 16
NX = 256
NY = 64
NZ = 64
C = 64
OWN = 16
SLAB = 128
PLANES = 2
LOW = 4
HIGH = 8
CELLS = NY * NZ
LANES = 128
HALF = 64
CHUNK = 10
BACK = 4
SHARE = 7
PITCH = 66
OWN_ROOM = 56
INVERSE_ROOT = 1.0 / math.sqrt(NX * NY * NZ)
F32 = jnp.float32
BF16 = jnp.bfloat16


def kept(total, length):
    index = np.arange(total)
    return np.where(index < total // 2, index, index - total + length)


def waves(frequency, length):
    wound = (frequency[:, None] * np.arange(length)[None, :]) % length
    angle = np.float32(2.0 * math.pi / length) * wound.astype(np.float32)
    return np.cos(angle), np.sin(angle)


def table(values):
    return jnp.asarray(np.asarray(values, np.float32)).astype(BF16)


def axis_tables():
    cos_z, sin_z = waves(np.arange(MZ), NZ)
    cos_y, sin_y = waves(kept(MY, NY), NY)
    cos_x, sin_x = waves(kept(MX, NX), NX)
    return cos_z, sin_z, cos_y, sin_y, cos_x, sin_x


def rows_of_ky(real, imag):
    both = np.stack([real, imag], 1).reshape(HIGH, LOW, 2, -1)
    return np.transpose(both, (0, 2, 1, 3))


def pack_tables():
    cos_z, sin_z, cos_y, sin_y, cos_x, sin_x = axis_tables()
    weight = (np.where(np.arange(MZ) == 0, 1.0, 2.0) / (NX * NY * NZ))[:, None]
    plain_z = np.stack([cos_z, -sin_z], 1)
    wide = plain_z[:, :, None, None, :] * np.eye(8)[None, None, :, :, None]
    tall = (weight[:, :, None, None, None] * wide).reshape(256, 512).T
    wide = wide.reshape(256, 512)
    real = np.stack([cos_y, sin_y], 1).reshape(MY, 2 * NY)
    imag = np.stack([-sin_y, cos_y], 1).reshape(MY, 2 * NY)
    to_y = rows_of_ky(real, imag).reshape(2 * MY, 2 * NY).T
    from_y = rows_of_ky(real, imag).reshape(HIGH, 8, 2 * NY)
    from_y = np.concatenate([from_y, np.zeros((HIGH, CHUNK - 8, 2 * NY))], 1)
    from_y = from_y.reshape(HIGH * CHUNK, 2 * NY)
    pick = np.zeros((SLAB, 32))
    owner = np.arange(SLAB)
    pick[owner, np.minimum(owner // SHARE, OWN)] = 1.0
    split = np.concatenate([cos_x, sin_x], 0).reshape(2 * MX, SLAB, PLANES)
    gather = np.transpose(split, (2, 0, 1)).reshape(2 * PLANES * MX, SLAB)
    quarter = NY // 4
    cos_q = np.transpose(cos_y[:, :quarter].reshape(HIGH, LOW, quarter), (1, 0, 2))
    sin_q = np.transpose(sin_y[:, :quarter].reshape(HIGH, LOW, quarter), (1, 0, 2))
    real = np.stack([cos_q, sin_q], 2)
    imag = np.stack([-sin_q, cos_q], 2)
    own_from_y = np.stack([real, imag], 2).reshape(2 * MY, 2 * quarter)
    real = np.stack([cos_q, -sin_q], -1)
    imag = np.stack([sin_q, cos_q], -1)
    own_to_y = np.stack([real, imag], 1)
    own_to_y = np.pad(own_to_y, ((0, 0), (0, 0), (0, 0), (0, 0), (0, BACK - 2)))
    own_to_y = np.transpose(own_to_y, (0, 1, 3, 2, 4)).reshape(LOW * 2 * quarter, HIGH * BACK)
    parts = dict(
        to_y=to_y, from_y=from_y, pick=pick,
    )
    side = np.zeros((256, LANES))
    side[: 2 * MY, : 2 * quarter] = own_from_y
    side[2 * MY : 2 * MY + 8 * quarter, : HIGH * BACK] = own_to_y
    wide = np.concatenate([wide, side], 1)
    places = {}
    rows = []
    start = 0
    for name, part in parts.items():
        places[name] = (start, part.shape[0], part.shape[1])
        start += part.shape[0]
        rows.append(np.pad(part, ((0, 0), (0, LANES - part.shape[1]))))
    places["gather"] = (0, SLAB, SLAB)
    places["spread"] = (SLAB, SLAB, SLAB)
    pencil = np.concatenate([gather, gather.T], 0)
    return places, np.concatenate(rows, 0), pencil, wide, tall


PLACES, PACKED, PENCIL, WIDE, TALL = pack_tables()


def wide_part(wide):
    return wide[:, :512]


def own_from_y(wide):
    return wide[:64, 512:544]


def own_to_y(wide):
    return wide[64:192, 512:544]


def get(tables, name):
    start, rows, lanes = PLACES[name]
    return tables[start : start + rows, :lanes]


def mm(left, right):
    return jnp.dot(left, right, preferred_element_type=F32)


def swap(values):
    return pltpu.roll(values, HALF, 1)


def turn(values, shift):
    return pltpu.roll(values, shift, 1)


def quarter_turns(real, imag, forward):
    lane = lane_of(real.shape)
    even = (lane // 32) % 2 == 0
    sign = jnp.where(lane < HALF, 1.0, -1.0)
    sums, gaps = [], []
    for part in (real, imag):
        other = swap(part)
        sums.append(part + other)
        gaps.append(part - other)
    if forward:
        cross = (gaps[1], -gaps[0])
    else:
        cross = (-gaps[1], gaps[0])
    return [
        jnp.where(even, e + sign * turn(e, 96), sign * turn(d, 32) + c)
        for e, d, c in zip(sums, gaps, cross)
    ]


def by_group(blocks):
    group = lane_of(blocks[0].shape) // 32
    out = blocks[0]
    for index in range(1, 4):
        out = jnp.where(group == index, blocks[index], out)
    return out


def lane_of(shape):
    return lax.broadcasted_iota(jnp.int32, shape, 1)


def twice_gelu_grad(pre_act):
    bell = jnp.exp2(pre_act * pre_act * (-0.5 * math.log2(math.e)))
    bell = (pre_act * math.sqrt(2.0 / math.pi)) * bell
    return (1.0 + lax.erf(pre_act * (1.0 / math.sqrt(2.0)))) + bell


def two_words(values):
    head = values.astype(BF16).astype(F32)
    rest = values - head
    return jnp.where(lane_of(values.shape) < HALF, head, swap(rest))


def middle_kernel(
    modes, bases, cots, own, wide, tall, tables, grad_out, out,
    up, flat, down, rows, grad, base, cot, sem
):
    pairs = ((bases, base), (cots, cot))
    loads = [
        pltpu.make_async_copy(source, target, sem.at[index + 1])
        for index, (source, target) in enumerate(pairs)
    ]
    for load in loads:
        load.start()

    @pl.loop(0, MZ, unroll=4)
    def _(kz):
        start = pl.multiple_of(kz * 64, 64)
        lines = mm(get(tables, "to_y"), modes[pl.ds(start, 64), :])
        up[pl.ds(2 * kz, 2), :, :] = lines.reshape(2, NY, LANES)

    loads[0].wait()
    for pair in range(4):
        sides = [
            up[:, (2 * pair + side) * 8 : (2 * pair + side) * 8 + 8, :].reshape(256, LANES)
            for side in range(2)
        ]
        grid = mm(tall[...], jnp.concatenate(sides, 1).astype(BF16))
        for side in range(2):
            cells = pl.ds((2 * pair + side) * 512, 512)
            flat[cells, :] = grid[:, side * LANES : (side + 1) * LANES] + base[cells, :]
    loads[1].wait()

    @pl.loop(0, CELLS // 64, unroll=4)
    def _(block):
        here = pl.ds(pl.multiple_of(block * 64, 64), 64)
        grad[here, :] = (cot[here, :].astype(F32) * twice_gelu_grad(flat[here, :])).astype(BF16)

    save = pltpu.make_async_copy(grad, grad_out, sem.at[0])
    save.start()
    for pair in range(4):
        sides = [grad[(2 * pair + side) * 512 : (2 * pair + side) * 512 + 512, :] for side in range(2)]
        lines = mm(wide_part(wide), jnp.concatenate(sides, 1)).reshape(2 * MZ, 8, 2 * LANES)
        for side in range(2):
            group = (2 * pair + side) * 8
            down[:, group : group + 8, :] = lines[:, :, side * LANES : (side + 1) * LANES]

    sums = jnp.zeros((3 * OWN, LANES), F32)
    for quarter in range(4):
        cells = pl.ds(quarter * 1024, 1024)
        left = own[quarter * 32 : quarter * 32 + 32, :]
        left = jnp.concatenate([left, jnp.ones((OWN, CELLS // 4), BF16)], 0)
        sums += mm(left, grad[cells, :])
    lower = sums[:OWN] + swap(sums[OWN : 2 * OWN])
    bias = sums[2 * OWN : 2 * OWN + 8] + swap(sums[2 * OWN : 2 * OWN + 8])
    words = two_words(jnp.concatenate([lower, bias, jnp.zeros_like(bias)], 0)).astype(BF16)

    flat[:SLAB, :] = mm(get(tables, "pick"), words)
    half_rows = SLAB * CHUNK // 2
    for half in range(2):

        @pl.loop(half * MZ // 2, (half + 1) * MZ // 2, unroll=4)
        def _(kz):
            lines = down[pl.ds(2 * kz, 2), :, :].reshape(2 * NY, LANES).astype(BF16)
            start = pl.multiple_of(kz * HIGH * CHUNK, HIGH * CHUNK)
            rows[pl.ds(start, HIGH * CHUNK), :] = mm(get(tables, "from_y"), lines)

        here = pl.ds(half * half_rows, half_rows)
        rows[pl.ds(half * half_rows + 8, SLAB // 2, stride=CHUNK), :] = flat[
            half * SLAB // 2 : (half + 1) * SLAB // 2, :
        ]
        out[here, :] = rows[here, :].astype(BF16)
    save.wait()


def places(count, anywhere):
    kinds = [pltpu.HBM if index in anywhere else pltpu.VMEM for index in range(count)]
    return [pl.BlockSpec(memory_space=kind) for kind in kinds]


def call(kernel, shapes, scratch, flops, room, *operands, anywhere=(), anywhere_out=()):
    moved = sum(s.size * s.dtype.itemsize for s in list(operands) + list(shapes))
    return pl.pallas_call(
        kernel,
        out_shape=shapes,
        in_specs=places(len(operands), anywhere),
        out_specs=places(len(shapes), anywhere_out),
        scratch_shapes=scratch,
        cost_estimate=pl.CostEstimate(flops=flops, bytes_accessed=moved, transcendentals=0),
        compiler_params=pltpu.CompilerParams(vmem_limit_bytes=room * 2**20),
    )(*operands)


def middle(modes, base, cot, own, wide, tables):
    shapes = (
        jax.ShapeDtypeStruct((CELLS, LANES), BF16),
        jax.ShapeDtypeStruct((SLAB * CHUNK, LANES), BF16),
    )
    scratch = [
        pltpu.VMEM((2 * MZ, NY, LANES), F32),
        pltpu.VMEM((CELLS, LANES), F32),
        pltpu.VMEM((2 * MZ, NY, LANES), F32),
        pltpu.VMEM((SLAB * CHUNK, LANES), F32),
        pltpu.VMEM((CELLS, LANES), BF16),
        pltpu.VMEM((CELLS, LANES), F32),
        pltpu.VMEM((CELLS, LANES), BF16),
        pltpu.SemaphoreType.DMA((3,)),
    ]
    return call(
        middle_kernel, shapes, scratch, 400_000_000, 52,
        modes, base, cot, own, wide, table(TALL), tables,
        anywhere=(1, 2), anywhere_out=(0,),
    )


def own_kernel(field, wides, out, own, raw, spread, lines, wide, sem):
    start = pl.multiple_of(lax.axis_index("chan") * (OWN * HALF), OWN * HALF)
    fetch = pltpu.make_async_copy(field.at[pl.ds(start, OWN * HALF), :], raw, sem.at[0])
    fetch.start()
    load = pltpu.make_async_copy(wides, wide, sem.at[1])
    load.start()
    fetch.wait()
    for c in range(OWN):
        spread[c * PITCH : c * PITCH + HALF, :] = raw[c * HALF : (c + 1) * HALF, :].astype(F32)
    for tile in range(8):
        parts = [
            spread[pl.ds((quarter * 8 + tile) * 2 + plane, OWN, stride=PITCH), :]
            for quarter in range(4)
            for plane in range(PLANES)
        ]
        own[:, tile * LANES : (tile + 1) * LANES] = jnp.concatenate(parts, 0).astype(BF16)
    load.wait()
    for group in range(2):
        part = lax.dot_general(
            wide_part(wide),
            own[:, group * 512 : (group + 1) * 512],
            (((1,), (1,)), ((), ())),
            preferred_element_type=F32,
        ).reshape(MZ, 2, 8, LANES)
        real = part[:, 0].reshape(MZ * 8, LANES)
        imag = part[:, 1].reshape(MZ * 8, LANES)
        real, imag = quarter_turns(real, imag, True)
        lines[:, 0, group * 8 : group * 8 + 8, :] = real.reshape(MZ, 8, LANES)
        lines[:, 1, group * 8 : group * 8 + 8, :] = imag.reshape(MZ, 8, LANES)
    for pair in range(MZ // 2):
        left = lines[2 * pair].reshape(32, LANES)
        right = lines[2 * pair + 1].reshape(32, LANES)
        both = jnp.concatenate([left, right], 1).astype(BF16)
        both = mm(own_from_y(wide), both)
        for half in range(2):
            part = both[:, half * LANES : (half + 1) * LANES]
            part = by_group([part[low * 16 : low * 16 + 16] for low in range(LOW)])
            start = (2 * pair + half) * 16
            out[start : start + 16, :] = part.astype(BF16)


def own_modes(field, wide):
    shapes = (
        jax.ShapeDtypeStruct((2 * SLAB, LANES), BF16),
        jax.ShapeDtypeStruct((LANES, CELLS // 4), BF16),
    )
    scratch = [
        pltpu.VMEM((OWN * HALF, LANES), BF16),
        pltpu.VMEM((OWN * PITCH, LANES), F32),
        pltpu.VMEM((MZ, 2, NY // 4, LANES), F32),
        pltpu.VMEM((256, 640), BF16),
        pltpu.SemaphoreType.DMA((2,)),
    ]
    return call(own_kernel, shapes, scratch, 4_000_000, OWN_ROOM, field, wide, anywhere=(0, 1))


def grid_kernel(modes, point, wide_z, out, sums, bias, lines, wide, spread):
    wide[...] = modes[...].astype(F32)
    for kz in range(MZ):
        both = mm(own_to_y(wide_z), modes[kz * 32 : kz * 32 + 32, :])
        both = by_group([both[low * 32 : low * 32 + 32] for low in range(LOW)])
        real, imag = quarter_turns(both[:16], both[16:], False)
        lines[kz, 0] = real
        lines[kz, 1] = imag
    for group in range(2):
        both = lines[:, :, group * 8 : group * 8 + 8, :].reshape(256, LANES)
        both = mm(both.T.astype(BF16), wide_part(wide_z))
        for quarter in range(4):
            cells = pl.ds(quarter * 1024 + group * 512, 512)
            here = both[quarter * 32 : quarter * 32 + 32] + point[:, cells]
            for plane in range(PLANES):
                for tile in range(4):
                    first = (quarter * 8 + group * 4 + tile) * 2 + plane
                    spread[pl.ds(first, OWN, stride=PITCH), :] = here[
                        plane * OWN : (plane + 1) * OWN, tile * LANES : (tile + 1) * LANES
                    ]
    for i in range(OWN):
        out[i * HALF : (i + 1) * HALF, :] = spread[i * PITCH : i * PITCH + HALF, :].astype(BF16)
    words = wide[pl.ds(2, OWN, stride=BACK * SHARE), :]
    sums[...] = (words + swap(words))[:, :HALF]
    words = wide[pl.ds(BACK * SHARE * OWN + 2, 8, stride=1), :]
    bias[...] = (words + swap(words))[:1, :HALF]


def own_grid(modes, point, wide):
    shapes = (
        jax.ShapeDtypeStruct((OWN * HALF, LANES), BF16),
        jax.ShapeDtypeStruct((OWN, C), F32),
        jax.ShapeDtypeStruct((1, C), F32),
    )
    scratch = [
        pltpu.VMEM((MZ, 2, NY // 4, LANES), F32),
        pltpu.VMEM((SLAB * BACK, LANES), F32),
        pltpu.VMEM((OWN * PITCH, LANES), F32),
    ]
    return call(grid_kernel, shapes, scratch, 8_000_000, 8, modes, point, wide)


def along_x(tables, left, right):
    both = mm(get(tables, "gather"), jnp.concatenate([left, right], 1).astype(BF16))
    return both[: 2 * MX], both[2 * MX :]


def mix_kernel(pencils, weight, tables, coeff, out, wide):
    wide[...] = pencils[...].astype(F32)
    left = wide[pl.ds(0, SLAB, stride=2), :]
    right = wide[pl.ds(1, SLAB, stride=2), :]
    near, far = along_x(tables, left, right)
    near = near + jnp.concatenate([turn(far[:, :LANES], 112), turn(far[:, LANES:], 112)], 1)
    modes_real = (near[:MX, :LANES] + near[MX:, LANES:]).astype(BF16).astype(F32)
    modes_imag = (near[:MX, LANES:] - near[MX:, :LANES]).astype(BF16).astype(F32)
    coeff[0] = modes_real
    coeff[1] = modes_imag
    for m in range(LOW):
        rows = pl.ds(m * MX, MX)
        real = jnp.zeros((MX, C), F32)
        imag = jnp.zeros((MX, C), F32)
        for i in range(OWN):
            at = m * 32 + i
            left = jnp.broadcast_to(modes_real[:, at : at + 1], (MX, C))
            right = jnp.broadcast_to(modes_imag[:, at : at + 1], (MX, C))
            weight_real = weight[0, i, rows, :].astype(F32)
            weight_imag = weight[1, i, rows, :].astype(F32)
            real += left * weight_real - right * weight_imag
            imag += left * weight_imag + right * weight_real
        part = jnp.concatenate([real, imag], 1).astype(BF16)
        for peer in range(4):
            out[peer, rows, :] = part


def mix(pencils, weight, tables):
    shapes = (
        jax.ShapeDtypeStruct((2, MX, LANES), F32),
        jax.ShapeDtypeStruct((4, LOW * MX, LANES), BF16),
    )
    scratch = [pltpu.VMEM((2 * SLAB, LANES), F32)]
    return call(mix_kernel, shapes, scratch, 4_000_000, 8, pencils, weight, tables)


def spread_kernel(parts, tables, out, rows):
    total = parts[0].astype(F32)
    for peer in range(1, 4):
        total += parts[peer].astype(F32)
    lane = lane_of((MX, LANES))
    for m in range(LOW):
        here = total[m * MX : (m + 1) * MX]
        there = swap(here)
        zero = jnp.zeros_like(here)
        a = jnp.where(lane < HALF, here, zero)
        b = jnp.where(lane < HALF, there, zero)
        c = jnp.where(lane < HALF, zero, there)
        d = jnp.where(lane < HALF, zero, here)
        top = jnp.concatenate([a, b], 1)
        second = jnp.concatenate([-b, a], 1)
        third = jnp.concatenate([c, d], 1)
        last = jnp.concatenate([-d, c], 1)
        block = jnp.concatenate([top, second, third, last], 0).astype(BF16)
        planes = mm(get(tables, "spread"), block)
        rows[pl.ds(m, SLAB, stride=8), :] = planes[:, :LANES]
        rows[pl.ds(LOW + m, SLAB, stride=8), :] = planes[:, LANES:]
    out[...] = rows[...].astype(BF16)


def spread_planes(parts, tables):
    shapes = (jax.ShapeDtypeStruct((SLAB * 8, LANES), BF16),)
    scratch = [pltpu.VMEM((SLAB * 8, LANES), F32)]
    return call(spread_kernel, shapes, scratch, 40_000_000, 8, parts, tables)[0]


def adjoint_kernel(pencils, weights, tables, scale, hat, out, wide, rows, weight, sem):
    load = pltpu.make_async_copy(weights, weight, sem)
    load.start()
    wide[...] = pencils[...].astype(F32)
    lane = lane_of((MX, LANES))
    near_real = jnp.zeros((MX, LANES), F32)
    near_imag = jnp.zeros((MX, LANES), F32)
    factor = scale[0:1, :]
    for m in range(LOW):
        left = wide[pl.ds(m, SLAB, stride=CHUNK), :]
        right = wide[pl.ds(LOW + m, SLAB, stride=CHUNK), :]
        near, far = along_x(tables, left, right)
        first = near[:, :LANES] + swap(far[:, :LANES])
        second = near[:, LANES:] + swap(far[:, LANES:])
        real = (first[:MX] + second[MX:]) * factor
        imag = (second[:MX] - first[MX:]) * factor
        hat[0, pl.ds(m * MX, MX), :] = real.astype(BF16).astype(F32)[:, :C]
        hat[1, pl.ds(m * MX, MX), :] = imag.astype(BF16).astype(F32)[:, :C]
    load.wait()
    for m in range(LOW):
        at_m = pl.ds(m * MX, MX)
        real = hat[0, at_m, :]
        imag = hat[1, at_m, :]
        for i in range(OWN):
            weight_real = weight[0, i, at_m, :].astype(F32)
            weight_imag = weight[1, i, at_m, :].astype(F32)
            sum_real = jnp.sum(real * weight_real + imag * weight_imag, 1, keepdims=True)
            sum_imag = jnp.sum(imag * weight_real - real * weight_imag, 1, keepdims=True)
            near_real = jnp.where(lane == m * 32 + i, sum_real, near_real)
            near_imag = jnp.where(lane == m * 32 + i, sum_imag, near_imag)
    far_real = turn(near_real, 16)
    far_imag = turn(near_imag, 16)
    top = jnp.concatenate([near_real, near_imag], 1)
    second = jnp.concatenate([-near_imag, near_real], 1)
    third = jnp.concatenate([far_real, far_imag], 1)
    last = jnp.concatenate([-far_imag, far_real], 1)
    block = jnp.concatenate([top, second, third, last], 0).astype(BF16)
    planes = mm(get(tables, "spread"), block)
    rows[pl.ds(0, SLAB, stride=BACK), :] = planes[:, :LANES]
    rows[pl.ds(1, SLAB, stride=BACK), :] = planes[:, LANES:]
    rider = wide[pl.ds(8, SLAB, stride=CHUNK), :]
    total = jnp.sum(rider, 0, keepdims=True)
    total = jnp.broadcast_to(total, (8, LANES))
    total = two_words((total + swap(total)) * INVERSE_ROOT)
    rows[pl.ds(2, SLAB, stride=BACK), :] = jnp.broadcast_to(total[:1], (SLAB, LANES))
    rows[pl.ds(3, SLAB, stride=BACK), :] = jnp.zeros((SLAB, LANES), F32)
    out[...] = rows[...].astype(BF16)


def adjoint_planes(pencils, weight, tables, scale):
    shapes = (
        jax.ShapeDtypeStruct((2, LOW * MX, C), F32),
        jax.ShapeDtypeStruct((SLAB * BACK, LANES), BF16),
    )
    scratch = [
        pltpu.VMEM((SLAB * CHUNK, LANES), F32),
        pltpu.VMEM((SLAB * BACK, LANES), F32),
        pltpu.VMEM((2, OWN, LOW * MX, C), BF16),
        pltpu.SemaphoreType.DMA,
    ]
    return call(
        adjoint_kernel, shapes, scratch, 40_000_000, 50, pencils, weight, tables, scale, anywhere=(1,)
    )


def outer_kernel(coeff, hat, out):
    modes_real = coeff[0]
    modes_imag = coeff[1]
    for m in range(LOW):
        rows = pl.ds(m * MX, MX)
        real = hat[0, rows, :]
        imag = hat[1, rows, :]
        for i in range(OWN):
            at = m * 32 + i
            left = jnp.broadcast_to(modes_real[:, at : at + 1], (MX, C))
            right = jnp.broadcast_to(modes_imag[:, at : at + 1], (MX, C))
            out[0, i, rows, :] = left * real + right * imag
            out[1, i, rows, :] = left * imag - right * real


def outer(coeff, hat):
    shapes = (jax.ShapeDtypeStruct((2, OWN, LOW * MX, C), F32),)
    return call(outer_kernel, shapes, [], 8_000_000, 8, coeff, hat)[0]


def over(values, axis):
    return lax.all_to_all(values, axis, split_axis=0, concat_axis=0, tiled=True)


def paired(matrix):
    zero = jnp.zeros_like(matrix)
    upper = jnp.concatenate([matrix, zero], 1)
    lower = jnp.concatenate([zero, matrix], 1)
    return jnp.concatenate([upper, lower], 0)


def body(field, cotangent, spectral_weight, point_weight, point_bias):
    chan_start = lax.axis_index("chan") * OWN
    own_rows = paired(lax.dynamic_slice_in_dim(point_weight, chan_start, OWN, 0))
    weight = jnp.transpose(spectral_weight, (0, 1, 3, 4, 2)).reshape(2, OWN, LOW * MX, C)
    tables = table(PENCIL)
    wide = table(WIDE)
    rows = jnp.transpose(field.reshape(C, PLANES, 32, LANES), (0, 2, 1, 3)).reshape(CELLS, LANES)
    first, own = own_modes(rows, wide)
    pencils = over(first.reshape(SLAB, PLANES, LANES), "slab").reshape(NX, LANES)
    coeff, parts = mix(pencils, weight, tables)

    field, cotangent, own_rows, parts = lax.optimization_barrier(
        (field, cotangent, own_rows, parts)
    )
    kz_weight = jnp.where(lax.axis_index("slab") < HIGH, 1.0, 2.0) / (NX * NY * NZ)
    scale = jnp.full((8, LANES), kz_weight, F32)
    cells = jnp.transpose(field, (2, 1, 0)).reshape(CELLS, LANES)
    cot = jnp.transpose(cotangent, (2, 1, 0)).reshape(CELLS, LANES)
    cot = mm(cot, 0.5 * jnp.eye(LANES, dtype=BF16)).astype(BF16)
    bias = jnp.tile(point_bias.astype(F32), 2)[None]
    base = mm(cells, paired(point_weight)) + bias
    parts = over(parts, "chan")
    parts, base, cot, own_rows, scale = lax.optimization_barrier(
        (parts, base, cot, own_rows, scale)
    )

    planes = spread_planes(parts, tables)
    modes = over(planes.reshape(SLAB, 8, LANES), "slab").reshape(SLAB * 8, LANES)
    grad, rows = middle(modes, base, cot, own, wide, table(PACKED))
    arrived = over(rows.reshape(SLAB * CHUNK // 2, 2, LANES), "slab")
    hat, rows = adjoint_planes(arrived.reshape(SLAB * CHUNK, LANES), weight, tables, scale)
    final = over(rows.reshape(SLAB, BACK, LANES), "slab").reshape(SLAB * BACK, LANES)
    point_back = mm(own_rows, grad.T)
    outer_part = outer(coeff, hat).reshape(2, OWN, LOW, MX, C)
    grad_spectral = jnp.transpose(outer_part, (0, 1, 4, 2, 3))
    planes, grad_pointwise, grad_bias = own_grid(final, point_back, wide)
    grad_input = jnp.transpose(planes.reshape(OWN, 32, PLANES, LANES), (0, 2, 1, 3))
    grad_input = grad_input.reshape(OWN, PLANES, CELLS)
    return grad_input, grad_spectral, grad_pointwise, grad_bias[0]


def solution(mesh):
    placed = (
        P(None, "slab", None),
        P(None, "slab", None),
        P(None, "chan", None, "slab", None),
        P(),
        P(),
    )
    return jax.shard_map(
        body,
        mesh=mesh,
        in_specs=placed,
        out_specs=(
            P("chan", "slab", None),
            P(None, "chan", None, "slab", None),
            P("chan", None),
            P(),
        ),
        check_vma=False,
    )
```

```python
import math

import jax
import jax.numpy as jnp
import numpy as np
from jax import lax
from jax.experimental import pallas as pl
from jax.experimental.pallas import tpu as pltpu
from jax.sharding import PartitionSpec as P

MX = 32
MY = 32
MZ = 16
NX = 256
NY = 64
NZ = 64
C = 64
OWN = 16
SLAB = 128
PLANES = 2
LOW = 4
HIGH = 8
CELLS = NY * NZ
LANES = 128
HALF = 64
CHUNK = 10
BACK = 4
SHARE = 7
PITCH = 66
OWN_ROOM = 56
INVERSE_ROOT = 1.0 / math.sqrt(NX * NY * NZ)
F32 = jnp.float32
BF16 = jnp.bfloat16


def kept(total, length):
    index = np.arange(total)
    return np.where(index < total // 2, index, index - total + length)


def waves(frequency, length):
    wound = (frequency[:, None] * np.arange(length)[None, :]) % length
    angle = np.float32(2.0 * math.pi / length) * wound.astype(np.float32)
    return np.cos(angle), np.sin(angle)


def table(values):
    return jnp.asarray(np.asarray(values, np.float32)).astype(BF16)


def axis_tables():
    cos_z, sin_z = waves(np.arange(MZ), NZ)
    cos_y, sin_y = waves(kept(MY, NY), NY)
    cos_x, sin_x = waves(kept(MX, NX), NX)
    return cos_z, sin_z, cos_y, sin_y, cos_x, sin_x


def rows_of_ky(real, imag):
    both = np.stack([real, imag], 1).reshape(HIGH, LOW, 2, -1)
    return np.transpose(both, (0, 2, 1, 3))


def pack_tables():
    cos_z, sin_z, cos_y, sin_y, cos_x, sin_x = axis_tables()
    weight = (np.where(np.arange(MZ) == 0, 1.0, 2.0) / (NX * NY * NZ))[:, None]
    plain_z = np.stack([cos_z, -sin_z], 1)
    wide = plain_z[:, :, None, None, :] * np.eye(8)[None, None, :, :, None]
    tall = (weight[:, :, None, None, None] * wide).reshape(256, 512).T
    wide = wide.reshape(256, 512)
    real = np.stack([cos_y, sin_y], 1).reshape(MY, 2 * NY)
    imag = np.stack([-sin_y, cos_y], 1).reshape(MY, 2 * NY)
    to_y = rows_of_ky(real, imag).reshape(2 * MY, 2 * NY).T
    from_y = rows_of_ky(real, imag).reshape(HIGH, 8, 2 * NY)
    from_y = np.concatenate([from_y, np.zeros((HIGH, CHUNK - 8, 2 * NY))], 1)
    from_y = from_y.reshape(HIGH * CHUNK, 2 * NY)
    pick = np.zeros((SLAB, 32))
    owner = np.arange(SLAB)
    pick[owner, np.minimum(owner // SHARE, OWN)] = 1.0
    split = np.concatenate([cos_x, sin_x], 0).reshape(2 * MX, SLAB, PLANES)
    gather = np.transpose(split, (2, 0, 1)).reshape(2 * PLANES * MX, SLAB)
    quarter = NY // 4
    cos_q = np.transpose(cos_y[:, :quarter].reshape(HIGH, LOW, quarter), (1, 0, 2))
    sin_q = np.transpose(sin_y[:, :quarter].reshape(HIGH, LOW, quarter), (1, 0, 2))
    real = np.stack([cos_q, sin_q], 2)
    imag = np.stack([-sin_q, cos_q], 2)
    own_from_y = np.stack([real, imag], 2).reshape(2 * MY, 2 * quarter)
    real = np.stack([cos_q, -sin_q], -1)
    imag = np.stack([sin_q, cos_q], -1)
    own_to_y = np.stack([real, imag], 1)
    own_to_y = np.pad(own_to_y, ((0, 0), (0, 0), (0, 0), (0, 0), (0, BACK - 2)))
    own_to_y = np.transpose(own_to_y, (0, 1, 3, 2, 4)).reshape(LOW * 2 * quarter, HIGH * BACK)
    parts = dict(
        to_y=to_y, from_y=from_y, pick=pick,
    )
    side = np.zeros((256, LANES))
    side[: 2 * MY, : 2 * quarter] = own_from_y
    side[2 * MY : 2 * MY + 8 * quarter, : HIGH * BACK] = own_to_y
    wide = np.concatenate([wide, side], 1)
    places = {}
    rows = []
    start = 0
    for name, part in parts.items():
        places[name] = (start, part.shape[0], part.shape[1])
        start += part.shape[0]
        rows.append(np.pad(part, ((0, 0), (0, LANES - part.shape[1]))))
    places["gather"] = (0, SLAB, SLAB)
    places["spread"] = (SLAB, SLAB, SLAB)
    pencil = np.concatenate([gather, gather.T], 0)
    return places, np.concatenate(rows, 0), pencil, wide, tall


PLACES, PACKED, PENCIL, WIDE, TALL = pack_tables()


def wide_part(wide):
    return wide[:, :512]


def own_from_y(wide):
    return wide[:64, 512:544]


def own_to_y(wide):
    return wide[64:192, 512:544]


def get(tables, name):
    start, rows, lanes = PLACES[name]
    return tables[start : start + rows, :lanes]


def mm(left, right):
    return jnp.dot(left, right, preferred_element_type=F32)


def swap(values):
    return pltpu.roll(values, HALF, 1)


def turn(values, shift):
    return pltpu.roll(values, shift, 1)


def quarter_turns(real, imag, forward):
    lane = lane_of(real.shape)
    even = (lane // 32) % 2 == 0
    sign = jnp.where(lane < HALF, 1.0, -1.0)
    sums, gaps = [], []
    for part in (real, imag):
        other = swap(part)
        sums.append(part + other)
        gaps.append(part - other)
    if forward:
        cross = (gaps[1], -gaps[0])
    else:
        cross = (-gaps[1], gaps[0])
    return [
        jnp.where(even, e + sign * turn(e, 96), sign * turn(d, 32) + c)
        for e, d, c in zip(sums, gaps, cross)
    ]


def by_group(blocks):
    group = lane_of(blocks[0].shape) // 32
    out = blocks[0]
    for index in range(1, 4):
        out = jnp.where(group == index, blocks[index], out)
    return out


def lane_of(shape):
    return lax.broadcasted_iota(jnp.int32, shape, 1)


def twice_gelu_grad(pre_act):
    bell = jnp.exp2(pre_act * pre_act * (-0.5 * math.log2(math.e)))
    bell = (pre_act * math.sqrt(2.0 / math.pi)) * bell
    return (1.0 + lax.erf(pre_act * (1.0 / math.sqrt(2.0)))) + bell


def two_words(values):
    head = values.astype(BF16).astype(F32)
    rest = values - head
    return jnp.where(lane_of(values.shape) < HALF, head, swap(rest))


def middle_kernel(
    modes, bases, cots, own, wide, tall, tables, grad_out, out,
    up, flat, down, rows, grad, base, cot, sem
):
    pairs = ((bases, base), (cots, cot))
    loads = [
        pltpu.make_async_copy(source, target, sem.at[index + 1])
        for index, (source, target) in enumerate(pairs)
    ]
    for load in loads:
        load.start()

    @pl.loop(0, MZ, unroll=4)
    def _(kz):
        start = pl.multiple_of(kz * 64, 64)
        lines = mm(get(tables, "to_y"), modes[pl.ds(start, 64), :])
        up[pl.ds(2 * kz, 2), :, :] = lines.reshape(2, NY, LANES)

    loads[0].wait()
    for pair in range(4):
        sides = [
            up[:, (2 * pair + side) * 8 : (2 * pair + side) * 8 + 8, :].reshape(256, LANES)
            for side in range(2)
        ]
        grid = mm(tall[...], jnp.concatenate(sides, 1).astype(BF16))
        for side in range(2):
            cells = pl.ds((2 * pair + side) * 512, 512)
            flat[cells, :] = grid[:, side * LANES : (side + 1) * LANES] + base[cells, :]
    loads[1].wait()

    @pl.loop(0, CELLS // 64, unroll=4)
    def _(block):
        here = pl.ds(pl.multiple_of(block * 64, 64), 64)
        grad[here, :] = (cot[here, :].astype(F32) * twice_gelu_grad(flat[here, :])).astype(BF16)

    save = pltpu.make_async_copy(grad, grad_out, sem.at[0])
    save.start()
    for pair in range(4):
        sides = [grad[(2 * pair + side) * 512 : (2 * pair + side) * 512 + 512, :] for side in range(2)]
        lines = mm(wide_part(wide), jnp.concatenate(sides, 1)).reshape(2 * MZ, 8, 2 * LANES)
        for side in range(2):
            group = (2 * pair + side) * 8
            down[:, group : group + 8, :] = lines[:, :, side * LANES : (side + 1) * LANES]

    sums = jnp.zeros((3 * OWN, LANES), F32)
    for quarter in range(4):
        cells = pl.ds(quarter * 1024, 1024)
        left = own[quarter * 32 : quarter * 32 + 32, :]
        left = jnp.concatenate([left, jnp.ones((OWN, CELLS // 4), BF16)], 0)
        sums += mm(left, grad[cells, :])
    lower = sums[:OWN] + swap(sums[OWN : 2 * OWN])
    bias = sums[2 * OWN : 2 * OWN + 8] + swap(sums[2 * OWN : 2 * OWN + 8])
    words = two_words(jnp.concatenate([lower, bias, jnp.zeros_like(bias)], 0)).astype(BF16)

    flat[:SLAB, :] = mm(get(tables, "pick"), words)
    half_rows = SLAB * CHUNK // 2
    for half in range(2):

        @pl.loop(half * MZ // 2, (half + 1) * MZ // 2, unroll=4)
        def _(kz):
            lines = down[pl.ds(2 * kz, 2), :, :].reshape(2 * NY, LANES).astype(BF16)
            start = pl.multiple_of(kz * HIGH * CHUNK, HIGH * CHUNK)
            rows[pl.ds(start, HIGH * CHUNK), :] = mm(get(tables, "from_y"), lines)

        here = pl.ds(half * half_rows, half_rows)
        rows[pl.ds(half * half_rows + 8, SLAB // 2, stride=CHUNK), :] = flat[
            half * SLAB // 2 : (half + 1) * SLAB // 2, :
        ]
        out[here, :] = rows[here, :].astype(BF16)
    save.wait()


def places(count, anywhere):
    kinds = [pltpu.HBM if index in anywhere else pltpu.VMEM for index in range(count)]
    return [pl.BlockSpec(memory_space=kind) for kind in kinds]


def call(kernel, shapes, scratch, flops, room, *operands, anywhere=(), anywhere_out=()):
    moved = sum(s.size * s.dtype.itemsize for s in list(operands) + list(shapes))
    return pl.pallas_call(
        kernel,
        out_shape=shapes,
        in_specs=places(len(operands), anywhere),
        out_specs=places(len(shapes), anywhere_out),
        scratch_shapes=scratch,
        cost_estimate=pl.CostEstimate(flops=flops, bytes_accessed=moved, transcendentals=0),
        compiler_params=pltpu.CompilerParams(vmem_limit_bytes=room * 2**20),
    )(*operands)


def middle(modes, base, cot, own, wide, tables):
    shapes = (
        jax.ShapeDtypeStruct((CELLS, LANES), BF16),
        jax.ShapeDtypeStruct((SLAB * CHUNK, LANES), BF16),
    )
    scratch = [
        pltpu.VMEM((2 * MZ, NY, LANES), F32),
        pltpu.VMEM((CELLS, LANES), F32),
        pltpu.VMEM((2 * MZ, NY, LANES), F32),
        pltpu.VMEM((SLAB * CHUNK, LANES), F32),
        pltpu.VMEM((CELLS, LANES), BF16),
        pltpu.VMEM((CELLS, LANES), F32),
        pltpu.VMEM((CELLS, LANES), BF16),
        pltpu.SemaphoreType.DMA((3,)),
    ]
    return call(
        middle_kernel, shapes, scratch, 400_000_000, 52,
        modes, base, cot, own, wide, table(TALL), tables,
        anywhere=(1, 2), anywhere_out=(0,),
    )


def own_kernel(field, wides, out, own, raw, spread, lines, wide, sem):
    start = pl.multiple_of(lax.axis_index("chan") * (OWN * HALF), OWN * HALF)
    fetch = pltpu.make_async_copy(field.at[pl.ds(start, OWN * HALF), :], raw, sem.at[0])
    fetch.start()
    load = pltpu.make_async_copy(wides, wide, sem.at[1])
    load.start()
    fetch.wait()
    for c in range(OWN):
        spread[c * PITCH : c * PITCH + HALF, :] = raw[c * HALF : (c + 1) * HALF, :].astype(F32)
    for tile in range(8):
        parts = [
            spread[pl.ds((quarter * 8 + tile) * 2 + plane, OWN, stride=PITCH), :]
            for quarter in range(4)
            for plane in range(PLANES)
        ]
        own[:, tile * LANES : (tile + 1) * LANES] = jnp.concatenate(parts, 0).astype(BF16)
    load.wait()
    for group in range(2):
        part = lax.dot_general(
            wide_part(wide),
            own[:, group * 512 : (group + 1) * 512],
            (((1,), (1,)), ((), ())),
            preferred_element_type=F32,
        ).reshape(MZ, 2, 8, LANES)
        real = part[:, 0].reshape(MZ * 8, LANES)
        imag = part[:, 1].reshape(MZ * 8, LANES)
        real, imag = quarter_turns(real, imag, True)
        lines[:, 0, group * 8 : group * 8 + 8, :] = real.reshape(MZ, 8, LANES)
        lines[:, 1, group * 8 : group * 8 + 8, :] = imag.reshape(MZ, 8, LANES)
    for pair in range(MZ // 2):
        left = lines[2 * pair].reshape(32, LANES)
        right = lines[2 * pair + 1].reshape(32, LANES)
        both = jnp.concatenate([left, right], 1).astype(BF16)
        both = mm(own_from_y(wide), both)
        for half in range(2):
            part = both[:, half * LANES : (half + 1) * LANES]
            part = by_group([part[low * 16 : low * 16 + 16] for low in range(LOW)])
            start = (2 * pair + half) * 16
            out[start : start + 16, :] = part.astype(BF16)


def own_modes(field, wide):
    shapes = (
        jax.ShapeDtypeStruct((2 * SLAB, LANES), BF16),
        jax.ShapeDtypeStruct((LANES, CELLS // 4), BF16),
    )
    scratch = [
        pltpu.VMEM((OWN * HALF, LANES), BF16),
        pltpu.VMEM((OWN * PITCH, LANES), F32),
        pltpu.VMEM((MZ, 2, NY // 4, LANES), F32),
        pltpu.VMEM((256, 640), BF16),
        pltpu.SemaphoreType.DMA((2,)),
    ]
    return call(own_kernel, shapes, scratch, 4_000_000, OWN_ROOM, field, wide, anywhere=(0, 1))


def grid_kernel(modes, point, wide_z, out, sums, bias, lines, wide, spread):
    wide[...] = modes[...].astype(F32)
    for kz in range(MZ):
        both = mm(own_to_y(wide_z), modes[kz * 32 : kz * 32 + 32, :])
        both = by_group([both[low * 32 : low * 32 + 32] for low in range(LOW)])
        real, imag = quarter_turns(both[:16], both[16:], False)
        lines[kz, 0] = real
        lines[kz, 1] = imag
    for group in range(2):
        both = lines[:, :, group * 8 : group * 8 + 8, :].reshape(256, LANES)
        both = mm(both.T.astype(BF16), wide_part(wide_z))
        for quarter in range(4):
            cells = pl.ds(quarter * 1024 + group * 512, 512)
            here = both[quarter * 32 : quarter * 32 + 32] + point[:, cells]
            for plane in range(PLANES):
                for tile in range(4):
                    first = (quarter * 8 + group * 4 + tile) * 2 + plane
                    spread[pl.ds(first, OWN, stride=PITCH), :] = here[
                        plane * OWN : (plane + 1) * OWN, tile * LANES : (tile + 1) * LANES
                    ]
    for i in range(OWN):
        out[i * HALF : (i + 1) * HALF, :] = spread[i * PITCH : i * PITCH + HALF, :].astype(BF16)
    words = wide[pl.ds(2, OWN, stride=BACK * SHARE), :]
    sums[...] = (words + swap(words))[:, :HALF]
    words = wide[pl.ds(BACK * SHARE * OWN + 2, 8, stride=1), :]
    bias[...] = (words + swap(words))[:1, :HALF]


def own_grid(modes, point, wide):
    shapes = (
        jax.ShapeDtypeStruct((OWN * HALF, LANES), BF16),
        jax.ShapeDtypeStruct((OWN, C), F32),
        jax.ShapeDtypeStruct((1, C), F32),
    )
    scratch = [
        pltpu.VMEM((MZ, 2, NY // 4, LANES), F32),
        pltpu.VMEM((SLAB * BACK, LANES), F32),
        pltpu.VMEM((OWN * PITCH, LANES), F32),
    ]
    return call(grid_kernel, shapes, scratch, 8_000_000, 8, modes, point, wide)


def along_x(tables, left, right):
    both = mm(get(tables, "gather"), jnp.concatenate([left, right], 1).astype(BF16))
    return both[: 2 * MX], both[2 * MX :]


def mix_kernel(pencils, weight, tables, coeff, out, wide):
    wide[...] = pencils[...].astype(F32)
    left = wide[pl.ds(0, SLAB, stride=2), :]
    right = wide[pl.ds(1, SLAB, stride=2), :]
    near, far = along_x(tables, left, right)
    near = near + jnp.concatenate([turn(far[:, :LANES], 112), turn(far[:, LANES:], 112)], 1)
    modes_real = (near[:MX, :LANES] + near[MX:, LANES:]).astype(BF16).astype(F32)
    modes_imag = (near[:MX, LANES:] - near[MX:, :LANES]).astype(BF16).astype(F32)
    coeff[0] = modes_real
    coeff[1] = modes_imag
    for m in range(LOW):
        rows = pl.ds(m * MX, MX)
        real = jnp.zeros((MX, C), F32)
        imag = jnp.zeros((MX, C), F32)
        for i in range(OWN):
            at = m * 32 + i
            left = jnp.broadcast_to(modes_real[:, at : at + 1], (MX, C))
            right = jnp.broadcast_to(modes_imag[:, at : at + 1], (MX, C))
            weight_real = weight[0, i, rows, :].astype(F32)
            weight_imag = weight[1, i, rows, :].astype(F32)
            real += left * weight_real - right * weight_imag
            imag += left * weight_imag + right * weight_real
        part = jnp.concatenate([real, imag], 1).astype(BF16)
        for peer in range(4):
            out[peer, rows, :] = part


def mix(pencils, weight, tables):
    shapes = (
        jax.ShapeDtypeStruct((2, MX, LANES), F32),
        jax.ShapeDtypeStruct((4, LOW * MX, LANES), BF16),
    )
    scratch = [pltpu.VMEM((2 * SLAB, LANES), F32)]
    return call(mix_kernel, shapes, scratch, 4_000_000, 8, pencils, weight, tables)


def spread_kernel(parts, tables, out, rows):
    total = parts[0].astype(F32)
    for peer in range(1, 4):
        total += parts[peer].astype(F32)
    lane = lane_of((MX, LANES))
    for m in range(LOW):
        here = total[m * MX : (m + 1) * MX]
        there = swap(here)
        zero = jnp.zeros_like(here)
        a = jnp.where(lane < HALF, here, zero)
        b = jnp.where(lane < HALF, there, zero)
        c = jnp.where(lane < HALF, zero, there)
        d = jnp.where(lane < HALF, zero, here)
        top = jnp.concatenate([a, b], 1)
        second = jnp.concatenate([-b, a], 1)
        third = jnp.concatenate([c, d], 1)
        last = jnp.concatenate([-d, c], 1)
        block = jnp.concatenate([top, second, third, last], 0).astype(BF16)
        planes = mm(get(tables, "spread"), block)
        rows[pl.ds(m, SLAB, stride=8), :] = planes[:, :LANES]
        rows[pl.ds(LOW + m, SLAB, stride=8), :] = planes[:, LANES:]
    out[...] = rows[...].astype(BF16)


def spread_planes(parts, tables):
    shapes = (jax.ShapeDtypeStruct((SLAB * 8, LANES), BF16),)
    scratch = [pltpu.VMEM((SLAB * 8, LANES), F32)]
    return call(spread_kernel, shapes, scratch, 40_000_000, 8, parts, tables)[0]


def adjoint_kernel(pencils, weights, tables, scale, hat, out, wide, rows, weight, sem):
    load = pltpu.make_async_copy(weights, weight, sem)
    load.start()
    wide[...] = pencils[...].astype(F32)
    lane = lane_of((MX, LANES))
    near_real = jnp.zeros((MX, LANES), F32)
    near_imag = jnp.zeros((MX, LANES), F32)
    factor = scale[0:1, :]
    for m in range(LOW):
        left = wide[pl.ds(m, SLAB, stride=CHUNK), :]
        right = wide[pl.ds(LOW + m, SLAB, stride=CHUNK), :]
        near, far = along_x(tables, left, right)
        first = near[:, :LANES] + swap(far[:, :LANES])
        second = near[:, LANES:] + swap(far[:, LANES:])
        real = (first[:MX] + second[MX:]) * factor
        imag = (second[:MX] - first[MX:]) * factor
        hat[0, pl.ds(m * MX, MX), :] = real.astype(BF16).astype(F32)[:, :C]
        hat[1, pl.ds(m * MX, MX), :] = imag.astype(BF16).astype(F32)[:, :C]
    load.wait()
    for m in range(LOW):
        at_m = pl.ds(m * MX, MX)
        real = hat[0, at_m, :]
        imag = hat[1, at_m, :]
        for i in range(OWN):
            weight_real = weight[0, i, at_m, :].astype(F32)
            weight_imag = weight[1, i, at_m, :].astype(F32)
            sum_real = jnp.sum(real * weight_real + imag * weight_imag, 1, keepdims=True)
            sum_imag = jnp.sum(imag * weight_real - real * weight_imag, 1, keepdims=True)
            near_real = jnp.where(lane == m * 32 + i, sum_real, near_real)
            near_imag = jnp.where(lane == m * 32 + i, sum_imag, near_imag)
    far_real = turn(near_real, 16)
    far_imag = turn(near_imag, 16)
    top = jnp.concatenate([near_real, near_imag], 1)
    second = jnp.concatenate([-near_imag, near_real], 1)
    third = jnp.concatenate([far_real, far_imag], 1)
    last = jnp.concatenate([-far_imag, far_real], 1)
    block = jnp.concatenate([top, second, third, last], 0).astype(BF16)
    planes = mm(get(tables, "spread"), block)
    rows[pl.ds(0, SLAB, stride=BACK), :] = planes[:, :LANES]
    rows[pl.ds(1, SLAB, stride=BACK), :] = planes[:, LANES:]
    rider = wide[pl.ds(8, SLAB, stride=CHUNK), :]
    total = jnp.sum(rider, 0, keepdims=True)
    total = jnp.broadcast_to(total, (8, LANES))
    total = two_words((total + swap(total)) * INVERSE_ROOT)
    rows[pl.ds(2, SLAB, stride=BACK), :] = jnp.broadcast_to(total[:1], (SLAB, LANES))
    rows[pl.ds(3, SLAB, stride=BACK), :] = jnp.zeros((SLAB, LANES), F32)
    out[...] = rows[...].astype(BF16)


def adjoint_planes(pencils, weight, tables, scale):
    shapes = (
        jax.ShapeDtypeStruct((2, LOW * MX, C), F32),
        jax.ShapeDtypeStruct((SLAB * BACK, LANES), BF16),
    )
    scratch = [
        pltpu.VMEM((SLAB * CHUNK, LANES), F32),
        pltpu.VMEM((SLAB * BACK, LANES), F32),
        pltpu.VMEM((2, OWN, LOW * MX, C), BF16),
        pltpu.SemaphoreType.DMA,
    ]
    return call(
        adjoint_kernel, shapes, scratch, 40_000_000, 50, pencils, weight, tables, scale, anywhere=(1,)
    )


def outer_kernel(coeff, hat, out):
    modes_real = coeff[0]
    modes_imag = coeff[1]
    for m in range(LOW):
        rows = pl.ds(m * MX, MX)
        real = hat[0, rows, :]
        imag = hat[1, rows, :]
        for i in range(OWN):
            at = m * 32 + i
            left = jnp.broadcast_to(modes_real[:, at : at + 1], (MX, C))
            right = jnp.broadcast_to(modes_imag[:, at : at + 1], (MX, C))
            out[0, i, rows, :] = left * real + right * imag
            out[1, i, rows, :] = left * imag - right * real


def outer(coeff, hat):
    shapes = (jax.ShapeDtypeStruct((2, OWN, LOW * MX, C), F32),)
    return call(outer_kernel, shapes, [], 8_000_000, 8, coeff, hat)[0]


def over(values, axis):
    return lax.all_to_all(values, axis, split_axis=0, concat_axis=0, tiled=True)


def paired(matrix):
    zero = jnp.zeros_like(matrix)
    upper = jnp.concatenate([matrix, zero], 1)
    lower = jnp.concatenate([zero, matrix], 1)
    return jnp.concatenate([upper, lower], 0)


def body(field, cotangent, spectral_weight, point_weight, point_bias):
    chan_start = lax.axis_index("chan") * OWN
    own_rows = paired(lax.dynamic_slice_in_dim(point_weight, chan_start, OWN, 0))
    weight = jnp.transpose(spectral_weight, (0, 1, 3, 4, 2)).reshape(2, OWN, LOW * MX, C)
    tables = table(PENCIL)
    wide = table(WIDE)
    rows = jnp.transpose(field.reshape(C, PLANES, 32, LANES), (0, 2, 1, 3)).reshape(CELLS, LANES)
    first, own = own_modes(rows, wide)
    cotangent, first = lax.optimization_barrier((cotangent, first))
    cot = jnp.transpose(cotangent, (2, 1, 0)).reshape(CELLS, LANES)
    cot = mm(cot, 0.5 * jnp.eye(LANES, dtype=BF16)).astype(BF16)
    pencils = over(first.reshape(SLAB, PLANES, LANES), "slab").reshape(NX, LANES)
    pencils, cot = lax.optimization_barrier((pencils, cot))
    coeff, parts = mix(pencils, weight, tables)

    field, own_rows, parts = lax.optimization_barrier((field, own_rows, parts))
    kz_weight = jnp.where(lax.axis_index("slab") < HIGH, 1.0, 2.0) / (NX * NY * NZ)
    scale = jnp.full((8, LANES), kz_weight, F32)
    cells = jnp.transpose(field, (2, 1, 0)).reshape(CELLS, LANES)
    bias = jnp.tile(point_bias.astype(F32), 2)[None]
    base = mm(cells, paired(point_weight)) + bias
    parts = over(parts, "chan")
    parts, base, own_rows, scale = lax.optimization_barrier((parts, base, own_rows, scale))

    planes = spread_planes(parts, tables)
    modes = over(planes.reshape(SLAB, 8, LANES), "slab").reshape(SLAB * 8, LANES)
    grad, rows = middle(modes, base, cot, own, wide, table(PACKED))
    arrived = over(rows.reshape(SLAB * CHUNK // 2, 2, LANES), "slab")
    hat, rows = adjoint_planes(arrived.reshape(SLAB * CHUNK, LANES), weight, tables, scale)
    final = over(rows.reshape(SLAB, BACK, LANES), "slab").reshape(SLAB * BACK, LANES)
    point_back = mm(own_rows, grad.T)
    outer_part = outer(coeff, hat).reshape(2, OWN, LOW, MX, C)
    grad_spectral = jnp.transpose(outer_part, (0, 1, 4, 2, 3))
    planes, grad_pointwise, grad_bias = own_grid(final, point_back, wide)
    grad_input = jnp.transpose(planes.reshape(OWN, 32, PLANES, LANES), (0, 2, 1, 3))
    grad_input = grad_input.reshape(OWN, PLANES, CELLS)
    return grad_input, grad_spectral, grad_pointwise, grad_bias[0]


def solution(mesh):
    placed = (
        P(None, "slab", None),
        P(None, "slab", None),
        P(None, "chan", None, "slab", None),
        P(),
        P(),
    )
    return jax.shard_map(
        body,
        mesh=mesh,
        in_specs=placed,
        out_specs=(
            P("chan", "slab", None),
            P(None, "chan", None, "slab", None),
            P("chan", None),
            P(),
        ),
        check_vma=False,
    )
```
